128 devices in a mesh: alpha: 8 (over y, x_lo), beta: 16 (over x_hi, z, core).
Axes of the slice: x: 4 (x_hi: 2, x_lo: 2; x = x_hi * 2 + x_lo), y: 4, z: 4, core: 2. Of those that a mesh axis runs over, the one named last changes fastest.
Arguments:
- coefficients: bfloat16 [2048, 4096], P('alpha', 'beta'), may hold values from -6 to 6
- diagonal: float32 [2048, 4096], P('alpha', 'beta'), may hold values from 0.3 to 3
- integrals: bfloat16 [324, 324], replicated, may hold values from -0.02734375 to 0.02734375
- alpha_row: int32 [324, 2048], replicated, may hold values from 0 to 2047
- alpha_sign: int32 [324, 2048], replicated, may hold values from -1 to 1
- beta_block: int32 [64, 324], P('beta'), may hold values from 0 to 63
- beta_sign: int32 [64, 20736], P('beta'), may hold values from -1 to 1
- block_irrep: int32 [32], replicated, may hold values from 0 to 7, as said below
Outputs:
- sigma: float32 [2048, 4096], P('alpha', 'beta')
The draws below stay inside these ranges and needn't reach their ends.
Inputs may be any that keep to these rules, and one draw needn't show every extreme that they name: `block_irrep`: irrep 0 is the window's. The 4 blocks held by one index of alpha include 1 to 4 blocks of irrep 0, and some index holds 4 of them.
All inputs are finite; a program needn't handle non-finite values.
Results may differ from the reference program's by a relative error of at most 0.0003.
Values may be sent and summed in bfloat16 or wider, within the bound.
A program may use at most 128 MiB of HBM per device.

```python
import math
import jax
import jax.numpy as jnp
from jax import lax

P_SIZE = 324
BLOCK = 64
AB_DEV = 4
NA = 2048
NB = 4096
NBB = 64
N_ALPHA = 8


def draw_block_irrep(key, part):
    key_count, key_heavy, key_order, key_other = jax.random.split(key, 4)
    upper = max(1, AB_DEV // 2)
    counts = jax.random.randint(key_count, (N_ALPHA,), 1, upper + 1)
    heavy = jax.random.randint(key_heavy, (), 0, N_ALPHA)
    device_iota = jnp.arange(N_ALPHA, dtype=jnp.int32)
    counts = jnp.where(device_iota == heavy, AB_DEV, counts)
    order_keys = jax.random.split(key_order, N_ALPHA)
    orders = jax.vmap(lambda single: jax.random.permutation(single, AB_DEV))(order_keys)
    live_mask = orders < counts[:, None]
    others = jax.random.randint(key_other, (N_ALPHA, AB_DEV), 1, 8)
    return jnp.where(live_mask, 0, others).reshape(-1).astype(jnp.int32)


def plant(entries, own_key, low, top_value):
    longest = entries.shape.index(max(entries.shape))
    spots = []
    for shift in (0, 1):
        where = [jax.random.randint(jax.random.fold_in(own_key, axis), (), 0, length) for axis, length in enumerate(entries.shape)]
        where[longest] = (where[longest] + shift) % entries.shape[longest]
        spots.append(tuple(where))
    return entries.at[spots[0]].set(low).at[spots[1]].set(top_value)


def steps_of(stream_key, dims, cuts, least, largest):
    level = 1.0
    for dim, parts in cuts:
        heights = jax.random.uniform(jax.random.fold_in(jax.random.fold_in(stream_key, 6), dim), (parts,), jnp.float32, least / len(cuts), largest / len(cuts))
        level = level * jnp.repeat(jnp.exp(heights), dims[dim] // parts).reshape((-1,) + (1,) * (len(dims) - 1 - dim))
    return level


def centred(own_key, shape, spread, limit, shards=(), kind=jnp.bfloat16):
    values = spread * jax.random.normal(own_key, shape, jnp.float32)
    if shards:
        values = values * steps_of(own_key, shape, shards, -0.22, 0.18)
    return jnp.clip(values, -limit, limit).astype(kind)


def setup_inputs(seed: int = 0) -> dict:
    streams_of = jax.random.split(jax.random.key(seed), 9)
    return {
        "coefficients": centred(streams_of[0], (NA, NB), 1.0, 6.0, ((0, 8), (1, 16))),
        "diagonal": jnp.clip(jnp.exp(math.log(3.0) - 2.3025851 * jax.random.uniform(streams_of[1], (NA, NB), jnp.float32) ** steps_of(streams_of[1], (NA, NB), ((0, 8), (1, 16)), -0.2, 0.2)), 0.3, 3.0),
        "integrals": centred(streams_of[2], (P_SIZE, P_SIZE), (P_SIZE * P_SIZE // 2) ** -0.5, 0.02734375),
        "alpha_row": plant(jax.random.randint(streams_of[3], (P_SIZE, NA), 0, NA), jax.random.fold_in(streams_of[3], 1), 0, NA - 1).astype(jnp.int32),
        "alpha_sign": plant(jax.random.randint(streams_of[4], (P_SIZE, NA), -1, 2), jax.random.fold_in(streams_of[4], 1), -1, 1).astype(jnp.int32),
        "beta_block": plant(jax.random.randint(streams_of[5], (NBB, P_SIZE), 0, NBB), jax.random.fold_in(streams_of[5], 1), 0, NBB - 1).astype(jnp.int32),
        "beta_sign": plant(jax.random.randint(streams_of[6], (NBB, P_SIZE * BLOCK), -1, 2), jax.random.fold_in(streams_of[6], 1), -1, 1).astype(jnp.int32),
        "block_irrep": draw_block_irrep(jax.random.fold_in(streams_of[8], 71), 0),
    }


def reference(coefficients, diagonal, integrals, alpha_row, alpha_sign, beta_block, beta_sign, block_irrep):
    live_rows = jnp.repeat((block_irrep == 0).astype(jnp.int32), BLOCK)
    coeff_live = jnp.where(live_rows[:, None] == 1, coefficients, jnp.zeros_like(coefficients))
    coeff_float = coeff_live.astype(jnp.float32)
    integ_float = integrals.astype(jnp.float32)
    beta_ids = beta_block.reshape(-1)
    beta_signs = beta_sign.reshape(NBB, P_SIZE, BLOCK).astype(jnp.float32)
    step_rows = min(16, BLOCK)
    first_rows = jnp.arange(NA // step_rows, dtype=jnp.int32) * step_rows

    def one_block(first_row):
        row_ids = lax.dynamic_slice_in_dim(alpha_row, first_row, step_rows, 1)
        sign_vals = lax.dynamic_slice_in_dim(alpha_sign, first_row, step_rows, 1).astype(jnp.float32)
        replaced = coeff_float[row_ids] * sign_vals[:, :, None]
        mixed = jnp.einsum("qp,prj->qrj", integ_float, replaced, precision=lax.Precision.HIGHEST)
        mixed = mixed.reshape(P_SIZE, step_rows, NBB, BLOCK).transpose(2, 0, 1, 3)
        weighted = mixed * beta_signs[:, :, None, :]
        summed = jax.ops.segment_sum(weighted.reshape(NBB * P_SIZE, step_rows * BLOCK), beta_ids, num_segments=NBB)
        return summed.reshape(NBB, step_rows, BLOCK).transpose(1, 0, 2).reshape(step_rows, NB)

    ab_term = lax.map(one_block, first_rows).reshape(NA, NB)
    total = diagonal * coefficients.astype(jnp.float32) + ab_term
    return jnp.where(live_rows[:, None] == 1, total, jnp.zeros_like(total))
```

```python
import jax
import jax.numpy as jnp
from jax import lax
from jax.sharding import PartitionSpec as P


def split_bf16(values):
    rounded = lax.reduce_precision(values, exponent_bits=8, mantissa_bits=7)
    return rounded.astype(jnp.bfloat16), (values - rounded).astype(jnp.bfloat16)


def on_device(
    coefficients, diagonal, integrals, alpha_row, alpha_sign, beta_block, beta_sign, block_irrep
):
    alpha_rank = lax.axis_index("alpha")
    pair_count = integrals.shape[0]
    local_rows, local_cols = coefficients.shape
    block_len = beta_sign.shape[1] // pair_count
    per_device = local_rows // block_len
    src_blocks = local_cols // block_len
    total_blocks = lax.axis_size("beta") * src_blocks

    gathered = lax.all_gather(coefficients, "alpha", axis=0, tiled=True)
    live_flags = (block_irrep == 0).astype(jnp.int32)
    live_rows = jnp.repeat(live_flags, block_len)
    gathered = gathered * live_rows[:, None].astype(jnp.bfloat16)
    window_rows = gathered.shape[0]
    coeff3 = gathered.reshape(window_rows, src_blocks, block_len)

    beta_ids = beta_block.T.reshape(-1)
    target_iota = jnp.arange(total_blocks, dtype=jnp.int32)
    target_table = (target_iota[:, None] == beta_ids[None, :]).astype(jnp.bfloat16)
    signs_qs = (
        beta_sign.reshape(src_blocks, pair_count, block_len).transpose(1, 0, 2).astype(jnp.float32)
    )

    own_flags = lax.dynamic_slice_in_dim(live_flags, alpha_rank * per_device, per_device, 0)
    own_count = jnp.sum(own_flags)
    own_pos = jnp.cumsum(own_flags) - own_flags
    local_iota = jnp.arange(per_device, dtype=jnp.int32)

    dims = lax.GatherDimensionNumbers(
        offset_dims=(1, 3), collapsed_slice_dims=(0,), start_index_map=(0,)
    )

    def one_block(slot_idx, buffer):
        local_blk = jnp.sum(jnp.where((own_flags == 1) & (own_pos == slot_idx), local_iota, 0))
        first_row = (alpha_rank * per_device + local_blk) * block_len
        row_ids = lax.dynamic_slice_in_dim(alpha_row, first_row, block_len, 1)
        sign_vals = lax.dynamic_slice_in_dim(alpha_sign, first_row, block_len, 1).astype(
            jnp.bfloat16
        )
        picked = lax.gather(
            coeff3,
            row_ids[:, :, None],
            dims,
            slice_sizes=(1, src_blocks, block_len),
            mode=lax.GatherScatterMode.PROMISE_IN_BOUNDS,
        )
        picked = picked * sign_vals[:, None, :, None]
        mixed = jnp.dot(
            integrals,
            picked.reshape(pair_count, src_blocks * block_len * block_len),
            preferred_element_type=jnp.float32,
        ).reshape(pair_count, src_blocks, block_len, block_len)
        weighted = mixed * signs_qs[:, :, None, :]
        high, low = split_bf16(
            weighted.reshape(pair_count * src_blocks, block_len * block_len)
        )
        summed = jnp.dot(target_table, high, preferred_element_type=jnp.float32) + jnp.dot(
            target_table, low, preferred_element_type=jnp.float32
        )
        rows_out = (
            summed.reshape(total_blocks, block_len, block_len)
            .transpose(1, 0, 2)
            .reshape(block_len, total_blocks * block_len)
        )
        return lax.dynamic_update_index_in_dim(buffer, rows_out, local_blk, 0)

    empty = jnp.zeros((per_device, block_len, total_blocks * block_len), jnp.float32)
    buffer = lax.fori_loop(0, own_count, one_block, empty)
    summed = lax.psum_scatter(buffer, "beta", scatter_dimension=2, tiled=True)
    placed = summed.reshape(local_rows, local_cols)
    own_live_rows = jnp.repeat(own_flags, block_len)
    total = diagonal * coefficients.astype(jnp.float32) + placed
    return jnp.where(own_live_rows[:, None] == 1, total, jnp.zeros_like(total))


def solution(mesh):
    return jax.shard_map(
        on_device,
        mesh=mesh,
        in_specs=(
            P("alpha", "beta"),
            P("alpha", "beta"),
            P(),
            P(),
            P(),
            P("beta", None),
            P("beta", None),
            P(),
        ),
        out_specs=P("alpha", "beta"),
        check_vma=False,
    )
```

```python
import jax
import jax.numpy as jnp
from jax import lax
from jax.experimental import pallas as pl
from jax.experimental.pallas import tpu as pltpu
from jax.sharding import PartitionSpec as P

TILE = 1024


def mix_kernel(integ_ref, picked_ref, sign_ref, table_ref, out_ref):
    step_s = pl.program_id(1)
    mixed = jnp.dot(integ_ref[...], picked_ref[...], preferred_element_type=jnp.float32)
    weighted = mixed * sign_ref[0].astype(jnp.float32)
    high = weighted.astype(jnp.bfloat16)
    low = (weighted - high.astype(jnp.float32)).astype(jnp.bfloat16)
    table = table_ref[0]
    part = jnp.dot(table, high, preferred_element_type=jnp.float32) + jnp.dot(
        table, low, preferred_element_type=jnp.float32
    )

    @pl.when(step_s == 0)
    def _():
        out_ref[...] = part

    @pl.when(step_s > 0)
    def _():
        out_ref[...] += part


def mix_block(integrals, picked, sign_tiled, tables, src_blocks, block_len, total_blocks):
    pair_count = integrals.shape[0]
    cols = block_len * block_len
    tiles = cols // TILE
    return pl.pallas_call(
        mix_kernel,
        out_shape=jax.ShapeDtypeStruct((total_blocks, cols), jnp.float32),
        grid=(tiles, src_blocks),
        in_specs=[
            pl.BlockSpec((pair_count, pair_count), lambda r, s: (0, 0)),
            pl.BlockSpec((pair_count, TILE), lambda r, s: (0, s * tiles + r)),
            pl.BlockSpec((1, pair_count, TILE), lambda r, s: (s, 0, 0)),
            pl.BlockSpec((1, total_blocks, pair_count), lambda r, s: (s, 0, 0)),
        ],
        out_specs=pl.BlockSpec((total_blocks, TILE), lambda r, s: (0, r)),
        compiler_params=pltpu.CompilerParams(dimension_semantics=("arbitrary", "arbitrary")),
    )(integrals, picked, sign_tiled, tables)


def on_device(
    coefficients, diagonal, integrals, alpha_row, alpha_sign, beta_block, beta_sign, block_irrep
):
    alpha_rank = lax.axis_index("alpha")
    pair_count = integrals.shape[0]
    local_rows, local_cols = coefficients.shape
    block_len = beta_sign.shape[1] // pair_count
    per_device = local_rows // block_len
    src_blocks = local_cols // block_len
    total_blocks = lax.axis_size("beta") * src_blocks

    gathered = lax.all_gather(coefficients, "alpha", axis=0, tiled=True)
    live_flags = (block_irrep == 0).astype(jnp.int32)
    live_rows = jnp.repeat(live_flags, block_len)
    gathered = gathered * live_rows[:, None].astype(jnp.bfloat16)
    window_rows = gathered.shape[0]
    coeff3 = gathered.reshape(window_rows, src_blocks, block_len)

    target_iota = jnp.arange(total_blocks, dtype=jnp.int32)
    tables = (target_iota[None, :, None] == beta_block[:, None, :]).astype(jnp.bfloat16)
    signs = beta_sign.reshape(src_blocks, pair_count, 1, block_len).astype(jnp.bfloat16)
    sign_tiled = jnp.broadcast_to(
        signs, (src_blocks, pair_count, TILE // block_len, block_len)
    ).reshape(src_blocks, pair_count, TILE)

    own_flags = lax.dynamic_slice_in_dim(live_flags, alpha_rank * per_device, per_device, 0)
    own_count = jnp.sum(own_flags)
    own_pos = jnp.cumsum(own_flags) - own_flags
    local_iota = jnp.arange(per_device, dtype=jnp.int32)

    dims = lax.GatherDimensionNumbers(
        offset_dims=(1, 3), collapsed_slice_dims=(0,), start_index_map=(0,)
    )

    def one_block(slot_idx, buffer):
        local_blk = jnp.sum(jnp.where((own_flags == 1) & (own_pos == slot_idx), local_iota, 0))
        first_row = (alpha_rank * per_device + local_blk) * block_len
        row_ids = lax.dynamic_slice_in_dim(alpha_row, first_row, block_len, 1)
        sign_vals = lax.dynamic_slice_in_dim(alpha_sign, first_row, block_len, 1).astype(
            jnp.bfloat16
        )
        picked = lax.gather(
            coeff3,
            row_ids[:, :, None],
            dims,
            slice_sizes=(1, src_blocks, block_len),
            mode=lax.GatherScatterMode.PROMISE_IN_BOUNDS,
        )
        picked = picked * sign_vals[:, None, :, None]
        summed = mix_block(
            integrals,
            picked.reshape(pair_count, src_blocks * block_len * block_len),
            sign_tiled,
            tables,
            src_blocks,
            block_len,
            total_blocks,
        )
        rows_out = (
            summed.reshape(total_blocks, block_len, block_len)
            .transpose(1, 0, 2)
            .reshape(block_len, total_blocks * block_len)
        )
        return lax.dynamic_update_index_in_dim(buffer, rows_out, local_blk, 0)

    empty = jnp.zeros((per_device, block_len, total_blocks * block_len), jnp.float32)
    buffer = lax.fori_loop(0, own_count, one_block, empty)
    summed = lax.psum_scatter(buffer, "beta", scatter_dimension=2, tiled=True)
    placed = summed.reshape(local_rows, local_cols)
    own_live_rows = jnp.repeat(own_flags, block_len)
    total = diagonal * coefficients.astype(jnp.float32) + placed
    return jnp.where(own_live_rows[:, None] == 1, total, jnp.zeros_like(total))


def solution(mesh):
    return jax.shard_map(
        on_device,
        mesh=mesh,
        in_specs=(
            P("alpha", "beta"),
            P("alpha", "beta"),
            P(),
            P(),
            P(),
            P("beta", None),
            P("beta", None),
            P(),
        ),
        out_specs=P("alpha", "beta"),
        check_vma=False,
    )
```

```python
import jax
import jax.numpy as jnp
from jax import lax
from jax.experimental import pallas as pl
from jax.experimental.pallas import tpu as pltpu
from jax.sharding import PartitionSpec as P

ROWS = 8


def mix_kernel(integ_ref, picked_ref, sign_ref, table_ref, out_ref):
    width = sign_ref.shape[1]
    targets = out_ref.shape[1]
    block_len = out_ref.shape[2]
    src_blocks = width // block_len
    lane = lax.broadcasted_iota(jnp.int32, (targets, 2 * block_len), 1)
    upper = lane >= block_len
    integ = integ_ref[...]
    table = table_ref[...]
    sign = sign_ref[...].astype(jnp.float32)
    for row in range(picked_ref.shape[0]):
        mixed = jnp.dot(integ, picked_ref[row], preferred_element_type=jnp.float32)
        weighted = mixed * sign
        high = weighted.astype(jnp.bfloat16)
        low = (weighted - high.astype(jnp.float32)).astype(jnp.bfloat16)
        res = jnp.dot(table, high, preferred_element_type=jnp.float32) + jnp.dot(
            table, low, preferred_element_type=jnp.float32
        )
        folded = jnp.zeros((targets, 2 * block_len), jnp.float32)
        for s in range(src_blocks):
            lanes = (s // 2) * 2 * block_len
            piece = res[s * targets : (s + 1) * targets, lanes : lanes + 2 * block_len]
            keep = upper if s % 2 else jnp.logical_not(upper)
            folded = folded + jnp.where(keep, piece, 0.0)
        folded = folded + pltpu.roll(folded, block_len, 1)
        out_ref[row] = folded[:, :block_len]


def mix_block(integ_pad, picked, sign_q, table_all, targets, block_len):
    rows, pairs, width = picked.shape
    return pl.pallas_call(
        mix_kernel,
        out_shape=jax.ShapeDtypeStruct((rows, targets, block_len), jnp.float32),
        grid=(rows // ROWS,),
        in_specs=[
            pl.BlockSpec((pairs, pairs), lambda i: (0, 0)),
            pl.BlockSpec((ROWS, pairs, width), lambda i: (i, 0, 0)),
            pl.BlockSpec((pairs, width), lambda i: (0, 0)),
            pl.BlockSpec(table_all.shape, lambda i: (0, 0)),
        ],
        out_specs=pl.BlockSpec((ROWS, targets, block_len), lambda i: (i, 0, 0)),
        compiler_params=pltpu.CompilerParams(dimension_semantics=("arbitrary",)),
    )(integ_pad, picked, sign_q, table_all)


def on_device(
    coefficients, diagonal, integrals, alpha_row, alpha_sign, beta_block, beta_sign, block_irrep
):
    alpha_rank = lax.axis_index("alpha")
    pair_count = integrals.shape[0]
    local_rows, local_cols = coefficients.shape
    block_len = beta_sign.shape[1] // pair_count
    per_device = local_rows // block_len
    src_blocks = local_cols // block_len
    total_blocks = lax.axis_size("beta") * src_blocks
    pairs = -(-pair_count // 16) * 16
    extra = pairs - pair_count

    gathered = lax.all_gather(coefficients, "alpha", axis=0, tiled=True)
    live_flags = (block_irrep == 0).astype(jnp.int32)
    live_rows = jnp.repeat(live_flags, block_len)
    gathered = gathered * live_rows[:, None].astype(jnp.bfloat16)
    window_rows = gathered.shape[0]
    coeff_ext = jnp.concatenate(
        [gathered, -gathered, jnp.zeros((16, local_cols), jnp.bfloat16)], axis=0
    )
    zero_row = 2 * window_rows
    row_ext = jnp.where(
        alpha_sign == 0, zero_row, jnp.where(alpha_sign < 0, alpha_row + window_rows, alpha_row)
    )
    row_ext = jnp.pad(row_ext, ((0, extra), (0, 0)), constant_values=zero_row).T

    integ_pad = jnp.pad(integrals, ((0, extra), (0, extra)))
    sign_q = (
        beta_sign.reshape(src_blocks, pair_count, block_len)
        .transpose(1, 0, 2)
        .reshape(pair_count, local_cols)
    )
    sign_q = jnp.pad(sign_q, ((0, extra), (0, 0))).astype(jnp.bfloat16)
    target_iota = jnp.arange(total_blocks, dtype=jnp.int32)
    table_all = (target_iota[None, :, None] == beta_block[:, None, :]).astype(jnp.bfloat16)
    table_all = jnp.pad(
        table_all.reshape(src_blocks * total_blocks, pair_count), ((0, 0), (0, extra))
    )

    own_flags = lax.dynamic_slice_in_dim(live_flags, alpha_rank * per_device, per_device, 0)
    own_count = jnp.sum(own_flags)
    own_pos = jnp.cumsum(own_flags) - own_flags
    local_iota = jnp.arange(per_device, dtype=jnp.int32)

    dims = lax.GatherDimensionNumbers(
        offset_dims=(2,), collapsed_slice_dims=(0,), start_index_map=(0,)
    )

    def one_block(slot_idx, buffer):
        local_blk = jnp.sum(jnp.where((own_flags == 1) & (own_pos == slot_idx), local_iota, 0))
        first_row = (alpha_rank * per_device + local_blk) * block_len
        row_ids = lax.dynamic_slice_in_dim(row_ext, first_row, block_len, 0)
        picked = lax.gather(
            coeff_ext,
            row_ids[:, :, None],
            dims,
            slice_sizes=(1, local_cols),
            mode=lax.GatherScatterMode.PROMISE_IN_BOUNDS,
        )
        summed = mix_block(integ_pad, picked, sign_q, table_all, total_blocks, block_len)
        rows_out = summed.reshape(block_len, total_blocks * block_len)
        return lax.dynamic_update_index_in_dim(buffer, rows_out, local_blk, 0)

    empty = jnp.zeros((per_device, block_len, total_blocks * block_len), jnp.float32)
    buffer = lax.fori_loop(0, own_count, one_block, empty)
    summed = lax.psum_scatter(buffer, "beta", scatter_dimension=2, tiled=True)
    placed = summed.reshape(local_rows, local_cols)
    own_live_rows = jnp.repeat(own_flags, block_len)
    total = diagonal * coefficients.astype(jnp.float32) + placed
    return jnp.where(own_live_rows[:, None] == 1, total, jnp.zeros_like(total))


def solution(mesh):
    return jax.shard_map(
        on_device,
        mesh=mesh,
        in_specs=(
            P("alpha", "beta"),
            P("alpha", "beta"),
            P(),
            P(),
            P(),
            P("beta", None),
            P("beta", None),
            P(),
        ),
        out_specs=P("alpha", "beta"),
        check_vma=False,
    )
```

```python
import jax
import jax.numpy as jnp
from jax import lax
from jax.experimental import pallas as pl
from jax.experimental.pallas import tpu as pltpu
from jax.sharding import Mesh
from jax.sharding import PartitionSpec as P

ROWS = 8
PAIR = 2


def mix_kernel(integ_ref, picked_ref, sign_ref, table_ref, out_ref):
    halves, _, width = sign_ref.shape
    targets = out_ref.shape[1]
    block_len = out_ref.shape[2]
    src_blocks = width // block_len
    lane = lax.broadcasted_iota(jnp.int32, (targets, 2 * block_len), 1)
    upper = lane >= block_len
    integ = integ_ref[...]
    for row in range(picked_ref.shape[0]):
        mixed = jnp.dot(integ, picked_ref[row], preferred_element_type=jnp.float32)
        folded = jnp.zeros((targets, 2 * block_len), jnp.float32)
        for half in range(halves):
            weighted = mixed[:, half * width : (half + 1) * width] * sign_ref[half].astype(
                jnp.float32
            )
            high = weighted.astype(jnp.bfloat16)
            low = (weighted - high.astype(jnp.float32)).astype(jnp.bfloat16)
            table = table_ref[half]
            res = jnp.dot(table, high, preferred_element_type=jnp.float32) + jnp.dot(
                table, low, preferred_element_type=jnp.float32
            )
            for s in range(src_blocks):
                lanes = (s // 2) * 2 * block_len
                piece = res[s * targets : (s + 1) * targets, lanes : lanes + 2 * block_len]
                keep = upper if s % 2 else jnp.logical_not(upper)
                folded = folded + jnp.where(keep, piece, 0.0)
        folded = folded + pltpu.roll(folded, block_len, 1)
        out_ref[row] = folded[:, :block_len]


def mix_block(integ_pad, picked, sign_q, table_all, targets, block_len):
    rows, pairs, width = picked.shape
    return pl.pallas_call(
        mix_kernel,
        out_shape=jax.ShapeDtypeStruct((rows, targets, block_len), jnp.float32),
        grid=(rows // ROWS,),
        in_specs=[
            pl.BlockSpec((pairs, pairs), lambda i: (0, 0)),
            pl.BlockSpec((ROWS, pairs, width), lambda i: (i, 0, 0)),
            pl.BlockSpec(sign_q.shape, lambda i: (0, 0, 0)),
            pl.BlockSpec(table_all.shape, lambda i: (0, 0, 0)),
        ],
        out_specs=pl.BlockSpec((ROWS, targets, block_len), lambda i: (i, 0, 0)),
        compiler_params=pltpu.CompilerParams(dimension_semantics=("arbitrary",)),
    )(integ_pad, picked, sign_q, table_all)


def on_device(
    coefficients, diagonal, integrals, alpha_row, alpha_sign, beta_block, beta_sign, block_irrep
):
    alpha_rank = lax.axis_index("alpha")
    member = lax.axis_index("m")
    pair_count = integrals.shape[0]
    local_rows, local_cols = coefficients.shape
    block_len = beta_sign.shape[1] // pair_count
    per_device = local_rows // block_len
    src_blocks = local_cols // block_len
    total_blocks = lax.axis_size("g") * PAIR * src_blocks
    pairs = -(-pair_count // 16) * 16
    extra = pairs - pair_count
    sub_rows = block_len // PAIR

    gathered = lax.all_gather(coefficients, "alpha", axis=0, tiled=True)
    live_flags = (block_irrep == 0).astype(jnp.int32)
    live_rows = jnp.repeat(live_flags, block_len)
    gathered = gathered * live_rows[:, None].astype(jnp.bfloat16)
    gathered = lax.all_gather(gathered, "m", axis=1, tiled=True)
    window_rows, wide_cols = gathered.shape
    coeff_ext = jnp.concatenate(
        [gathered, -gathered, jnp.zeros((16, wide_cols), jnp.bfloat16)], axis=0
    )
    zero_row = 2 * window_rows
    row_ext = jnp.where(
        alpha_sign == 0, zero_row, jnp.where(alpha_sign < 0, alpha_row + window_rows, alpha_row)
    )
    row_ext = jnp.pad(row_ext, ((0, extra), (0, 0)), constant_values=zero_row).T

    integ_pad = jnp.pad(integrals, ((0, extra), (0, extra)))
    beta_block2 = lax.all_gather(beta_block, "m", axis=0, tiled=True)
    beta_sign2 = lax.all_gather(beta_sign, "m", axis=0, tiled=True)
    sign_q = (
        beta_sign2.reshape(PAIR, src_blocks, pair_count, block_len)
        .transpose(0, 2, 1, 3)
        .reshape(PAIR, pair_count, local_cols)
    )
    sign_q = jnp.pad(sign_q, ((0, 0), (0, extra), (0, 0))).astype(jnp.bfloat16)
    target_iota = jnp.arange(total_blocks, dtype=jnp.int32)
    table_all = (target_iota[None, :, None] == beta_block2[:, None, :]).astype(jnp.bfloat16)
    table_all = jnp.pad(
        table_all.reshape(PAIR, src_blocks * total_blocks, pair_count),
        ((0, 0), (0, 0), (0, extra)),
    )

    own_flags = lax.dynamic_slice_in_dim(live_flags, alpha_rank * per_device, per_device, 0)
    own_count = jnp.sum(own_flags)
    own_pos = jnp.cumsum(own_flags) - own_flags
    local_iota = jnp.arange(per_device, dtype=jnp.int32)

    dims = lax.GatherDimensionNumbers(
        offset_dims=(2,), collapsed_slice_dims=(0,), start_index_map=(0,)
    )

    def one_block(slot_idx, buffer):
        local_blk = jnp.sum(jnp.where((own_flags == 1) & (own_pos == slot_idx), local_iota, 0))
        first_row = (alpha_rank * per_device + local_blk) * block_len + member * sub_rows
        row_ids = lax.dynamic_slice_in_dim(row_ext, first_row, sub_rows, 0)
        picked = lax.gather(
            coeff_ext,
            row_ids[:, :, None],
            dims,
            slice_sizes=(1, wide_cols),
            mode=lax.GatherScatterMode.PROMISE_IN_BOUNDS,
        )
        summed = mix_block(integ_pad, picked, sign_q, table_all, total_blocks, block_len)
        rows_out = summed.reshape(sub_rows, total_blocks * block_len)
        return lax.dynamic_update_index_in_dim(buffer, rows_out, local_blk, 0)

    empty = jnp.zeros((per_device, sub_rows, total_blocks * block_len), jnp.float32)
    buffer = lax.fori_loop(0, own_count, one_block, empty)
    summed = lax.psum_scatter(buffer, "g", scatter_dimension=2, tiled=True)
    summed = lax.all_to_all(summed, "m", 2, 1, tiled=True)
    placed = summed.reshape(local_rows, local_cols)
    own_live_rows = jnp.repeat(own_flags, block_len)
    total = diagonal * coefficients.astype(jnp.float32) + placed
    return jnp.where(own_live_rows[:, None] == 1, total, jnp.zeros_like(total))


def solution(mesh):
    alpha_size, beta_size = mesh.devices.shape
    split_mesh = Mesh(
        mesh.devices.reshape(alpha_size, beta_size // PAIR, PAIR), ("alpha", "g", "m")
    )
    beta = ("g", "m")
    return jax.shard_map(
        on_device,
        mesh=split_mesh,
        in_specs=(
            P("alpha", beta),
            P("alpha", beta),
            P(),
            P(),
            P(),
            P(beta, None),
            P(beta, None),
            P(),
        ),
        out_specs=P("alpha", beta),
        check_vma=False,
    )
```

```python
import jax
import jax.numpy as jnp
from jax import lax
from jax.experimental import pallas as pl
from jax.experimental.pallas import tpu as pltpu
from jax.sharding import Mesh
from jax.sharding import PartitionSpec as P

ROWS = 8
PAIR = 2


def mix_kernel(integ_ref, picked_ref, sign_ref, table_ref, out_ref):
    halves, _, width = sign_ref.shape
    targets = out_ref.shape[1]
    block_len = out_ref.shape[2]
    src_blocks = width // block_len
    lane = lax.broadcasted_iota(jnp.int32, (targets, 2 * block_len), 1)
    upper = lane >= block_len
    integ = integ_ref[...]
    for row in range(picked_ref.shape[0]):
        mixed = jnp.dot(integ, picked_ref[row], preferred_element_type=jnp.float32)
        folded = jnp.zeros((targets, 2 * block_len), jnp.float32)
        for half in range(halves):
            weighted = mixed[:, half * width : (half + 1) * width] * sign_ref[half].astype(
                jnp.float32
            )
            high = weighted.astype(jnp.bfloat16)
            low = (weighted - high.astype(jnp.float32)).astype(jnp.bfloat16)
            table = table_ref[half]
            res = jnp.dot(table, high, preferred_element_type=jnp.float32) + jnp.dot(
                table, low, preferred_element_type=jnp.float32
            )
            for s in range(src_blocks):
                lanes = (s // 2) * 2 * block_len
                piece = res[s * targets : (s + 1) * targets, lanes : lanes + 2 * block_len]
                keep = upper if s % 2 else jnp.logical_not(upper)
                folded = folded + jnp.where(keep, piece, 0.0)
        folded = folded + pltpu.roll(folded, block_len, 1)
        out_ref[row] = folded[:, :block_len]


def mix_block(integ_pad, picked, sign_q, table_all, targets, block_len):
    rows, pairs, width = picked.shape
    return pl.pallas_call(
        mix_kernel,
        out_shape=jax.ShapeDtypeStruct((rows, targets, block_len), jnp.float32),
        grid=(rows // ROWS,),
        in_specs=[
            pl.BlockSpec((pairs, pairs), lambda i: (0, 0)),
            pl.BlockSpec((ROWS, pairs, width), lambda i: (i, 0, 0)),
            pl.BlockSpec(sign_q.shape, lambda i: (0, 0, 0)),
            pl.BlockSpec(table_all.shape, lambda i: (0, 0, 0)),
        ],
        out_specs=pl.BlockSpec((ROWS, targets, block_len), lambda i: (i, 0, 0)),
        compiler_params=pltpu.CompilerParams(dimension_semantics=("arbitrary",)),
    )(integ_pad, picked, sign_q, table_all)


def on_device(
    coefficients, diagonal, integrals, alpha_row, alpha_sign, beta_block, beta_sign, block_irrep
):
    alpha_rank = lax.axis_index("alpha")
    member = lax.axis_index("m")
    pair_count = integrals.shape[0]
    local_rows, local_cols = coefficients.shape
    block_len = beta_sign.shape[1] // pair_count
    per_device = local_rows // block_len
    src_blocks = local_cols // block_len
    total_blocks = lax.axis_size("g") * PAIR * src_blocks
    pairs = -(-pair_count // 16) * 16
    extra = pairs - pair_count
    sub_rows = block_len // PAIR

    gathered = lax.all_gather(coefficients, "alpha", axis=0, tiled=True)
    live_flags = (block_irrep == 0).astype(jnp.int32)
    live_rows = jnp.repeat(live_flags, block_len)
    gathered = gathered * live_rows[:, None].astype(jnp.bfloat16)
    gathered = lax.all_gather(gathered, "m", axis=1, tiled=True)
    window_rows, wide_cols = gathered.shape
    coeff_ext = jnp.concatenate(
        [gathered, -gathered, jnp.zeros((16, wide_cols), jnp.bfloat16)], axis=0
    )
    zero_row = 2 * window_rows
    row_ext = jnp.where(
        alpha_sign == 0, zero_row, jnp.where(alpha_sign < 0, alpha_row + window_rows, alpha_row)
    )
    row_ext = jnp.pad(row_ext, ((0, extra), (0, 0)), constant_values=zero_row).T

    integ_pad = jnp.pad(integrals, ((0, extra), (0, extra)))
    beta_block2 = lax.all_gather(beta_block, "m", axis=0, tiled=True)
    beta_sign2 = lax.all_gather(beta_sign, "m", axis=0, tiled=True)
    sign_q = (
        beta_sign2.reshape(PAIR, src_blocks, pair_count, block_len)
        .transpose(0, 2, 1, 3)
        .reshape(PAIR, pair_count, local_cols)
    )
    sign_q = jnp.pad(sign_q, ((0, 0), (0, extra), (0, 0))).astype(jnp.bfloat16)
    target_iota = jnp.arange(total_blocks, dtype=jnp.int32)
    table_all = (target_iota[None, :, None] == beta_block2[:, None, :]).astype(jnp.bfloat16)
    table_all = jnp.pad(
        table_all.reshape(PAIR, src_blocks * total_blocks, pair_count),
        ((0, 0), (0, 0), (0, extra)),
    )

    own_flags = lax.dynamic_slice_in_dim(live_flags, alpha_rank * per_device, per_device, 0)
    own_count = jnp.sum(own_flags)
    own_pos = jnp.cumsum(own_flags) - own_flags
    local_iota = jnp.arange(per_device, dtype=jnp.int32)

    dims = lax.GatherDimensionNumbers(
        offset_dims=(2,), collapsed_slice_dims=(0,), start_index_map=(0,)
    )

    def one_block(slot_idx, buffer):
        local_blk = jnp.sum(jnp.where((own_flags == 1) & (own_pos == slot_idx), local_iota, 0))
        first_row = (alpha_rank * per_device + local_blk) * block_len + member * sub_rows
        row_ids = lax.dynamic_slice_in_dim(row_ext, first_row, sub_rows, 0)
        picked = lax.gather(
            coeff_ext,
            row_ids[:, :, None],
            dims,
            slice_sizes=(1, wide_cols),
            mode=lax.GatherScatterMode.PROMISE_IN_BOUNDS,
        )
        summed = mix_block(integ_pad, picked, sign_q, table_all, total_blocks, block_len)
        rows_out = summed.reshape(sub_rows, total_blocks * block_len)
        return lax.dynamic_update_slice(
            buffer, rows_out[None], (local_blk, member * sub_rows, 0)
        )

    empty = jnp.zeros((per_device, block_len, total_blocks * block_len), jnp.float32)
    buffer = lax.fori_loop(0, own_count, one_block, empty)
    summed = lax.psum_scatter(buffer, ("g", "m"), scatter_dimension=2, tiled=True)
    placed = summed.reshape(local_rows, local_cols)
    own_live_rows = jnp.repeat(own_flags, block_len)
    total = diagonal * coefficients.astype(jnp.float32) + placed
    return jnp.where(own_live_rows[:, None] == 1, total, jnp.zeros_like(total))


def solution(mesh):
    alpha_size, beta_size = mesh.devices.shape
    split_mesh = Mesh(
        mesh.devices.reshape(alpha_size, beta_size // PAIR, PAIR), ("alpha", "g", "m")
    )
    beta = ("g", "m")
    return jax.shard_map(
        on_device,
        mesh=split_mesh,
        in_specs=(
            P("alpha", beta),
            P("alpha", beta),
            P(),
            P(),
            P(),
            P(beta, None),
            P(beta, None),
            P(),
        ),
        out_specs=P("alpha", beta),
        check_vma=False,
    )
```

```python
import jax
import jax.numpy as jnp
from jax import lax
from jax.experimental import pallas as pl
from jax.experimental.pallas import tpu as pltpu
from jax.sharding import Mesh
from jax.sharding import PartitionSpec as P

ROWS = 8
PAIR = 2


def mix_kernel(integ_ref, picked_ref, sign_ref, table_ref, out_ref):
    halves, _, width = sign_ref.shape
    targets = out_ref.shape[1]
    block_len = out_ref.shape[2]
    src_blocks = width // block_len
    lane = lax.broadcasted_iota(jnp.int32, (targets, 2 * block_len), 1)
    upper = lane >= block_len
    integ = integ_ref[...]
    for row in range(picked_ref.shape[0]):
        mixed = jnp.dot(integ, picked_ref[row], preferred_element_type=jnp.float32)
        folded = jnp.zeros((targets, 2 * block_len), jnp.float32)
        for half in range(halves):
            weighted = mixed[:, half * width : (half + 1) * width] * sign_ref[half].astype(
                jnp.float32
            )
            high = weighted.astype(jnp.bfloat16)
            low = (weighted - high.astype(jnp.float32)).astype(jnp.bfloat16)
            table = table_ref[half]
            res = jnp.dot(table, high, preferred_element_type=jnp.float32) + jnp.dot(
                table, low, preferred_element_type=jnp.float32
            )
            for s in range(src_blocks):
                lanes = (s // 2) * 2 * block_len
                piece = res[s * targets : (s + 1) * targets, lanes : lanes + 2 * block_len]
                keep = upper if s % 2 else jnp.logical_not(upper)
                folded = folded + jnp.where(keep, piece, 0.0)
        folded = folded + pltpu.roll(folded, block_len, 1)
        out_ref[row] = folded[:, :block_len]


def mix_block(integ_pad, picked, sign_q, table_all, targets, block_len):
    rows, pairs, width = picked.shape
    return pl.pallas_call(
        mix_kernel,
        out_shape=jax.ShapeDtypeStruct((rows, targets, block_len), jnp.float32),
        grid=(rows // ROWS,),
        in_specs=[
            pl.BlockSpec((pairs, pairs), lambda i: (0, 0)),
            pl.BlockSpec((ROWS, pairs, width), lambda i: (i, 0, 0)),
            pl.BlockSpec(sign_q.shape, lambda i: (0, 0, 0)),
            pl.BlockSpec(table_all.shape, lambda i: (0, 0, 0)),
        ],
        out_specs=pl.BlockSpec((ROWS, targets, block_len), lambda i: (i, 0, 0)),
        compiler_params=pltpu.CompilerParams(dimension_semantics=("arbitrary",)),
    )(integ_pad, picked, sign_q, table_all)


def on_device(
    coefficients, diagonal, integrals, alpha_row, alpha_sign, beta_block, beta_sign, block_irrep
):
    alpha_rank = lax.axis_index("alpha")
    member = lax.axis_index("m")
    pair_count = integrals.shape[0]
    local_rows, local_cols = coefficients.shape
    block_len = beta_sign.shape[1] // pair_count
    per_device = local_rows // block_len
    src_blocks = local_cols // block_len
    total_blocks = lax.axis_size("g") * PAIR * src_blocks
    pairs = -(-pair_count // 16) * 16
    extra = pairs - pair_count
    sub_rows = block_len // PAIR

    gathered = lax.all_gather(coefficients, "alpha", axis=0, tiled=True)
    live_flags = (block_irrep == 0).astype(jnp.int32)
    live_rows = jnp.repeat(live_flags, block_len)
    gathered = gathered * live_rows[:, None].astype(jnp.bfloat16)
    gathered = lax.all_gather(gathered, "m", axis=1, tiled=True)
    window_rows, wide_cols = gathered.shape
    coeff_ext = jnp.concatenate(
        [gathered, -gathered, jnp.zeros((16, wide_cols), jnp.bfloat16)], axis=0
    )
    zero_row = 2 * window_rows
    row_ext = jnp.where(
        alpha_sign == 0, zero_row, jnp.where(alpha_sign < 0, alpha_row + window_rows, alpha_row)
    )
    row_ext = jnp.pad(row_ext, ((0, extra), (0, 0)), constant_values=zero_row).T

    integ_pad = jnp.pad(integrals, ((0, extra), (0, extra)))
    beta_block2 = lax.all_gather(beta_block, "m", axis=0, tiled=True)
    beta_sign2 = lax.all_gather(beta_sign, "m", axis=0, tiled=True)
    sign_q = (
        beta_sign2.reshape(PAIR, src_blocks, pair_count, block_len)
        .transpose(0, 2, 1, 3)
        .reshape(PAIR, pair_count, local_cols)
    )
    sign_q = jnp.pad(sign_q, ((0, 0), (0, extra), (0, 0))).astype(jnp.bfloat16)
    target_iota = jnp.arange(total_blocks, dtype=jnp.int32)
    table_all = (target_iota[None, :, None] == beta_block2[:, None, :]).astype(jnp.bfloat16)
    table_all = jnp.pad(
        table_all.reshape(PAIR, src_blocks * total_blocks, pair_count),
        ((0, 0), (0, 0), (0, extra)),
    )

    own_flags = lax.dynamic_slice_in_dim(live_flags, alpha_rank * per_device, per_device, 0)

    dims = lax.GatherDimensionNumbers(
        offset_dims=(2,), collapsed_slice_dims=(0,), start_index_map=(0,)
    )

    parts = []
    for local_blk in range(per_device):
        first_row = (alpha_rank * per_device + local_blk) * block_len + member * sub_rows
        row_ids = lax.dynamic_slice_in_dim(row_ext, first_row, sub_rows, 0)
        picked = lax.gather(
            coeff_ext,
            row_ids[:, :, None],
            dims,
            slice_sizes=(1, wide_cols),
            mode=lax.GatherScatterMode.PROMISE_IN_BOUNDS,
        )
        summed = mix_block(integ_pad, picked, sign_q, table_all, total_blocks, block_len)
        rows_out = summed.reshape(sub_rows, total_blocks * block_len)
        full = lax.dynamic_update_slice(
            jnp.zeros((block_len, total_blocks * block_len), jnp.float32),
            rows_out,
            (member * sub_rows, 0),
        )
        parts.append(lax.psum_scatter(full, ("g", "m"), scatter_dimension=1, tiled=True))
    placed = jnp.concatenate(parts, axis=0)
    own_live_rows = jnp.repeat(own_flags, block_len)
    total = diagonal * coefficients.astype(jnp.float32) + placed
    return jnp.where(own_live_rows[:, None] == 1, total, jnp.zeros_like(total))


def solution(mesh):
    alpha_size, beta_size = mesh.devices.shape
    split_mesh = Mesh(
        mesh.devices.reshape(alpha_size, beta_size // PAIR, PAIR), ("alpha", "g", "m")
    )
    beta = ("g", "m")
    return jax.shard_map(
        on_device,
        mesh=split_mesh,
        in_specs=(
            P("alpha", beta),
            P("alpha", beta),
            P(),
            P(),
            P(),
            P(beta, None),
            P(beta, None),
            P(),
        ),
        out_specs=P("alpha", beta),
        check_vma=False,
    )
```

```python
import jax
import jax.numpy as jnp
from jax import lax
from jax.experimental import pallas as pl
from jax.experimental.pallas import tpu as pltpu
from jax.sharding import Mesh
from jax.sharding import PartitionSpec as P

ROWS = 8
PAIR = 2


def mix_kernel(integ_ref, picked_ref, sign_ref, table_ref, out_ref):
    halves, _, width = sign_ref.shape
    targets = out_ref.shape[1]
    block_len = out_ref.shape[2]
    src_blocks = width // block_len
    lane = lax.broadcasted_iota(jnp.int32, (targets, 2 * block_len), 1)
    upper = lane >= block_len
    integ = integ_ref[...]
    for row in range(picked_ref.shape[0]):
        mixed = jnp.dot(integ, picked_ref[row], preferred_element_type=jnp.float32)
        folded = jnp.zeros((targets, 2 * block_len), jnp.float32)
        for half in range(halves):
            weighted = mixed[:, half * width : (half + 1) * width] * sign_ref[half].astype(
                jnp.float32
            )
            high = weighted.astype(jnp.bfloat16)
            low = (weighted - high.astype(jnp.float32)).astype(jnp.bfloat16)
            table = table_ref[half]
            res = jnp.dot(table, high, preferred_element_type=jnp.float32) + jnp.dot(
                table, low, preferred_element_type=jnp.float32
            )
            for s in range(src_blocks):
                lanes = (s // 2) * 2 * block_len
                piece = res[s * targets : (s + 1) * targets, lanes : lanes + 2 * block_len]
                keep = upper if s % 2 else jnp.logical_not(upper)
                folded = folded + jnp.where(keep, piece, 0.0)
        folded = folded + pltpu.roll(folded, block_len, 1)
        out_ref[row] = folded[:, :block_len]


def mix_block(integ_pad, picked, sign_q, table_all, targets, block_len):
    rows, pairs, width = picked.shape
    return pl.pallas_call(
        mix_kernel,
        out_shape=jax.ShapeDtypeStruct((rows, targets, block_len), jnp.float32),
        grid=(rows // ROWS,),
        in_specs=[
            pl.BlockSpec((pairs, pairs), lambda i: (0, 0)),
            pl.BlockSpec((ROWS, pairs, width), lambda i: (i, 0, 0)),
            pl.BlockSpec(sign_q.shape, lambda i: (0, 0, 0)),
            pl.BlockSpec(table_all.shape, lambda i: (0, 0, 0)),
        ],
        out_specs=pl.BlockSpec((ROWS, targets, block_len), lambda i: (i, 0, 0)),
        compiler_params=pltpu.CompilerParams(dimension_semantics=("arbitrary",)),
    )(integ_pad, picked, sign_q, table_all)


def exchange_kernel(send_ref, recv_ref, send_sem, recv_sem, local_sem):
    groups = lax.axis_size("g")
    count = groups * PAIR
    alpha = lax.axis_index("alpha")
    me = lax.axis_index("g") * PAIR + lax.axis_index("m")

    def remote(slot, peer):
        return pltpu.make_async_remote_copy(
            src_ref=send_ref.at[slot],
            dst_ref=recv_ref.at[slot],
            send_sem=send_sem.at[slot],
            recv_sem=recv_sem.at[slot],
            device_id=(alpha, peer // PAIR, peer % PAIR),
            device_id_type=pl.DeviceIdType.MESH,
        )

    for step in range(1, count):
        dest = lax.rem(me + step, count)
        pltpu.make_async_remote_copy(
            src_ref=send_ref.at[dest],
            dst_ref=recv_ref.at[me],
            send_sem=send_sem.at[dest],
            recv_sem=recv_sem.at[me],
            device_id=(alpha, dest // PAIR, dest % PAIR),
            device_id_type=pl.DeviceIdType.MESH,
        ).start()
    local = pltpu.make_async_copy(send_ref.at[me], recv_ref.at[me], local_sem)
    local.start()
    local.wait()
    for step in range(1, count):
        dest = lax.rem(me + step, count)
        remote(dest, dest).wait_send()
    for step in range(1, count):
        src = lax.rem(me + count - step, count)
        remote(src, src).wait_recv()


def exchange(send):
    count = send.shape[0]
    return pl.pallas_call(
        exchange_kernel,
        out_shape=jax.ShapeDtypeStruct(send.shape, send.dtype),
        in_specs=[pl.BlockSpec(memory_space=pl.ANY)],
        out_specs=pl.BlockSpec(memory_space=pl.ANY),
        scratch_shapes=[
            pltpu.SemaphoreType.DMA((count,)),
            pltpu.SemaphoreType.DMA((count,)),
            pltpu.SemaphoreType.DMA,
        ],
        compiler_params=pltpu.CompilerParams(has_side_effects=True),
    )(send)


def on_device(
    coefficients, diagonal, integrals, alpha_row, alpha_sign, beta_block, beta_sign, block_irrep
):
    alpha_rank = lax.axis_index("alpha")
    member = lax.axis_index("m")
    pair_count = integrals.shape[0]
    local_rows, local_cols = coefficients.shape
    block_len = beta_sign.shape[1] // pair_count
    per_device = local_rows // block_len
    src_blocks = local_cols // block_len
    total_blocks = lax.axis_size("g") * PAIR * src_blocks
    pairs = -(-pair_count // 16) * 16
    extra = pairs - pair_count
    sub_rows = block_len // PAIR

    gathered = lax.all_gather(coefficients, "alpha", axis=0, tiled=True)
    live_flags = (block_irrep == 0).astype(jnp.int32)
    live_rows = jnp.repeat(live_flags, block_len)
    gathered = gathered * live_rows[:, None].astype(jnp.bfloat16)
    gathered = lax.all_gather(gathered, "m", axis=1, tiled=True)
    window_rows, wide_cols = gathered.shape
    coeff_ext = jnp.concatenate(
        [gathered, -gathered, jnp.zeros((16, wide_cols), jnp.bfloat16)], axis=0
    )
    zero_row = 2 * window_rows
    row_ext = jnp.where(
        alpha_sign == 0, zero_row, jnp.where(alpha_sign < 0, alpha_row + window_rows, alpha_row)
    )
    row_ext = jnp.pad(row_ext, ((0, extra), (0, 0)), constant_values=zero_row).T

    integ_pad = jnp.pad(integrals, ((0, extra), (0, extra)))
    beta_block2 = lax.all_gather(beta_block, "m", axis=0, tiled=True)
    beta_sign2 = lax.all_gather(beta_sign, "m", axis=0, tiled=True)
    sign_q = (
        beta_sign2.reshape(PAIR, src_blocks, pair_count, block_len)
        .transpose(0, 2, 1, 3)
        .reshape(PAIR, pair_count, local_cols)
    )
    sign_q = jnp.pad(sign_q, ((0, 0), (0, extra), (0, 0))).astype(jnp.bfloat16)
    target_iota = jnp.arange(total_blocks, dtype=jnp.int32)
    table_all = (target_iota[None, :, None] == beta_block2[:, None, :]).astype(jnp.bfloat16)
    table_all = jnp.pad(
        table_all.reshape(PAIR, src_blocks * total_blocks, pair_count),
        ((0, 0), (0, 0), (0, extra)),
    )

    own_flags = lax.dynamic_slice_in_dim(live_flags, alpha_rank * per_device, per_device, 0)

    dims = lax.GatherDimensionNumbers(
        offset_dims=(2,), collapsed_slice_dims=(0,), start_index_map=(0,)
    )

    parts = []
    for local_blk in range(per_device):
        first_row = (alpha_rank * per_device + local_blk) * block_len + member * sub_rows
        row_ids = lax.dynamic_slice_in_dim(row_ext, first_row, sub_rows, 0)
        picked = lax.gather(
            coeff_ext,
            row_ids[:, :, None],
            dims,
            slice_sizes=(1, wide_cols),
            mode=lax.GatherScatterMode.PROMISE_IN_BOUNDS,
        )
        summed = mix_block(integ_pad, picked, sign_q, table_all, total_blocks, block_len)
        parts.append(
            summed.reshape(sub_rows, total_blocks // src_blocks, local_cols).transpose(1, 0, 2)
        )
    send = jnp.stack(parts, axis=1)
    recv = exchange(send)
    groups = recv.shape[0] // PAIR
    recv = recv.reshape(groups, PAIR, per_device, sub_rows, local_cols).sum(axis=0)
    placed = recv.transpose(1, 0, 2, 3).reshape(local_rows, local_cols)
    own_live_rows = jnp.repeat(own_flags, block_len)
    total = diagonal * coefficients.astype(jnp.float32) + placed
    return jnp.where(own_live_rows[:, None] == 1, total, jnp.zeros_like(total))


def solution(mesh):
    alpha_size, beta_size = mesh.devices.shape
    split_mesh = Mesh(
        mesh.devices.reshape(alpha_size, beta_size // PAIR, PAIR), ("alpha", "g", "m")
    )
    beta = ("g", "m")
    return jax.shard_map(
        on_device,
        mesh=split_mesh,
        in_specs=(
            P("alpha", beta),
            P("alpha", beta),
            P(),
            P(),
            P(),
            P(beta, None),
            P(beta, None),
            P(),
        ),
        out_specs=P("alpha", beta),
        check_vma=False,
    )
```

```python
import jax
import jax.numpy as jnp
from jax import lax
from jax.experimental import pallas as pl
from jax.experimental.pallas import tpu as pltpu
from jax.sharding import Mesh
from jax.sharding import PartitionSpec as P

ROWS = 8
PAIR = 2


def mix_kernel(integ_ref, picked_ref, sign_ref, table_ref, out_ref):
    halves, _, width = sign_ref.shape
    targets = out_ref.shape[1]
    block_len = out_ref.shape[2]
    src_blocks = width // block_len
    lane = lax.broadcasted_iota(jnp.int32, (targets, 2 * block_len), 1)
    upper = lane >= block_len
    integ = integ_ref[...]
    for row in range(picked_ref.shape[0]):
        mixed = jnp.dot(integ, picked_ref[row], preferred_element_type=jnp.float32)
        folded = jnp.zeros((targets, 2 * block_len), jnp.float32)
        for half in range(halves):
            weighted = mixed[:, half * width : (half + 1) * width] * sign_ref[half].astype(
                jnp.float32
            )
            high = weighted.astype(jnp.bfloat16)
            low = (weighted - high.astype(jnp.float32)).astype(jnp.bfloat16)
            table = table_ref[half]
            res = jnp.dot(table, high, preferred_element_type=jnp.float32) + jnp.dot(
                table, low, preferred_element_type=jnp.float32
            )
            for s in range(src_blocks):
                lanes = (s // 2) * 2 * block_len
                piece = res[s * targets : (s + 1) * targets, lanes : lanes + 2 * block_len]
                keep = upper if s % 2 else jnp.logical_not(upper)
                folded = folded + jnp.where(keep, piece, 0.0)
        folded = folded + pltpu.roll(folded, block_len, 1)
        out_ref[row] = folded[:, :block_len]


def mix_block(integ_pad, picked, sign_q, table_all, targets, block_len):
    rows, pairs, width = picked.shape
    return pl.pallas_call(
        mix_kernel,
        out_shape=jax.ShapeDtypeStruct((rows, targets, block_len), jnp.float32),
        grid=(rows // ROWS,),
        in_specs=[
            pl.BlockSpec((pairs, pairs), lambda i: (0, 0)),
            pl.BlockSpec((ROWS, pairs, width), lambda i: (i, 0, 0)),
            pl.BlockSpec(sign_q.shape, lambda i: (0, 0, 0)),
            pl.BlockSpec(table_all.shape, lambda i: (0, 0, 0)),
        ],
        out_specs=pl.BlockSpec((ROWS, targets, block_len), lambda i: (i, 0, 0)),
        compiler_params=pltpu.CompilerParams(dimension_semantics=("arbitrary",)),
    )(integ_pad, picked, sign_q, table_all)


def exchange_kernel(send_ref, recv_ref, send_sem, recv_sem, local_sem):
    groups = lax.axis_size("g")
    count = groups * PAIR
    alpha = lax.axis_index("alpha")
    me = lax.axis_index("g") * PAIR + lax.axis_index("m")

    def remote(slot, peer):
        return pltpu.make_async_remote_copy(
            src_ref=send_ref.at[slot],
            dst_ref=recv_ref.at[slot],
            send_sem=send_sem.at[slot],
            recv_sem=recv_sem.at[slot],
            device_id=(alpha, peer // PAIR, peer % PAIR),
            device_id_type=pl.DeviceIdType.MESH,
        )

    for step in range(1, count):
        dest = lax.rem(me + step, count)
        pltpu.make_async_remote_copy(
            src_ref=send_ref.at[dest],
            dst_ref=recv_ref.at[me],
            send_sem=send_sem.at[dest],
            recv_sem=recv_sem.at[me],
            device_id=(alpha, dest // PAIR, dest % PAIR),
            device_id_type=pl.DeviceIdType.MESH,
        ).start()
    local = pltpu.make_async_copy(send_ref.at[me], recv_ref.at[me], local_sem)
    local.start()
    local.wait()
    for step in range(1, count):
        dest = lax.rem(me + step, count)
        remote(dest, dest).wait_send()
    for step in range(1, count):
        src = lax.rem(me + count - step, count)
        remote(src, src).wait_recv()


def exchange(send):
    count = send.shape[0]
    return pl.pallas_call(
        exchange_kernel,
        out_shape=jax.ShapeDtypeStruct(send.shape, send.dtype),
        in_specs=[pl.BlockSpec(memory_space=pl.ANY)],
        out_specs=pl.BlockSpec(memory_space=pl.ANY),
        scratch_shapes=[
            pltpu.SemaphoreType.DMA((count,)),
            pltpu.SemaphoreType.DMA((count,)),
            pltpu.SemaphoreType.DMA,
        ],
        compiler_params=pltpu.CompilerParams(has_side_effects=True),
    )(send)


def spread_kernel(own_ref, out_ref, send_sem, recv_sem, local_sem):
    count = lax.axis_size("alpha") * PAIR
    group = lax.axis_index("g")
    me = lax.axis_index("alpha") * PAIR + lax.axis_index("m")

    def remote(slot, sem_slot, peer):
        return pltpu.make_async_remote_copy(
            src_ref=own_ref,
            dst_ref=out_ref.at[slot],
            send_sem=send_sem.at[sem_slot],
            recv_sem=recv_sem.at[slot],
            device_id=(peer // PAIR, group, peer % PAIR),
            device_id_type=pl.DeviceIdType.MESH,
        )

    for step in range(1, count):
        dest = lax.rem(me + step, count)
        remote(me, dest, dest).start()
    local = pltpu.make_async_copy(own_ref, out_ref.at[me], local_sem)
    local.start()
    local.wait()
    for step in range(1, count):
        dest = lax.rem(me + step, count)
        remote(me, dest, dest).wait_send()
    for step in range(1, count):
        src = lax.rem(me + count - step, count)
        remote(src, src, src).wait_recv()


def spread(own, count):
    return pl.pallas_call(
        spread_kernel,
        out_shape=jax.ShapeDtypeStruct((count,) + own.shape, own.dtype),
        in_specs=[pl.BlockSpec(memory_space=pl.ANY)],
        out_specs=pl.BlockSpec(memory_space=pl.ANY),
        scratch_shapes=[
            pltpu.SemaphoreType.DMA((count,)),
            pltpu.SemaphoreType.DMA((count,)),
            pltpu.SemaphoreType.DMA,
        ],
        compiler_params=pltpu.CompilerParams(has_side_effects=True),
    )(own)


def on_device(
    coefficients, diagonal, integrals, alpha_row, alpha_sign, beta_block, beta_sign, block_irrep
):
    alpha_rank = lax.axis_index("alpha")
    member = lax.axis_index("m")
    pair_count = integrals.shape[0]
    local_rows, local_cols = coefficients.shape
    block_len = beta_sign.shape[1] // pair_count
    per_device = local_rows // block_len
    src_blocks = local_cols // block_len
    total_blocks = lax.axis_size("g") * PAIR * src_blocks
    pairs = -(-pair_count // 16) * 16
    extra = pairs - pair_count
    sub_rows = block_len // PAIR

    alpha_size = lax.axis_size("alpha")
    gathered = spread(coefficients, alpha_size * PAIR).reshape(
        alpha_size, PAIR, local_rows, local_cols
    )
    gathered = gathered.transpose(0, 2, 1, 3).reshape(alpha_size * local_rows, PAIR * local_cols)
    live_flags = (block_irrep == 0).astype(jnp.int32)
    live_rows = jnp.repeat(live_flags, block_len)
    gathered = gathered * live_rows[:, None].astype(jnp.bfloat16)
    window_rows, wide_cols = gathered.shape
    coeff_ext = jnp.concatenate(
        [gathered, -gathered, jnp.zeros((16, wide_cols), jnp.bfloat16)], axis=0
    )
    zero_row = 2 * window_rows
    row_ext = jnp.where(
        alpha_sign == 0, zero_row, jnp.where(alpha_sign < 0, alpha_row + window_rows, alpha_row)
    )
    row_ext = jnp.pad(row_ext, ((0, extra), (0, 0)), constant_values=zero_row).T

    integ_pad = jnp.pad(integrals, ((0, extra), (0, extra)))
    beta_block2 = lax.all_gather(beta_block, "m", axis=0, tiled=True)
    beta_sign2 = lax.all_gather(beta_sign, "m", axis=0, tiled=True)
    sign_q = (
        beta_sign2.reshape(PAIR, src_blocks, pair_count, block_len)
        .transpose(0, 2, 1, 3)
        .reshape(PAIR, pair_count, local_cols)
    )
    sign_q = jnp.pad(sign_q, ((0, 0), (0, extra), (0, 0))).astype(jnp.bfloat16)
    target_iota = jnp.arange(total_blocks, dtype=jnp.int32)
    table_all = (target_iota[None, :, None] == beta_block2[:, None, :]).astype(jnp.bfloat16)
    table_all = jnp.pad(
        table_all.reshape(PAIR, src_blocks * total_blocks, pair_count),
        ((0, 0), (0, 0), (0, extra)),
    )

    own_flags = lax.dynamic_slice_in_dim(live_flags, alpha_rank * per_device, per_device, 0)

    dims = lax.GatherDimensionNumbers(
        offset_dims=(2,), collapsed_slice_dims=(0,), start_index_map=(0,)
    )

    parts = []
    for local_blk in range(per_device):
        first_row = (alpha_rank * per_device + local_blk) * block_len + member * sub_rows
        row_ids = lax.dynamic_slice_in_dim(row_ext, first_row, sub_rows, 0)
        picked = lax.gather(
            coeff_ext,
            row_ids[:, :, None],
            dims,
            slice_sizes=(1, wide_cols),
            mode=lax.GatherScatterMode.PROMISE_IN_BOUNDS,
        )
        summed = mix_block(integ_pad, picked, sign_q, table_all, total_blocks, block_len)
        parts.append(
            summed.reshape(sub_rows, total_blocks // src_blocks, local_cols).transpose(1, 0, 2)
        )
    send = jnp.stack(parts, axis=1)
    recv = exchange(send)
    groups = recv.shape[0] // PAIR
    recv = recv.reshape(groups, PAIR, per_device, sub_rows, local_cols).sum(axis=0)
    placed = recv.transpose(1, 0, 2, 3).reshape(local_rows, local_cols)
    own_live_rows = jnp.repeat(own_flags, block_len)
    total = diagonal * coefficients.astype(jnp.float32) + placed
    return jnp.where(own_live_rows[:, None] == 1, total, jnp.zeros_like(total))


def solution(mesh):
    alpha_size, beta_size = mesh.devices.shape
    split_mesh = Mesh(
        mesh.devices.reshape(alpha_size, beta_size // PAIR, PAIR), ("alpha", "g", "m")
    )
    beta = ("g", "m")
    return jax.shard_map(
        on_device,
        mesh=split_mesh,
        in_specs=(
            P("alpha", beta),
            P("alpha", beta),
            P(),
            P(),
            P(),
            P(beta, None),
            P(beta, None),
            P(),
        ),
        out_specs=P("alpha", beta),
        check_vma=False,
    )
```

```python
import jax
import jax.numpy as jnp
from jax import lax
from jax.experimental import pallas as pl
from jax.experimental.pallas import tpu as pltpu
from jax.sharding import Mesh
from jax.sharding import PartitionSpec as P

ROWS = 8
PAIR = 2


def mix_kernel(integ_ref, picked_ref, sign_ref, table_ref, out_ref):
    halves, _, width = sign_ref.shape
    targets = out_ref.shape[1]
    block_len = out_ref.shape[2]
    src_blocks = width // block_len
    lane = lax.broadcasted_iota(jnp.int32, (targets, 2 * block_len), 1)
    upper = lane >= block_len
    integ = integ_ref[...]
    for row in range(picked_ref.shape[0]):
        mixed = jnp.dot(integ, picked_ref[row], preferred_element_type=jnp.float32)
        folded = jnp.zeros((targets, 2 * block_len), jnp.float32)
        for half in range(halves):
            weighted = mixed[:, half * width : (half + 1) * width] * sign_ref[half].astype(
                jnp.float32
            )
            high = weighted.astype(jnp.bfloat16)
            low = (weighted - high.astype(jnp.float32)).astype(jnp.bfloat16)
            table = table_ref[half]
            res = jnp.dot(table, high, preferred_element_type=jnp.float32) + jnp.dot(
                table, low, preferred_element_type=jnp.float32
            )
            for s in range(src_blocks):
                lanes = (s // 2) * 2 * block_len
                piece = res[s * targets : (s + 1) * targets, lanes : lanes + 2 * block_len]
                keep = upper if s % 2 else jnp.logical_not(upper)
                folded = folded + jnp.where(keep, piece, 0.0)
        folded = folded + pltpu.roll(folded, block_len, 1)
        out_ref[row] = folded[:, :block_len]


def mix_block(integ_pad, picked, sign_q, table_all, targets, block_len):
    rows, pairs, width = picked.shape
    return pl.pallas_call(
        mix_kernel,
        out_shape=jax.ShapeDtypeStruct((rows, targets, block_len), jnp.float32),
        grid=(rows // ROWS,),
        in_specs=[
            pl.BlockSpec((pairs, pairs), lambda i: (0, 0)),
            pl.BlockSpec((ROWS, pairs, width), lambda i: (i, 0, 0)),
            pl.BlockSpec(sign_q.shape, lambda i: (0, 0, 0)),
            pl.BlockSpec(table_all.shape, lambda i: (0, 0, 0)),
        ],
        out_specs=pl.BlockSpec((ROWS, targets, block_len), lambda i: (i, 0, 0)),
        compiler_params=pltpu.CompilerParams(dimension_semantics=("arbitrary",)),
    )(integ_pad, picked, sign_q, table_all)


def exchange_kernel(send_ref, recv_ref, send_sem, recv_sem, local_sem):
    groups = lax.axis_size("g")
    count = groups * PAIR
    alpha = lax.axis_index("alpha")
    me = lax.axis_index("g") * PAIR + lax.axis_index("m")

    def remote(slot, peer):
        return pltpu.make_async_remote_copy(
            src_ref=send_ref.at[slot],
            dst_ref=recv_ref.at[slot],
            send_sem=send_sem.at[slot],
            recv_sem=recv_sem.at[slot],
            device_id=(alpha, peer // PAIR, peer % PAIR),
            device_id_type=pl.DeviceIdType.MESH,
        )

    for step in range(1, count):
        dest = lax.rem(me + step, count)
        pltpu.make_async_remote_copy(
            src_ref=send_ref.at[dest],
            dst_ref=recv_ref.at[me],
            send_sem=send_sem.at[dest],
            recv_sem=recv_sem.at[me],
            device_id=(alpha, dest // PAIR, dest % PAIR),
            device_id_type=pl.DeviceIdType.MESH,
        ).start()
    local = pltpu.make_async_copy(send_ref.at[me], recv_ref.at[me], local_sem)
    local.start()
    local.wait()
    for step in range(1, count):
        dest = lax.rem(me + step, count)
        remote(dest, dest).wait_send()
    for step in range(1, count):
        src = lax.rem(me + count - step, count)
        remote(src, src).wait_recv()


def exchange(send):
    count = send.shape[0]
    return pl.pallas_call(
        exchange_kernel,
        out_shape=jax.ShapeDtypeStruct(send.shape, send.dtype),
        in_specs=[pl.BlockSpec(memory_space=pl.ANY)],
        out_specs=pl.BlockSpec(memory_space=pl.ANY),
        scratch_shapes=[
            pltpu.SemaphoreType.DMA((count,)),
            pltpu.SemaphoreType.DMA((count,)),
            pltpu.SemaphoreType.DMA,
        ],
        compiler_params=pltpu.CompilerParams(has_side_effects=True),
    )(send)


def spread_kernel(own_ref, out_ref, send_sem, recv_sem, local_sem):
    count = lax.axis_size("alpha") * PAIR
    group = lax.axis_index("g")
    me = lax.axis_index("alpha") * PAIR + lax.axis_index("m")

    def remote(slot, sem_slot, peer):
        return pltpu.make_async_remote_copy(
            src_ref=own_ref,
            dst_ref=out_ref.at[slot],
            send_sem=send_sem.at[sem_slot],
            recv_sem=recv_sem.at[slot],
            device_id=(peer // PAIR, group, peer % PAIR),
            device_id_type=pl.DeviceIdType.MESH,
        )

    for step in range(1, count):
        dest = lax.rem(me + step, count)
        remote(me, dest, dest).start()
    local = pltpu.make_async_copy(own_ref, out_ref.at[me], local_sem)
    local.start()
    local.wait()
    for step in range(1, count):
        dest = lax.rem(me + step, count)
        remote(me, dest, dest).wait_send()
    for step in range(1, count):
        src = lax.rem(me + count - step, count)
        remote(src, src, src).wait_recv()


def spread(own, count):
    return pl.pallas_call(
        spread_kernel,
        out_shape=jax.ShapeDtypeStruct((count,) + own.shape, own.dtype),
        in_specs=[pl.BlockSpec(memory_space=pl.ANY)],
        out_specs=pl.BlockSpec(memory_space=pl.ANY),
        scratch_shapes=[
            pltpu.SemaphoreType.DMA((count,)),
            pltpu.SemaphoreType.DMA((count,)),
            pltpu.SemaphoreType.DMA,
        ],
        compiler_params=pltpu.CompilerParams(has_side_effects=True),
    )(own)


def gather_alpha_kernel(own_ref, out_ref, send_sem, recv_sem, local_sem):
    count = lax.axis_size("alpha")
    group = lax.axis_index("g")
    member = lax.axis_index("m")
    me = lax.axis_index("alpha")

    def remote(slot, sem_slot, peer):
        return pltpu.make_async_remote_copy(
            src_ref=own_ref,
            dst_ref=out_ref.at[slot],
            send_sem=send_sem.at[sem_slot],
            recv_sem=recv_sem.at[slot],
            device_id=(peer, group, member),
            device_id_type=pl.DeviceIdType.MESH,
        )

    for step in range(1, count):
        dest = lax.rem(me + step, count)
        remote(me, dest, dest).start()
    local = pltpu.make_async_copy(own_ref, out_ref.at[me], local_sem)
    local.start()
    local.wait()
    for step in range(1, count):
        dest = lax.rem(me + step, count)
        remote(me, dest, dest).wait_send()
    for step in range(1, count):
        src = lax.rem(me + count - step, count)
        remote(src, src, src).wait_recv()


def gather_alpha(own, count):
    return pl.pallas_call(
        gather_alpha_kernel,
        out_shape=jax.ShapeDtypeStruct((count,) + own.shape, own.dtype),
        in_specs=[pl.BlockSpec(memory_space=pl.ANY)],
        out_specs=pl.BlockSpec(memory_space=pl.ANY),
        scratch_shapes=[
            pltpu.SemaphoreType.DMA((count,)),
            pltpu.SemaphoreType.DMA((count,)),
            pltpu.SemaphoreType.DMA,
        ],
        compiler_params=pltpu.CompilerParams(has_side_effects=True),
    )(own)


def on_device(
    coefficients, diagonal, integrals, alpha_row, alpha_sign, beta_block, beta_sign, block_irrep
):
    alpha_rank = lax.axis_index("alpha")
    member = lax.axis_index("m")
    pair_count = integrals.shape[0]
    local_rows, local_cols = coefficients.shape
    block_len = beta_sign.shape[1] // pair_count
    per_device = local_rows // block_len
    src_blocks = local_cols // block_len
    total_blocks = lax.axis_size("g") * PAIR * src_blocks
    pairs = -(-pair_count // 16) * 16
    extra = pairs - pair_count
    sub_rows = block_len // PAIR

    alpha_size = lax.axis_size("alpha")
    gathered = spread(coefficients, alpha_size * PAIR).reshape(
        alpha_size, PAIR, local_rows, local_cols
    )
    gathered = gathered.transpose(0, 2, 1, 3).reshape(alpha_size * local_rows, PAIR * local_cols)
    live_flags = (block_irrep == 0).astype(jnp.int32)
    live_rows = jnp.repeat(live_flags, block_len)
    gathered = gathered * live_rows[:, None].astype(jnp.bfloat16)
    window_rows, wide_cols = gathered.shape
    coeff_ext = jnp.concatenate(
        [gathered, -gathered, jnp.zeros((16, wide_cols), jnp.bfloat16)], axis=0
    )
    zero_row = 2 * window_rows
    row_ext = jnp.where(
        alpha_sign == 0, zero_row, jnp.where(alpha_sign < 0, alpha_row + window_rows, alpha_row)
    )
    row_ext = jnp.pad(row_ext, ((0, extra), (0, 0)), constant_values=zero_row).T

    integ_pad = jnp.pad(integrals, ((0, extra), (0, extra)))
    beta_block2 = lax.all_gather(beta_block, "m", axis=0, tiled=True)
    beta_sign2 = lax.all_gather(beta_sign, "m", axis=0, tiled=True)
    sign_q = (
        beta_sign2.reshape(PAIR, src_blocks, pair_count, block_len)
        .transpose(0, 2, 1, 3)
        .reshape(PAIR, pair_count, local_cols)
    )
    sign_q = jnp.pad(sign_q, ((0, 0), (0, extra), (0, 0))).astype(jnp.bfloat16)
    target_iota = jnp.arange(total_blocks, dtype=jnp.int32)
    table_all = (target_iota[None, :, None] == beta_block2[:, None, :]).astype(jnp.bfloat16)
    table_all = jnp.pad(
        table_all.reshape(PAIR, src_blocks * total_blocks, pair_count),
        ((0, 0), (0, 0), (0, extra)),
    )

    own_flags = lax.dynamic_slice_in_dim(live_flags, alpha_rank * per_device, per_device, 0)

    dims = lax.GatherDimensionNumbers(
        offset_dims=(2,), collapsed_slice_dims=(0,), start_index_map=(0,)
    )

    block_count = live_flags.shape[0]
    block_iota = jnp.arange(block_count, dtype=jnp.int32)
    live_rank = jnp.cumsum(live_flags) - live_flags
    live_total = jnp.sum(live_flags)
    block_of_rank = jnp.sum(
        jnp.where(
            (live_flags[None, :] == 1) & (live_rank[None, :] == block_iota[:, None]),
            block_iota[None, :],
            0,
        ),
        axis=1,
    )
    my_count = jnp.maximum(live_total - alpha_rank + alpha_size - 1, 0) // alpha_size
    beta_size = total_blocks // src_blocks

    def one_block(slot, buffer):
        block_id = block_of_rank[slot * alpha_size + alpha_rank]
        first_row = block_id * block_len + member * sub_rows
        row_ids = lax.dynamic_slice_in_dim(row_ext, first_row, sub_rows, 0)
        picked = lax.gather(
            coeff_ext,
            row_ids[:, :, None],
            dims,
            slice_sizes=(1, wide_cols),
            mode=lax.GatherScatterMode.PROMISE_IN_BOUNDS,
        )
        summed = mix_block(integ_pad, picked, sign_q, table_all, total_blocks, block_len)
        part = summed.reshape(sub_rows, beta_size, local_cols).transpose(1, 0, 2)
        return lax.dynamic_update_slice(buffer, part[:, None], (0, slot, 0, 0))

    empty = jnp.zeros((beta_size, per_device, sub_rows, local_cols), jnp.float32)
    send = lax.fori_loop(0, my_count, one_block, empty)
    recv = exchange(send)
    groups = recv.shape[0] // PAIR
    recv = recv.reshape(groups, PAIR, per_device, sub_rows, local_cols).sum(axis=0)
    done = recv.transpose(1, 0, 2, 3).reshape(per_device, block_len, local_cols)
    everyone = gather_alpha(done, alpha_size).reshape(
        alpha_size * per_device, block_len, local_cols
    )
    own_rank = lax.dynamic_slice_in_dim(live_rank, alpha_rank * per_device, per_device, 0)
    pick = (own_rank % alpha_size) * per_device + jnp.minimum(own_rank // alpha_size, per_device - 1)
    placed = everyone[pick].reshape(local_rows, local_cols)
    own_live_rows = jnp.repeat(own_flags, block_len)
    total = diagonal * coefficients.astype(jnp.float32) + placed
    return jnp.where(own_live_rows[:, None] == 1, total, jnp.zeros_like(total))


def solution(mesh):
    alpha_size, beta_size = mesh.devices.shape
    split_mesh = Mesh(
        mesh.devices.reshape(alpha_size, beta_size // PAIR, PAIR), ("alpha", "g", "m")
    )
    beta = ("g", "m")
    return jax.shard_map(
        on_device,
        mesh=split_mesh,
        in_specs=(
            P("alpha", beta),
            P("alpha", beta),
            P(),
            P(),
            P(),
            P(beta, None),
            P(beta, None),
            P(),
        ),
        out_specs=P("alpha", beta),
        check_vma=False,
    )
```

```python
import jax
import jax.numpy as jnp
from jax import lax
from jax.experimental import pallas as pl
from jax.experimental.pallas import tpu as pltpu
from jax.sharding import Mesh
from jax.sharding import PartitionSpec as P

ROWS = 8
PAIR = 2


def mix_kernel(integ_ref, picked_ref, sign_ref, table_ref, out_ref):
    halves, _, width = sign_ref.shape
    targets = out_ref.shape[1]
    block_len = out_ref.shape[2]
    src_blocks = width // block_len
    lane = lax.broadcasted_iota(jnp.int32, (targets, 2 * block_len), 1)
    upper = lane >= block_len
    integ = integ_ref[...]
    for row in range(picked_ref.shape[0]):
        mixed = jnp.dot(integ, picked_ref[row], preferred_element_type=jnp.float32)
        folded = jnp.zeros((targets, 2 * block_len), jnp.float32)
        for half in range(halves):
            weighted = mixed[:, half * width : (half + 1) * width] * sign_ref[half].astype(
                jnp.float32
            )
            high = weighted.astype(jnp.bfloat16)
            low = (weighted - high.astype(jnp.float32)).astype(jnp.bfloat16)
            table = table_ref[half]
            res = jnp.dot(table, high, preferred_element_type=jnp.float32) + jnp.dot(
                table, low, preferred_element_type=jnp.float32
            )
            for s in range(src_blocks):
                lanes = (s // 2) * 2 * block_len
                piece = res[s * targets : (s + 1) * targets, lanes : lanes + 2 * block_len]
                keep = upper if s % 2 else jnp.logical_not(upper)
                folded = folded + jnp.where(keep, piece, 0.0)
        folded = folded + pltpu.roll(folded, block_len, 1)
        out_ref[row] = folded[:, :block_len]


def mix_block(integ_pad, picked, sign_q, table_all, targets, block_len):
    rows, pairs, width = picked.shape
    return pl.pallas_call(
        mix_kernel,
        out_shape=jax.ShapeDtypeStruct((rows, targets, block_len), jnp.float32),
        grid=(rows // ROWS,),
        in_specs=[
            pl.BlockSpec((pairs, pairs), lambda i: (0, 0)),
            pl.BlockSpec((ROWS, pairs, width), lambda i: (i, 0, 0)),
            pl.BlockSpec(sign_q.shape, lambda i: (0, 0, 0)),
            pl.BlockSpec(table_all.shape, lambda i: (0, 0, 0)),
        ],
        out_specs=pl.BlockSpec((ROWS, targets, block_len), lambda i: (i, 0, 0)),
        compiler_params=pltpu.CompilerParams(dimension_semantics=("arbitrary",)),
    )(integ_pad, picked, sign_q, table_all)


def exchange_kernel(send_ref, recv_ref, send_sem, recv_sem, local_sem):
    groups = lax.axis_size("g")
    count = groups * PAIR
    alpha = lax.axis_index("alpha")
    me = lax.axis_index("g") * PAIR + lax.axis_index("m")

    def remote(slot, peer):
        return pltpu.make_async_remote_copy(
            src_ref=send_ref.at[slot],
            dst_ref=recv_ref.at[slot],
            send_sem=send_sem.at[slot],
            recv_sem=recv_sem.at[slot],
            device_id=(alpha, peer // PAIR, peer % PAIR),
            device_id_type=pl.DeviceIdType.MESH,
        )

    for step in range(1, count):
        dest = lax.rem(me + step, count)
        pltpu.make_async_remote_copy(
            src_ref=send_ref.at[dest],
            dst_ref=recv_ref.at[me],
            send_sem=send_sem.at[dest],
            recv_sem=recv_sem.at[me],
            device_id=(alpha, dest // PAIR, dest % PAIR),
            device_id_type=pl.DeviceIdType.MESH,
        ).start()
    local = pltpu.make_async_copy(send_ref.at[me], recv_ref.at[me], local_sem)
    local.start()
    local.wait()
    for step in range(1, count):
        dest = lax.rem(me + step, count)
        remote(dest, dest).wait_send()
    for step in range(1, count):
        src = lax.rem(me + count - step, count)
        remote(src, src).wait_recv()


def exchange(send):
    count = send.shape[0]
    return pl.pallas_call(
        exchange_kernel,
        out_shape=jax.ShapeDtypeStruct(send.shape, send.dtype),
        in_specs=[pl.BlockSpec(memory_space=pl.ANY)],
        out_specs=pl.BlockSpec(memory_space=pl.ANY),
        scratch_shapes=[
            pltpu.SemaphoreType.DMA((count,)),
            pltpu.SemaphoreType.DMA((count,)),
            pltpu.SemaphoreType.DMA,
        ],
        compiler_params=pltpu.CompilerParams(has_side_effects=True),
    )(send)


def spread_kernel(own_ref, out_ref, send_sem, recv_sem, local_sem):
    count = lax.axis_size("alpha") * PAIR
    group = lax.axis_index("g")
    me = lax.axis_index("alpha") * PAIR + lax.axis_index("m")

    def remote(slot, sem_slot, peer):
        return pltpu.make_async_remote_copy(
            src_ref=own_ref,
            dst_ref=out_ref.at[slot],
            send_sem=send_sem.at[sem_slot],
            recv_sem=recv_sem.at[slot],
            device_id=(peer // PAIR, group, peer % PAIR),
            device_id_type=pl.DeviceIdType.MESH,
        )

    for step in range(1, count):
        dest = lax.rem(me + step, count)
        remote(me, dest, dest).start()
    local = pltpu.make_async_copy(own_ref, out_ref.at[me], local_sem)
    local.start()
    local.wait()
    for step in range(1, count):
        dest = lax.rem(me + step, count)
        remote(me, dest, dest).wait_send()
    for step in range(1, count):
        src = lax.rem(me + count - step, count)
        remote(src, src, src).wait_recv()


def spread(own, count):
    return pl.pallas_call(
        spread_kernel,
        out_shape=jax.ShapeDtypeStruct((count,) + own.shape, own.dtype),
        in_specs=[pl.BlockSpec(memory_space=pl.ANY)],
        out_specs=pl.BlockSpec(memory_space=pl.ANY),
        scratch_shapes=[
            pltpu.SemaphoreType.DMA((count,)),
            pltpu.SemaphoreType.DMA((count,)),
            pltpu.SemaphoreType.DMA,
        ],
        compiler_params=pltpu.CompilerParams(has_side_effects=True),
    )(own)


def gather_alpha_kernel(own_ref, out_ref, send_sem, recv_sem, local_sem):
    count = lax.axis_size("alpha")
    group = lax.axis_index("g")
    member = lax.axis_index("m")
    me = lax.axis_index("alpha")

    def remote(slot, sem_slot, peer):
        return pltpu.make_async_remote_copy(
            src_ref=own_ref,
            dst_ref=out_ref.at[slot],
            send_sem=send_sem.at[sem_slot],
            recv_sem=recv_sem.at[slot],
            device_id=(peer, group, member),
            device_id_type=pl.DeviceIdType.MESH,
        )

    for step in range(1, count):
        dest = lax.rem(me + step, count)
        remote(me, dest, dest).start()
    local = pltpu.make_async_copy(own_ref, out_ref.at[me], local_sem)
    local.start()
    local.wait()
    for step in range(1, count):
        dest = lax.rem(me + step, count)
        remote(me, dest, dest).wait_send()
    for step in range(1, count):
        src = lax.rem(me + count - step, count)
        remote(src, src, src).wait_recv()


def gather_alpha(own, count):
    return pl.pallas_call(
        gather_alpha_kernel,
        out_shape=jax.ShapeDtypeStruct((count,) + own.shape, own.dtype),
        in_specs=[pl.BlockSpec(memory_space=pl.ANY)],
        out_specs=pl.BlockSpec(memory_space=pl.ANY),
        scratch_shapes=[
            pltpu.SemaphoreType.DMA((count,)),
            pltpu.SemaphoreType.DMA((count,)),
            pltpu.SemaphoreType.DMA,
        ],
        compiler_params=pltpu.CompilerParams(has_side_effects=True),
    )(own)


def on_device(
    coefficients, diagonal, integrals, alpha_row, alpha_sign, beta_block, beta_sign, block_irrep
):
    alpha_rank = lax.axis_index("alpha")
    member = lax.axis_index("m")
    pair_count = integrals.shape[0]
    local_rows, local_cols = coefficients.shape
    block_len = beta_sign.shape[1] // pair_count
    per_device = local_rows // block_len
    src_blocks = local_cols // block_len
    total_blocks = lax.axis_size("g") * PAIR * src_blocks
    pairs = -(-pair_count // 16) * 16
    extra = pairs - pair_count
    sub_rows = block_len // PAIR

    alpha_size = lax.axis_size("alpha")
    gathered = spread(coefficients, alpha_size * PAIR).reshape(
        alpha_size, PAIR, local_rows, local_cols
    )
    gathered = gathered.transpose(0, 2, 1, 3).reshape(alpha_size * local_rows, PAIR * local_cols)
    live_flags = (block_irrep == 0).astype(jnp.int32)
    live_rows = jnp.repeat(live_flags, block_len)
    gathered = gathered * live_rows[:, None].astype(jnp.bfloat16)
    window_rows, wide_cols = gathered.shape
    coeff_ext = jnp.concatenate(
        [gathered, -gathered, jnp.zeros((16, wide_cols), jnp.bfloat16)], axis=0
    )
    zero_row = 2 * window_rows
    row_ext = jnp.where(
        alpha_sign == 0, zero_row, jnp.where(alpha_sign < 0, alpha_row + window_rows, alpha_row)
    )
    row_ext = jnp.pad(row_ext, ((0, extra), (0, 0)), constant_values=zero_row)

    integ_pad = jnp.pad(integrals, ((0, extra), (0, extra)))
    beta_block2 = lax.all_gather(beta_block, "m", axis=0, tiled=True)
    beta_sign2 = lax.all_gather(beta_sign, "m", axis=0, tiled=True)
    sign_q = (
        beta_sign2.reshape(PAIR, src_blocks, pair_count, block_len)
        .transpose(0, 2, 1, 3)
        .reshape(PAIR, pair_count, local_cols)
    )
    sign_q = jnp.pad(sign_q, ((0, 0), (0, extra), (0, 0))).astype(jnp.bfloat16)
    target_iota = jnp.arange(total_blocks, dtype=jnp.int32)
    table_all = (target_iota[None, :, None] == beta_block2[:, None, :]).astype(jnp.bfloat16)
    table_all = jnp.pad(
        table_all.reshape(PAIR, src_blocks * total_blocks, pair_count),
        ((0, 0), (0, 0), (0, extra)),
    )

    own_flags = lax.dynamic_slice_in_dim(live_flags, alpha_rank * per_device, per_device, 0)

    dims = lax.GatherDimensionNumbers(
        offset_dims=(2,), collapsed_slice_dims=(0,), start_index_map=(0,)
    )

    block_count = live_flags.shape[0]
    block_iota = jnp.arange(block_count, dtype=jnp.int32)
    in_group = jnp.cumsum(live_flags.reshape(-1, per_device), axis=1).reshape(-1)
    is_first = (live_flags == 1) & (in_group == 1)
    is_extra = ((live_flags == 1) & jnp.logical_not(is_first)).astype(jnp.int32)
    extra_rank = jnp.cumsum(is_extra) - is_extra
    extra_total = jnp.sum(is_extra)
    block_of_extra = jnp.sum(
        jnp.where(
            (is_extra[None, :] == 1) & (extra_rank[None, :] == block_iota[:, None]),
            block_iota[None, :],
            0,
        ),
        axis=1,
    )
    own_first = lax.dynamic_slice_in_dim(is_first, alpha_rank * per_device, per_device, 0)
    first_blk = alpha_rank * per_device + jnp.argmax(own_first).astype(jnp.int32)
    my_count = 1 + jnp.maximum(extra_total - alpha_rank + alpha_size - 1, 0) // alpha_size
    beta_size = total_blocks // src_blocks

    def one_block(slot, buffer):
        block_id = jnp.where(
            slot == 0,
            first_blk,
            block_of_extra[jnp.maximum(slot - 1, 0) * alpha_size + alpha_rank],
        )
        first_row = block_id * block_len + member * sub_rows
        row_ids = lax.dynamic_slice_in_dim(row_ext, first_row, sub_rows, 1).T
        picked = lax.gather(
            coeff_ext,
            row_ids[:, :, None],
            dims,
            slice_sizes=(1, wide_cols),
            mode=lax.GatherScatterMode.PROMISE_IN_BOUNDS,
        )
        summed = mix_block(integ_pad, picked, sign_q, table_all, total_blocks, block_len)
        part = summed.reshape(sub_rows, beta_size, local_cols).transpose(1, 0, 2)
        return lax.dynamic_update_slice(buffer, part[:, None], (0, slot, 0, 0))

    empty = jnp.zeros((beta_size, per_device, sub_rows, local_cols), jnp.float32)
    send = lax.fori_loop(0, my_count, one_block, empty)
    recv = exchange(send)
    groups = recv.shape[0] // PAIR
    recv = recv.reshape(groups, PAIR, per_device, sub_rows, local_cols).sum(axis=0)
    done = recv.transpose(1, 0, 2, 3).reshape(per_device, block_len, local_cols)
    everyone = gather_alpha(done[1:], alpha_size).reshape(
        alpha_size * (per_device - 1), block_len, local_cols
    )
    own_rank = lax.dynamic_slice_in_dim(extra_rank, alpha_rank * per_device, per_device, 0)
    pick = (own_rank % alpha_size) * (per_device - 1) + jnp.minimum(
        own_rank // alpha_size, per_device - 2
    )
    placed = jnp.where(own_first[:, None, None], done[0][None], everyone[pick])
    placed = placed.reshape(local_rows, local_cols)
    own_live_rows = jnp.repeat(own_flags, block_len)
    total = diagonal * coefficients.astype(jnp.float32) + placed
    return jnp.where(own_live_rows[:, None] == 1, total, jnp.zeros_like(total))


def solution(mesh):
    alpha_size, beta_size = mesh.devices.shape
    split_mesh = Mesh(
        mesh.devices.reshape(alpha_size, beta_size // PAIR, PAIR), ("alpha", "g", "m")
    )
    beta = ("g", "m")
    return jax.shard_map(
        on_device,
        mesh=split_mesh,
        in_specs=(
            P("alpha", beta),
            P("alpha", beta),
            P(),
            P(),
            P(),
            P(beta, None),
            P(beta, None),
            P(),
        ),
        out_specs=P("alpha", beta),
        check_vma=False,
    )
```

```python
import jax
import jax.numpy as jnp
from jax import lax
from jax.experimental import pallas as pl
from jax.experimental.pallas import tpu as pltpu
from jax.sharding import Mesh
from jax.sharding import PartitionSpec as P

ROWS = 8
PAIR = 2


def mix_kernel(integ_ref, picked_ref, sign_ref, table_ref, out_ref):
    halves, _, width = sign_ref.shape
    targets = out_ref.shape[1]
    block_len = out_ref.shape[2]
    src_blocks = width // block_len
    lane = lax.broadcasted_iota(jnp.int32, (targets, 2 * block_len), 1)
    upper = lane >= block_len
    integ = integ_ref[...]
    for row in range(picked_ref.shape[0]):
        mixed = jnp.dot(integ, picked_ref[row], preferred_element_type=jnp.float32)
        folded = jnp.zeros((targets, 2 * block_len), jnp.float32)
        for half in range(halves):
            weighted = mixed[:, half * width : (half + 1) * width] * sign_ref[half].astype(
                jnp.float32
            )
            high = weighted.astype(jnp.bfloat16)
            low = (weighted - high.astype(jnp.float32)).astype(jnp.bfloat16)
            table = table_ref[half]
            res = jnp.dot(table, high, preferred_element_type=jnp.float32) + jnp.dot(
                table, low, preferred_element_type=jnp.float32
            )
            for s in range(src_blocks):
                lanes = (s // 2) * 2 * block_len
                piece = res[s * targets : (s + 1) * targets, lanes : lanes + 2 * block_len]
                keep = upper if s % 2 else jnp.logical_not(upper)
                folded = folded + jnp.where(keep, piece, 0.0)
        folded = folded + pltpu.roll(folded, block_len, 1)
        out_ref[row] = folded[:, :block_len]


def mix_block(integ_pad, picked, sign_q, table_all, targets, block_len):
    rows, pairs, width = picked.shape
    return pl.pallas_call(
        mix_kernel,
        out_shape=jax.ShapeDtypeStruct((rows, targets, block_len), jnp.float32),
        grid=(rows // ROWS,),
        in_specs=[
            pl.BlockSpec((pairs, pairs), lambda i: (0, 0)),
            pl.BlockSpec((ROWS, pairs, width), lambda i: (i, 0, 0)),
            pl.BlockSpec(sign_q.shape, lambda i: (0, 0, 0)),
            pl.BlockSpec(table_all.shape, lambda i: (0, 0, 0)),
        ],
        out_specs=pl.BlockSpec((ROWS, targets, block_len), lambda i: (i, 0, 0)),
        compiler_params=pltpu.CompilerParams(dimension_semantics=("arbitrary",)),
    )(integ_pad, picked, sign_q, table_all)


def exchange_kernel(send_ref, recv_ref, send_sem, recv_sem, local_sem):
    groups = lax.axis_size("g")
    count = groups * PAIR
    alpha = lax.axis_index("alpha")
    me = lax.axis_index("g") * PAIR + lax.axis_index("m")

    def remote(slot, peer):
        return pltpu.make_async_remote_copy(
            src_ref=send_ref.at[slot],
            dst_ref=recv_ref.at[slot],
            send_sem=send_sem.at[slot],
            recv_sem=recv_sem.at[slot],
            device_id=(alpha, peer // PAIR, peer % PAIR),
            device_id_type=pl.DeviceIdType.MESH,
        )

    for step in range(1, count):
        dest = lax.rem(me + step, count)
        pltpu.make_async_remote_copy(
            src_ref=send_ref.at[dest],
            dst_ref=recv_ref.at[me],
            send_sem=send_sem.at[dest],
            recv_sem=recv_sem.at[me],
            device_id=(alpha, dest // PAIR, dest % PAIR),
            device_id_type=pl.DeviceIdType.MESH,
        ).start()
    local = pltpu.make_async_copy(send_ref.at[me], recv_ref.at[me], local_sem)
    local.start()
    local.wait()
    for step in range(1, count):
        dest = lax.rem(me + step, count)
        remote(dest, dest).wait_send()
    for step in range(1, count):
        src = lax.rem(me + count - step, count)
        remote(src, src).wait_recv()


def exchange(send):
    count = send.shape[0]
    return pl.pallas_call(
        exchange_kernel,
        out_shape=jax.ShapeDtypeStruct(send.shape, send.dtype),
        in_specs=[pl.BlockSpec(memory_space=pl.ANY)],
        out_specs=pl.BlockSpec(memory_space=pl.ANY),
        scratch_shapes=[
            pltpu.SemaphoreType.DMA((count,)),
            pltpu.SemaphoreType.DMA((count,)),
            pltpu.SemaphoreType.DMA,
        ],
        compiler_params=pltpu.CompilerParams(has_side_effects=True),
    )(send)


def spread_kernel(own_ref, out_ref, send_sem, recv_sem, local_sem):
    count = lax.axis_size("alpha") * PAIR
    rows, cols = own_ref.shape
    group = lax.axis_index("g")
    me = lax.axis_index("alpha") * PAIR + lax.axis_index("m")

    def window(slot):
        return out_ref.at[pl.ds((slot // PAIR) * rows, rows), pl.ds((slot % PAIR) * cols, cols)]

    def remote(slot, sem_slot, peer):
        return pltpu.make_async_remote_copy(
            src_ref=own_ref,
            dst_ref=window(slot),
            send_sem=send_sem.at[sem_slot],
            recv_sem=recv_sem.at[slot],
            device_id=(peer // PAIR, group, peer % PAIR),
            device_id_type=pl.DeviceIdType.MESH,
        )

    for step in range(1, count):
        dest = lax.rem(me + step, count)
        remote(me, dest, dest).start()
    local = pltpu.make_async_copy(own_ref, window(me), local_sem)
    local.start()
    local.wait()
    for step in range(1, count):
        dest = lax.rem(me + step, count)
        remote(me, dest, dest).wait_send()
    for step in range(1, count):
        src = lax.rem(me + count - step, count)
        remote(src, src, src).wait_recv()


def spread(own, count):
    return pl.pallas_call(
        spread_kernel,
        out_shape=jax.ShapeDtypeStruct(
            (count // PAIR * own.shape[0], PAIR * own.shape[1]), own.dtype
        ),
        in_specs=[pl.BlockSpec(memory_space=pl.ANY)],
        out_specs=pl.BlockSpec(memory_space=pl.ANY),
        scratch_shapes=[
            pltpu.SemaphoreType.DMA((count,)),
            pltpu.SemaphoreType.DMA((count,)),
            pltpu.SemaphoreType.DMA,
        ],
        compiler_params=pltpu.CompilerParams(has_side_effects=True),
    )(own)


def gather_alpha_kernel(own_ref, out_ref, send_sem, recv_sem, local_sem):
    count = lax.axis_size("alpha")
    group = lax.axis_index("g")
    member = lax.axis_index("m")
    me = lax.axis_index("alpha")

    def remote(slot, sem_slot, peer):
        return pltpu.make_async_remote_copy(
            src_ref=own_ref,
            dst_ref=out_ref.at[slot],
            send_sem=send_sem.at[sem_slot],
            recv_sem=recv_sem.at[slot],
            device_id=(peer, group, member),
            device_id_type=pl.DeviceIdType.MESH,
        )

    for step in range(1, count):
        dest = lax.rem(me + step, count)
        remote(me, dest, dest).start()
    local = pltpu.make_async_copy(own_ref, out_ref.at[me], local_sem)
    local.start()
    local.wait()
    for step in range(1, count):
        dest = lax.rem(me + step, count)
        remote(me, dest, dest).wait_send()
    for step in range(1, count):
        src = lax.rem(me + count - step, count)
        remote(src, src, src).wait_recv()


def gather_alpha(own, count):
    return pl.pallas_call(
        gather_alpha_kernel,
        out_shape=jax.ShapeDtypeStruct((count,) + own.shape, own.dtype),
        in_specs=[pl.BlockSpec(memory_space=pl.ANY)],
        out_specs=pl.BlockSpec(memory_space=pl.ANY),
        scratch_shapes=[
            pltpu.SemaphoreType.DMA((count,)),
            pltpu.SemaphoreType.DMA((count,)),
            pltpu.SemaphoreType.DMA,
        ],
        compiler_params=pltpu.CompilerParams(has_side_effects=True),
    )(own)


def on_device(
    coefficients, diagonal, integrals, alpha_row, alpha_sign, beta_block, beta_sign, block_irrep
):
    alpha_rank = lax.axis_index("alpha")
    member = lax.axis_index("m")
    pair_count = integrals.shape[0]
    local_rows, local_cols = coefficients.shape
    block_len = beta_sign.shape[1] // pair_count
    per_device = local_rows // block_len
    src_blocks = local_cols // block_len
    total_blocks = lax.axis_size("g") * PAIR * src_blocks
    pairs = -(-pair_count // 16) * 16
    extra = pairs - pair_count
    sub_rows = block_len // PAIR

    alpha_size = lax.axis_size("alpha")
    gathered = spread(coefficients, alpha_size * PAIR)
    live_flags = (block_irrep == 0).astype(jnp.int32)
    live_rows = jnp.repeat(live_flags, block_len)
    gathered = gathered * live_rows[:, None].astype(jnp.bfloat16)
    window_rows, wide_cols = gathered.shape
    coeff_ext = jnp.concatenate(
        [gathered, -gathered, jnp.zeros((16, wide_cols), jnp.bfloat16)], axis=0
    )
    zero_row = 2 * window_rows

    integ_pad = jnp.pad(integrals, ((0, extra), (0, extra)))
    beta_block2 = lax.all_gather(beta_block.astype(jnp.bfloat16), "m", axis=0, tiled=True)
    beta_block2 = beta_block2.astype(jnp.int32)
    beta_sign2 = lax.all_gather(beta_sign.astype(jnp.bfloat16), "m", axis=0, tiled=True)
    sign_q = (
        beta_sign2.reshape(PAIR, src_blocks, pair_count, block_len)
        .transpose(0, 2, 1, 3)
        .reshape(PAIR, pair_count, local_cols)
    )
    sign_q = jnp.pad(sign_q, ((0, 0), (0, extra), (0, 0))).astype(jnp.bfloat16)
    target_iota = jnp.arange(total_blocks, dtype=jnp.int32)
    table_all = (target_iota[None, :, None] == beta_block2[:, None, :]).astype(jnp.bfloat16)
    table_all = jnp.pad(
        table_all.reshape(PAIR, src_blocks * total_blocks, pair_count),
        ((0, 0), (0, 0), (0, extra)),
    )

    own_flags = lax.dynamic_slice_in_dim(live_flags, alpha_rank * per_device, per_device, 0)

    dims = lax.GatherDimensionNumbers(
        offset_dims=(2,), collapsed_slice_dims=(0,), start_index_map=(0,)
    )

    block_count = live_flags.shape[0]
    block_iota = jnp.arange(block_count, dtype=jnp.int32)
    in_group = jnp.cumsum(live_flags.reshape(-1, per_device), axis=1).reshape(-1)
    is_first = (live_flags == 1) & (in_group == 1)
    is_extra = ((live_flags == 1) & jnp.logical_not(is_first)).astype(jnp.int32)
    extra_rank = jnp.cumsum(is_extra) - is_extra
    extra_total = jnp.sum(is_extra)
    block_of_extra = jnp.sum(
        jnp.where(
            (is_extra[None, :] == 1) & (extra_rank[None, :] == block_iota[:, None]),
            block_iota[None, :],
            0,
        ),
        axis=1,
    )
    own_first = lax.dynamic_slice_in_dim(is_first, alpha_rank * per_device, per_device, 0)
    first_blk = alpha_rank * per_device + jnp.argmax(own_first).astype(jnp.int32)
    my_count = 1 + jnp.maximum(extra_total - alpha_rank + alpha_size - 1, 0) // alpha_size
    beta_size = total_blocks // src_blocks

    def one_block(slot, buffer):
        block_id = jnp.where(
            slot == 0,
            first_blk,
            block_of_extra[jnp.maximum(slot - 1, 0) * alpha_size + alpha_rank],
        )
        first_row = block_id * block_len + member * sub_rows
        rows_src = lax.dynamic_slice_in_dim(alpha_row, first_row, sub_rows, 1)
        signs_src = lax.dynamic_slice_in_dim(alpha_sign, first_row, sub_rows, 1)
        row_ids = jnp.where(
            signs_src == 0,
            zero_row,
            jnp.where(signs_src < 0, rows_src + window_rows, rows_src),
        )
        row_ids = jnp.pad(row_ids, ((0, extra), (0, 0)), constant_values=zero_row).T
        picked = lax.gather(
            coeff_ext,
            row_ids[:, :, None],
            dims,
            slice_sizes=(1, wide_cols),
            mode=lax.GatherScatterMode.PROMISE_IN_BOUNDS,
        )
        summed = mix_block(integ_pad, picked, sign_q, table_all, total_blocks, block_len)
        part = summed.reshape(sub_rows, beta_size, local_cols).transpose(1, 0, 2)
        return lax.dynamic_update_slice(buffer, part[:, None], (0, slot, 0, 0))

    empty = jnp.zeros((beta_size, per_device, sub_rows, local_cols), jnp.float32)
    send = lax.fori_loop(0, my_count, one_block, empty)
    recv = exchange(send)
    groups = recv.shape[0] // PAIR
    recv = recv.reshape(groups, PAIR, per_device, sub_rows, local_cols).sum(axis=0)
    done = recv.transpose(1, 0, 2, 3).reshape(per_device, block_len, local_cols)
    everyone = gather_alpha(done[1:], alpha_size).reshape(
        alpha_size * (per_device - 1), block_len, local_cols
    )
    own_rank = lax.dynamic_slice_in_dim(extra_rank, alpha_rank * per_device, per_device, 0)
    pick = (own_rank % alpha_size) * (per_device - 1) + jnp.minimum(
        own_rank // alpha_size, per_device - 2
    )
    placed = jnp.where(own_first[:, None, None], done[0][None], everyone[pick])
    placed = placed.reshape(local_rows, local_cols)
    own_live_rows = jnp.repeat(own_flags, block_len)
    total = diagonal * coefficients.astype(jnp.float32) + placed
    return jnp.where(own_live_rows[:, None] == 1, total, jnp.zeros_like(total))


def solution(mesh):
    alpha_size, beta_size = mesh.devices.shape
    split_mesh = Mesh(
        mesh.devices.reshape(alpha_size, beta_size // PAIR, PAIR), ("alpha", "g", "m")
    )
    beta = ("g", "m")
    return jax.shard_map(
        on_device,
        mesh=split_mesh,
        in_specs=(
            P("alpha", beta),
            P("alpha", beta),
            P(),
            P(),
            P(),
            P(beta, None),
            P(beta, None),
            P(),
        ),
        out_specs=P("alpha", beta),
        check_vma=False,
    )
```

```python
import jax
import jax.numpy as jnp
from jax import lax
from jax.experimental import pallas as pl
from jax.experimental.pallas import tpu as pltpu
from jax.sharding import Mesh
from jax.sharding import PartitionSpec as P

ROWS = 8
PAIR = 2


def mix_kernel(integ_ref, picked_ref, sign_ref, table_ref, out_ref):
    halves, _, width = sign_ref.shape
    targets = out_ref.shape[1]
    block_len = out_ref.shape[2]
    src_blocks = width // block_len
    lane = lax.broadcasted_iota(jnp.int32, (targets, 2 * block_len), 1)
    upper = lane >= block_len
    integ = integ_ref[...]
    for row in range(picked_ref.shape[0]):
        mixed = jnp.dot(integ, picked_ref[row], preferred_element_type=jnp.float32)
        folded = jnp.zeros((targets, 2 * block_len), jnp.float32)
        for half in range(halves):
            weighted = mixed[:, half * width : (half + 1) * width] * sign_ref[half].astype(
                jnp.float32
            )
            high = weighted.astype(jnp.bfloat16)
            low = (weighted - high.astype(jnp.float32)).astype(jnp.bfloat16)
            table = table_ref[half]
            res = jnp.dot(table, high, preferred_element_type=jnp.float32) + jnp.dot(
                table, low, preferred_element_type=jnp.float32
            )
            for s in range(src_blocks):
                lanes = (s // 2) * 2 * block_len
                piece = res[s * targets : (s + 1) * targets, lanes : lanes + 2 * block_len]
                keep = upper if s % 2 else jnp.logical_not(upper)
                folded = folded + jnp.where(keep, piece, 0.0)
        folded = folded + pltpu.roll(folded, block_len, 1)
        out_ref[row] = folded[:, :block_len]


def mix_block(integ_pad, picked, sign_q, table_all, targets, block_len):
    rows, pairs, width = picked.shape
    return pl.pallas_call(
        mix_kernel,
        out_shape=jax.ShapeDtypeStruct((rows, targets, block_len), jnp.float32),
        grid=(rows // ROWS,),
        in_specs=[
            pl.BlockSpec((pairs, pairs), lambda i: (0, 0)),
            pl.BlockSpec((ROWS, pairs, width), lambda i: (i, 0, 0)),
            pl.BlockSpec(sign_q.shape, lambda i: (0, 0, 0)),
            pl.BlockSpec(table_all.shape, lambda i: (0, 0, 0)),
        ],
        out_specs=pl.BlockSpec((ROWS, targets, block_len), lambda i: (i, 0, 0)),
        compiler_params=pltpu.CompilerParams(dimension_semantics=("arbitrary",)),
    )(integ_pad, picked, sign_q, table_all)


def exchange_kernel(send_ref, recv_ref, send_sem, recv_sem, local_sem):
    groups = lax.axis_size("g")
    count = groups * PAIR
    alpha = lax.axis_index("alpha")
    me = lax.axis_index("g") * PAIR + lax.axis_index("m")

    def remote(slot, peer):
        return pltpu.make_async_remote_copy(
            src_ref=send_ref.at[slot],
            dst_ref=recv_ref.at[slot],
            send_sem=send_sem.at[slot],
            recv_sem=recv_sem.at[slot],
            device_id=(alpha, peer // PAIR, peer % PAIR),
            device_id_type=pl.DeviceIdType.MESH,
        )

    for step in range(1, count):
        dest = lax.rem(me + step, count)
        pltpu.make_async_remote_copy(
            src_ref=send_ref.at[dest],
            dst_ref=recv_ref.at[me],
            send_sem=send_sem.at[dest],
            recv_sem=recv_sem.at[me],
            device_id=(alpha, dest // PAIR, dest % PAIR),
            device_id_type=pl.DeviceIdType.MESH,
        ).start()
    local = pltpu.make_async_copy(send_ref.at[me], recv_ref.at[me], local_sem)
    local.start()
    local.wait()
    for step in range(1, count):
        dest = lax.rem(me + step, count)
        remote(dest, dest).wait_send()
    for step in range(1, count):
        src = lax.rem(me + count - step, count)
        remote(src, src).wait_recv()


def exchange(send):
    count = send.shape[0]
    return pl.pallas_call(
        exchange_kernel,
        out_shape=jax.ShapeDtypeStruct(send.shape, send.dtype),
        in_specs=[pl.BlockSpec(memory_space=pltpu.VMEM)],
        out_specs=pl.BlockSpec(memory_space=pl.ANY),
        scratch_shapes=[
            pltpu.SemaphoreType.DMA((count,)),
            pltpu.SemaphoreType.DMA((count,)),
            pltpu.SemaphoreType.DMA,
        ],
        compiler_params=pltpu.CompilerParams(has_side_effects=True),
    )(send)


def spread_kernel(own_ref, out_ref, send_sem, recv_sem, local_sem):
    count = lax.axis_size("alpha") * PAIR
    rows, cols = own_ref.shape
    group = lax.axis_index("g")
    me = lax.axis_index("alpha") * PAIR + lax.axis_index("m")

    def window(slot):
        return out_ref.at[pl.ds((slot // PAIR) * rows, rows), pl.ds((slot % PAIR) * cols, cols)]

    def remote(slot, sem_slot, peer):
        return pltpu.make_async_remote_copy(
            src_ref=own_ref,
            dst_ref=window(slot),
            send_sem=send_sem.at[sem_slot],
            recv_sem=recv_sem.at[slot],
            device_id=(peer // PAIR, group, peer % PAIR),
            device_id_type=pl.DeviceIdType.MESH,
        )

    for step in range(1, count):
        dest = lax.rem(me + step, count)
        remote(me, dest, dest).start()
    local = pltpu.make_async_copy(own_ref, window(me), local_sem)
    local.start()
    local.wait()
    for step in range(1, count):
        dest = lax.rem(me + step, count)
        remote(me, dest, dest).wait_send()
    for step in range(1, count):
        src = lax.rem(me + count - step, count)
        remote(src, src, src).wait_recv()


def spread(own, count):
    return pl.pallas_call(
        spread_kernel,
        out_shape=jax.ShapeDtypeStruct(
            (count // PAIR * own.shape[0], PAIR * own.shape[1]), own.dtype
        ),
        in_specs=[pl.BlockSpec(memory_space=pltpu.VMEM)],
        out_specs=pl.BlockSpec(memory_space=pl.ANY),
        scratch_shapes=[
            pltpu.SemaphoreType.DMA((count,)),
            pltpu.SemaphoreType.DMA((count,)),
            pltpu.SemaphoreType.DMA,
        ],
        compiler_params=pltpu.CompilerParams(has_side_effects=True),
    )(own)


def gather_alpha_kernel(own_ref, out_ref, send_sem, recv_sem, local_sem):
    count = lax.axis_size("alpha")
    group = lax.axis_index("g")
    member = lax.axis_index("m")
    me = lax.axis_index("alpha")

    def remote(slot, sem_slot, peer):
        return pltpu.make_async_remote_copy(
            src_ref=own_ref,
            dst_ref=out_ref.at[slot],
            send_sem=send_sem.at[sem_slot],
            recv_sem=recv_sem.at[slot],
            device_id=(peer, group, member),
            device_id_type=pl.DeviceIdType.MESH,
        )

    for step in range(1, count):
        dest = lax.rem(me + step, count)
        remote(me, dest, dest).start()
    local = pltpu.make_async_copy(own_ref, out_ref.at[me], local_sem)
    local.start()
    local.wait()
    for step in range(1, count):
        dest = lax.rem(me + step, count)
        remote(me, dest, dest).wait_send()
    for step in range(1, count):
        src = lax.rem(me + count - step, count)
        remote(src, src, src).wait_recv()


def gather_alpha(own, count):
    return pl.pallas_call(
        gather_alpha_kernel,
        out_shape=jax.ShapeDtypeStruct((count,) + own.shape, own.dtype),
        in_specs=[pl.BlockSpec(memory_space=pltpu.VMEM)],
        out_specs=pl.BlockSpec(memory_space=pl.ANY),
        scratch_shapes=[
            pltpu.SemaphoreType.DMA((count,)),
            pltpu.SemaphoreType.DMA((count,)),
            pltpu.SemaphoreType.DMA,
        ],
        compiler_params=pltpu.CompilerParams(has_side_effects=True),
    )(own)


def on_device(
    coefficients, diagonal, integrals, alpha_row, alpha_sign, beta_block, beta_sign, block_irrep
):
    alpha_rank = lax.axis_index("alpha")
    member = lax.axis_index("m")
    pair_count = integrals.shape[0]
    local_rows, local_cols = coefficients.shape
    block_len = beta_sign.shape[1] // pair_count
    per_device = local_rows // block_len
    src_blocks = local_cols // block_len
    total_blocks = lax.axis_size("g") * PAIR * src_blocks
    pairs = -(-pair_count // 16) * 16
    extra = pairs - pair_count
    sub_rows = block_len // PAIR

    alpha_size = lax.axis_size("alpha")
    gathered = spread(coefficients, alpha_size * PAIR)
    live_flags = (block_irrep == 0).astype(jnp.int32)
    live_rows = jnp.repeat(live_flags, block_len)
    gathered = gathered * live_rows[:, None].astype(jnp.bfloat16)
    window_rows, wide_cols = gathered.shape
    coeff_ext = jnp.concatenate(
        [gathered, -gathered, jnp.zeros((16, wide_cols), jnp.bfloat16)], axis=0
    )
    zero_row = 2 * window_rows

    integ_pad = jnp.pad(integrals, ((0, extra), (0, extra)))
    beta_block2 = lax.all_gather(beta_block.astype(jnp.bfloat16), "m", axis=0, tiled=True)
    beta_block2 = beta_block2.astype(jnp.int32)
    beta_sign2 = lax.all_gather(beta_sign.astype(jnp.bfloat16), "m", axis=0, tiled=True)
    sign_q = (
        beta_sign2.reshape(PAIR, src_blocks, pair_count, block_len)
        .transpose(0, 2, 1, 3)
        .reshape(PAIR, pair_count, local_cols)
    )
    sign_q = jnp.pad(sign_q, ((0, 0), (0, extra), (0, 0))).astype(jnp.bfloat16)
    target_iota = jnp.arange(total_blocks, dtype=jnp.int32)
    table_all = (target_iota[None, :, None] == beta_block2[:, None, :]).astype(jnp.bfloat16)
    table_all = jnp.pad(
        table_all.reshape(PAIR, src_blocks * total_blocks, pair_count),
        ((0, 0), (0, 0), (0, extra)),
    )

    own_flags = lax.dynamic_slice_in_dim(live_flags, alpha_rank * per_device, per_device, 0)

    dims = lax.GatherDimensionNumbers(
        offset_dims=(2,), collapsed_slice_dims=(0,), start_index_map=(0,)
    )

    block_count = live_flags.shape[0]
    block_iota = jnp.arange(block_count, dtype=jnp.int32)
    in_group = jnp.cumsum(live_flags.reshape(-1, per_device), axis=1).reshape(-1)
    is_first = (live_flags == 1) & (in_group == 1)
    is_extra = ((live_flags == 1) & jnp.logical_not(is_first)).astype(jnp.int32)
    extra_rank = jnp.cumsum(is_extra) - is_extra
    extra_total = jnp.sum(is_extra)
    block_of_extra = jnp.sum(
        jnp.where(
            (is_extra[None, :] == 1) & (extra_rank[None, :] == block_iota[:, None]),
            block_iota[None, :],
            0,
        ),
        axis=1,
    )
    own_first = lax.dynamic_slice_in_dim(is_first, alpha_rank * per_device, per_device, 0)
    first_blk = alpha_rank * per_device + jnp.argmax(own_first).astype(jnp.int32)
    my_count = 1 + jnp.maximum(extra_total - alpha_rank + alpha_size - 1, 0) // alpha_size
    beta_size = total_blocks // src_blocks

    def one_block(slot, buffer):
        block_id = jnp.where(
            slot == 0,
            first_blk,
            block_of_extra[jnp.maximum(slot - 1, 0) * alpha_size + alpha_rank],
        )
        first_row = block_id * block_len + member * sub_rows
        rows_src = lax.dynamic_slice_in_dim(alpha_row, first_row, sub_rows, 1)
        signs_src = lax.dynamic_slice_in_dim(alpha_sign, first_row, sub_rows, 1)
        row_ids = jnp.where(
            signs_src == 0,
            zero_row,
            jnp.where(signs_src < 0, rows_src + window_rows, rows_src),
        )
        row_ids = jnp.pad(row_ids, ((0, extra), (0, 0)), constant_values=zero_row).T
        picked = lax.gather(
            coeff_ext,
            row_ids[:, :, None],
            dims,
            slice_sizes=(1, wide_cols),
            mode=lax.GatherScatterMode.PROMISE_IN_BOUNDS,
        )
        summed = mix_block(integ_pad, picked, sign_q, table_all, total_blocks, block_len)
        part = summed.reshape(sub_rows, beta_size, local_cols).transpose(1, 0, 2)
        return lax.dynamic_update_slice(buffer, part[:, None], (0, slot, 0, 0))

    empty = jnp.zeros((beta_size, per_device, sub_rows, local_cols), jnp.float32)
    send = lax.fori_loop(0, my_count, one_block, empty)
    recv = exchange(send)
    groups = recv.shape[0] // PAIR
    recv = recv.reshape(groups, PAIR, per_device, sub_rows, local_cols).sum(axis=0)
    done = recv.transpose(1, 0, 2, 3).reshape(per_device, block_len, local_cols)
    everyone = gather_alpha(done[1:], alpha_size).reshape(
        alpha_size * (per_device - 1), block_len, local_cols
    )
    own_rank = lax.dynamic_slice_in_dim(extra_rank, alpha_rank * per_device, per_device, 0)
    pick = (own_rank % alpha_size) * (per_device - 1) + jnp.minimum(
        own_rank // alpha_size, per_device - 2
    )
    placed = jnp.where(own_first[:, None, None], done[0][None], everyone[pick])
    placed = placed.reshape(local_rows, local_cols)
    own_live_rows = jnp.repeat(own_flags, block_len)
    total = diagonal * coefficients.astype(jnp.float32) + placed
    return jnp.where(own_live_rows[:, None] == 1, total, jnp.zeros_like(total))


def solution(mesh):
    alpha_size, beta_size = mesh.devices.shape
    split_mesh = Mesh(
        mesh.devices.reshape(alpha_size, beta_size // PAIR, PAIR), ("alpha", "g", "m")
    )
    beta = ("g", "m")
    return jax.shard_map(
        on_device,
        mesh=split_mesh,
        in_specs=(
            P("alpha", beta),
            P("alpha", beta),
            P(),
            P(),
            P(),
            P(beta, None),
            P(beta, None),
            P(),
        ),
        out_specs=P("alpha", beta),
        check_vma=False,
    )
```

```python
import jax
import jax.numpy as jnp
from jax import lax
from jax.experimental import pallas as pl
from jax.experimental.pallas import tpu as pltpu
from jax.sharding import Mesh
from jax.sharding import PartitionSpec as P

ROWS = 8
PAIR = 2


def mix_kernel(integ_ref, picked_ref, sign_ref, table_ref, out_ref):
    halves, _, width = sign_ref.shape
    targets = out_ref.shape[1]
    block_len = out_ref.shape[2]
    src_blocks = width // block_len
    lane = lax.broadcasted_iota(jnp.int32, (targets, 2 * block_len), 1)
    upper = lane >= block_len
    integ = integ_ref[...]
    for row in range(picked_ref.shape[0]):
        mixed = jnp.dot(integ, picked_ref[row], preferred_element_type=jnp.float32)
        folded = jnp.zeros((targets, 2 * block_len), jnp.float32)
        for half in range(halves):
            weighted = mixed[:, half * width : (half + 1) * width] * sign_ref[half].astype(
                jnp.float32
            )
            high = weighted.astype(jnp.bfloat16)
            low = (weighted - high.astype(jnp.float32)).astype(jnp.bfloat16)
            table = table_ref[half]
            res = jnp.dot(table, high, preferred_element_type=jnp.float32) + jnp.dot(
                table, low, preferred_element_type=jnp.float32
            )
            for s in range(src_blocks):
                lanes = (s // 2) * 2 * block_len
                piece = res[s * targets : (s + 1) * targets, lanes : lanes + 2 * block_len]
                keep = upper if s % 2 else jnp.logical_not(upper)
                folded = folded + jnp.where(keep, piece, 0.0)
        folded = folded + pltpu.roll(folded, block_len, 1)
        out_ref[row] = folded[:, :block_len]


def mix_block(integ_pad, picked, sign_q, table_all, targets, block_len):
    rows, pairs, width = picked.shape
    return pl.pallas_call(
        mix_kernel,
        out_shape=jax.ShapeDtypeStruct((rows, targets, block_len), jnp.float32),
        grid=(rows // ROWS,),
        in_specs=[
            pl.BlockSpec((pairs, pairs), lambda i: (0, 0)),
            pl.BlockSpec((ROWS, pairs, width), lambda i: (i, 0, 0)),
            pl.BlockSpec(sign_q.shape, lambda i: (0, 0, 0)),
            pl.BlockSpec(table_all.shape, lambda i: (0, 0, 0)),
        ],
        out_specs=pl.BlockSpec((ROWS, targets, block_len), lambda i: (i, 0, 0)),
        compiler_params=pltpu.CompilerParams(dimension_semantics=("arbitrary",)),
    )(integ_pad, picked, sign_q, table_all)


def exchange_kernel(send_ref, recv_ref, send_sem, recv_sem, local_sem):
    groups = lax.axis_size("g")
    count = groups * PAIR
    alpha = lax.axis_index("alpha")
    me = lax.axis_index("g") * PAIR + lax.axis_index("m")

    def remote(src_slot, dst_slot, sem_slot, peer):
        return pltpu.make_async_remote_copy(
            src_ref=send_ref.at[src_slot],
            dst_ref=recv_ref.at[dst_slot],
            send_sem=send_sem.at[sem_slot],
            recv_sem=recv_sem.at[dst_slot],
            device_id=(alpha, peer // PAIR, peer % PAIR),
            device_id_type=pl.DeviceIdType.MESH,
        )

    barrier = pltpu.get_barrier_semaphore()
    for step in range(1, count):
        peer = lax.rem(me + step, count)
        pl.semaphore_signal(
            barrier, 1, device_id=(alpha, peer // PAIR, peer % PAIR),
            device_id_type=pl.DeviceIdType.MESH,
        )
    pl.semaphore_wait(barrier, count - 1)

    for step in range(1, count):
        dest = lax.rem(me + step, count)
        remote(dest, me, dest, dest).start()
    local = pltpu.make_async_copy(send_ref.at[me], recv_ref.at[me], local_sem)
    local.start()
    local.wait()
    for step in range(1, count):
        dest = lax.rem(me + step, count)
        remote(dest, me, dest, dest).wait_send()
    for step in range(1, count):
        src = lax.rem(me + count - step, count)
        remote(src, src, src, src).wait_recv()


def exchange(send):
    count = send.shape[0]
    return pl.pallas_call(
        exchange_kernel,
        out_shape=jax.ShapeDtypeStruct(send.shape, send.dtype),
        in_specs=[pl.BlockSpec(memory_space=pl.ANY)],
        out_specs=pl.BlockSpec(memory_space=pl.ANY),
        scratch_shapes=[
            pltpu.SemaphoreType.DMA((count,)),
            pltpu.SemaphoreType.DMA((count,)),
            pltpu.SemaphoreType.DMA,
        ],
        compiler_params=pltpu.CompilerParams(collective_id=0, has_side_effects=True),
    )(send)


def spread_kernel(own_ref, out_ref, send_sem, recv_sem, local_sem):
    count = lax.axis_size("alpha") * PAIR
    rows, cols = own_ref.shape
    group = lax.axis_index("g")
    me = lax.axis_index("alpha") * PAIR + lax.axis_index("m")

    def window(slot):
        return out_ref.at[pl.ds((slot // PAIR) * rows, rows), pl.ds((slot % PAIR) * cols, cols)]

    def remote(slot, sem_slot, peer):
        return pltpu.make_async_remote_copy(
            src_ref=own_ref,
            dst_ref=window(slot),
            send_sem=send_sem.at[sem_slot],
            recv_sem=recv_sem.at[slot],
            device_id=(peer // PAIR, group, peer % PAIR),
            device_id_type=pl.DeviceIdType.MESH,
        )

    for step in range(1, count):
        dest = lax.rem(me + step, count)
        remote(me, dest, dest).start()
    local = pltpu.make_async_copy(own_ref, window(me), local_sem)
    local.start()
    local.wait()
    for step in range(1, count):
        dest = lax.rem(me + step, count)
        remote(me, dest, dest).wait_send()
    for step in range(1, count):
        src = lax.rem(me + count - step, count)
        remote(src, src, src).wait_recv()


def spread(own, count):
    return pl.pallas_call(
        spread_kernel,
        out_shape=jax.ShapeDtypeStruct(
            (count // PAIR * own.shape[0], PAIR * own.shape[1]), own.dtype
        ),
        in_specs=[pl.BlockSpec(memory_space=pl.ANY)],
        out_specs=pl.BlockSpec(memory_space=pl.ANY),
        scratch_shapes=[
            pltpu.SemaphoreType.DMA((count,)),
            pltpu.SemaphoreType.DMA((count,)),
            pltpu.SemaphoreType.DMA,
        ],
        compiler_params=pltpu.CompilerParams(has_side_effects=True),
    )(own)


def gather_alpha_kernel(own_ref, out_ref, send_sem, recv_sem, local_sem):
    count = lax.axis_size("alpha")
    group = lax.axis_index("g")
    member = lax.axis_index("m")
    me = lax.axis_index("alpha")

    def remote(slot, sem_slot, peer):
        return pltpu.make_async_remote_copy(
            src_ref=own_ref,
            dst_ref=out_ref.at[slot],
            send_sem=send_sem.at[sem_slot],
            recv_sem=recv_sem.at[slot],
            device_id=(peer, group, member),
            device_id_type=pl.DeviceIdType.MESH,
        )

    for step in range(1, count):
        dest = lax.rem(me + step, count)
        remote(me, dest, dest).start()
    local = pltpu.make_async_copy(own_ref, out_ref.at[me], local_sem)
    local.start()
    local.wait()
    for step in range(1, count):
        dest = lax.rem(me + step, count)
        remote(me, dest, dest).wait_send()
    for step in range(1, count):
        src = lax.rem(me + count - step, count)
        remote(src, src, src).wait_recv()


def gather_alpha(own, count):
    return pl.pallas_call(
        gather_alpha_kernel,
        out_shape=jax.ShapeDtypeStruct((count,) + own.shape, own.dtype),
        in_specs=[pl.BlockSpec(memory_space=pl.ANY)],
        out_specs=pl.BlockSpec(memory_space=pl.ANY),
        scratch_shapes=[
            pltpu.SemaphoreType.DMA((count,)),
            pltpu.SemaphoreType.DMA((count,)),
            pltpu.SemaphoreType.DMA,
        ],
        compiler_params=pltpu.CompilerParams(has_side_effects=True),
    )(own)


def on_device(
    coefficients, diagonal, integrals, alpha_row, alpha_sign, beta_block, beta_sign, block_irrep
):
    alpha_rank = lax.axis_index("alpha")
    member = lax.axis_index("m")
    pair_count = integrals.shape[0]
    local_rows, local_cols = coefficients.shape
    block_len = beta_sign.shape[1] // pair_count
    per_device = local_rows // block_len
    src_blocks = local_cols // block_len
    total_blocks = lax.axis_size("g") * PAIR * src_blocks
    pairs = -(-pair_count // 16) * 16
    extra = pairs - pair_count
    sub_rows = block_len // PAIR

    alpha_size = lax.axis_size("alpha")
    gathered = spread(coefficients, alpha_size * PAIR)
    live_flags = (block_irrep == 0).astype(jnp.int32)
    live_rows = jnp.repeat(live_flags, block_len)
    gathered = gathered * live_rows[:, None].astype(jnp.bfloat16)
    window_rows, wide_cols = gathered.shape
    coeff_ext = jnp.concatenate(
        [gathered, -gathered, jnp.zeros((16, wide_cols), jnp.bfloat16)], axis=0
    )
    zero_row = 2 * window_rows

    integ_pad = jnp.pad(integrals, ((0, extra), (0, extra)))
    beta_block2 = lax.all_gather(beta_block.astype(jnp.bfloat16), "m", axis=0, tiled=True)
    beta_block2 = beta_block2.astype(jnp.int32)
    beta_sign2 = lax.all_gather(beta_sign.astype(jnp.bfloat16), "m", axis=0, tiled=True)
    sign_q = (
        beta_sign2.reshape(PAIR, src_blocks, pair_count, block_len)
        .transpose(0, 2, 1, 3)
        .reshape(PAIR, pair_count, local_cols)
    )
    sign_q = jnp.pad(sign_q, ((0, 0), (0, extra), (0, 0))).astype(jnp.bfloat16)
    target_iota = jnp.arange(total_blocks, dtype=jnp.int32)
    table_all = (target_iota[None, :, None] == beta_block2[:, None, :]).astype(jnp.bfloat16)
    table_all = jnp.pad(
        table_all.reshape(PAIR, src_blocks * total_blocks, pair_count),
        ((0, 0), (0, 0), (0, extra)),
    )

    own_flags = lax.dynamic_slice_in_dim(live_flags, alpha_rank * per_device, per_device, 0)

    dims = lax.GatherDimensionNumbers(
        offset_dims=(2,), collapsed_slice_dims=(0,), start_index_map=(0,)
    )

    block_count = live_flags.shape[0]
    block_iota = jnp.arange(block_count, dtype=jnp.int32)
    in_group = jnp.cumsum(live_flags.reshape(-1, per_device), axis=1).reshape(-1)
    is_first = (live_flags == 1) & (in_group == 1)
    is_extra = ((live_flags == 1) & jnp.logical_not(is_first)).astype(jnp.int32)
    extra_rank = jnp.cumsum(is_extra) - is_extra
    extra_total = jnp.sum(is_extra)
    block_of_extra = jnp.sum(
        jnp.where(
            (is_extra[None, :] == 1) & (extra_rank[None, :] == block_iota[:, None]),
            block_iota[None, :],
            0,
        ),
        axis=1,
    )
    own_first = lax.dynamic_slice_in_dim(is_first, alpha_rank * per_device, per_device, 0)
    first_blk = alpha_rank * per_device + jnp.argmax(own_first).astype(jnp.int32)
    my_count = 1 + jnp.maximum(extra_total - alpha_rank + alpha_size - 1, 0) // alpha_size
    beta_size = total_blocks // src_blocks

    def one_block(slot, buffer):
        block_id = jnp.where(
            slot == 0,
            first_blk,
            block_of_extra[jnp.maximum(slot - 1, 0) * alpha_size + alpha_rank],
        )
        first_row = block_id * block_len + member * sub_rows
        rows_src = lax.dynamic_slice_in_dim(alpha_row, first_row, sub_rows, 1)
        signs_src = lax.dynamic_slice_in_dim(alpha_sign, first_row, sub_rows, 1)
        row_ids = jnp.where(
            signs_src == 0,
            zero_row,
            jnp.where(signs_src < 0, rows_src + window_rows, rows_src),
        )
        row_ids = jnp.pad(row_ids, ((0, extra), (0, 0)), constant_values=zero_row).T
        picked = lax.gather(
            coeff_ext,
            row_ids[:, :, None],
            dims,
            slice_sizes=(1, wide_cols),
            mode=lax.GatherScatterMode.PROMISE_IN_BOUNDS,
        )
        summed = mix_block(integ_pad, picked, sign_q, table_all, total_blocks, block_len)
        part = summed.reshape(sub_rows, beta_size, local_cols).transpose(1, 0, 2)
        recv = exchange(part)
        groups = recv.shape[0] // PAIR
        rows = recv.reshape(groups, PAIR * sub_rows, local_cols).sum(axis=0)
        return lax.dynamic_update_slice(buffer, rows[None], (slot, 0, 0))

    empty = jnp.zeros((per_device, block_len, local_cols), jnp.float32)
    done = lax.fori_loop(0, my_count, one_block, empty)
    everyone = gather_alpha(done[1:], alpha_size).reshape(
        alpha_size * (per_device - 1), block_len, local_cols
    )
    own_rank = lax.dynamic_slice_in_dim(extra_rank, alpha_rank * per_device, per_device, 0)
    pick = (own_rank % alpha_size) * (per_device - 1) + jnp.minimum(
        own_rank // alpha_size, per_device - 2
    )
    placed = jnp.where(own_first[:, None, None], done[0][None], everyone[pick])
    placed = placed.reshape(local_rows, local_cols)
    own_live_rows = jnp.repeat(own_flags, block_len)
    total = diagonal * coefficients.astype(jnp.float32) + placed
    return jnp.where(own_live_rows[:, None] == 1, total, jnp.zeros_like(total))


def solution(mesh):
    alpha_size, beta_size = mesh.devices.shape
    split_mesh = Mesh(
        mesh.devices.reshape(alpha_size, beta_size // PAIR, PAIR), ("alpha", "g", "m")
    )
    beta = ("g", "m")
    return jax.shard_map(
        on_device,
        mesh=split_mesh,
        in_specs=(
            P("alpha", beta),
            P("alpha", beta),
            P(),
            P(),
            P(),
            P(beta, None),
            P(beta, None),
            P(),
        ),
        out_specs=P("alpha", beta),
        check_vma=False,
    )
```

```python
import jax
import jax.numpy as jnp
from jax import lax
from jax.experimental import pallas as pl
from jax.experimental.pallas import tpu as pltpu
from jax.sharding import Mesh
from jax.sharding import PartitionSpec as P

ROWS = 8
PAIR = 2


def mix_kernel(integ_ref, picked_ref, sign_ref, table_ref, out_ref):
    halves, _, width = sign_ref.shape
    targets = out_ref.shape[1]
    block_len = out_ref.shape[2]
    src_blocks = width // block_len
    lane = lax.broadcasted_iota(jnp.int32, (targets, 2 * block_len), 1)
    upper = lane >= block_len
    integ = integ_ref[...]
    for row in range(picked_ref.shape[0]):
        mixed = jnp.dot(integ, picked_ref[row], preferred_element_type=jnp.float32)
        folded = jnp.zeros((targets, 2 * block_len), jnp.float32)
        for half in range(halves):
            weighted = mixed[:, half * width : (half + 1) * width] * sign_ref[half].astype(
                jnp.float32
            )
            high = weighted.astype(jnp.bfloat16)
            low = (weighted - high.astype(jnp.float32)).astype(jnp.bfloat16)
            table = table_ref[half]
            res = jnp.dot(table, high, preferred_element_type=jnp.float32) + jnp.dot(
                table, low, preferred_element_type=jnp.float32
            )
            for s in range(src_blocks):
                lanes = (s // 2) * 2 * block_len
                piece = res[s * targets : (s + 1) * targets, lanes : lanes + 2 * block_len]
                keep = upper if s % 2 else jnp.logical_not(upper)
                folded = folded + jnp.where(keep, piece, 0.0)
        folded = folded + pltpu.roll(folded, block_len, 1)
        out_ref[row] = folded[:, :block_len]


def mix_block(integ_pad, picked, sign_q, table_all, targets, block_len):
    rows, pairs, width = picked.shape
    return pl.pallas_call(
        mix_kernel,
        out_shape=jax.ShapeDtypeStruct((rows, targets, block_len), jnp.float32),
        grid=(rows // ROWS,),
        in_specs=[
            pl.BlockSpec((pairs, pairs), lambda i: (0, 0)),
            pl.BlockSpec((ROWS, pairs, width), lambda i: (i, 0, 0)),
            pl.BlockSpec(sign_q.shape, lambda i: (0, 0, 0)),
            pl.BlockSpec(table_all.shape, lambda i: (0, 0, 0)),
        ],
        out_specs=pl.BlockSpec((ROWS, targets, block_len), lambda i: (i, 0, 0)),
        compiler_params=pltpu.CompilerParams(dimension_semantics=("arbitrary",)),
    )(integ_pad, picked, sign_q, table_all)


def exchange_kernel(send_ref, recv_ref, send_sem, recv_sem, local_sem):
    groups = lax.axis_size("g")
    count = groups * PAIR
    alpha = lax.axis_index("alpha")
    me = lax.axis_index("g") * PAIR + lax.axis_index("m")

    def remote(src_slot, dst_slot, sem_slot, peer):
        return pltpu.make_async_remote_copy(
            src_ref=send_ref.at[src_slot],
            dst_ref=recv_ref.at[dst_slot],
            send_sem=send_sem.at[sem_slot],
            recv_sem=recv_sem.at[dst_slot],
            device_id=(alpha, peer // PAIR, peer % PAIR),
            device_id_type=pl.DeviceIdType.MESH,
        )

    barrier = pltpu.get_barrier_semaphore()
    for step in range(1, count):
        peer = lax.rem(me + step, count)
        pl.semaphore_signal(
            barrier, 1, device_id=(alpha, peer // PAIR, peer % PAIR),
            device_id_type=pl.DeviceIdType.MESH,
        )
    pl.semaphore_wait(barrier, count - 1)

    for step in range(1, count):
        dest = lax.rem(me + step, count)
        remote(dest, me, dest, dest).start()
    local = pltpu.make_async_copy(send_ref.at[me], recv_ref.at[me], local_sem)
    local.start()
    local.wait()
    for step in range(1, count):
        dest = lax.rem(me + step, count)
        remote(dest, me, dest, dest).wait_send()
    for step in range(1, count):
        src = lax.rem(me + count - step, count)
        remote(src, src, src, src).wait_recv()


def exchange(send):
    count = send.shape[0]
    return pl.pallas_call(
        exchange_kernel,
        out_shape=jax.ShapeDtypeStruct(send.shape, send.dtype),
        in_specs=[pl.BlockSpec(memory_space=pl.ANY)],
        out_specs=pl.BlockSpec(memory_space=pl.ANY),
        scratch_shapes=[
            pltpu.SemaphoreType.DMA((count,)),
            pltpu.SemaphoreType.DMA((count,)),
            pltpu.SemaphoreType.DMA,
        ],
        compiler_params=pltpu.CompilerParams(collective_id=0, has_side_effects=True),
    )(send)


def spread_kernel(own_ref, out_ref, send_sem, recv_sem, local_sem):
    count = lax.axis_size("alpha") * PAIR
    rows, cols = own_ref.shape
    group = lax.axis_index("g")
    me = lax.axis_index("alpha") * PAIR + lax.axis_index("m")

    def window(slot):
        return out_ref.at[pl.ds((slot // PAIR) * rows, rows), pl.ds((slot % PAIR) * cols, cols)]

    def remote(slot, sem_slot, peer):
        return pltpu.make_async_remote_copy(
            src_ref=own_ref,
            dst_ref=window(slot),
            send_sem=send_sem.at[sem_slot],
            recv_sem=recv_sem.at[slot],
            device_id=(peer // PAIR, group, peer % PAIR),
            device_id_type=pl.DeviceIdType.MESH,
        )

    for step in range(1, count):
        dest = lax.rem(me + step, count)
        remote(me, dest, dest).start()
    local = pltpu.make_async_copy(own_ref, window(me), local_sem)
    local.start()
    local.wait()
    for step in range(1, count):
        dest = lax.rem(me + step, count)
        remote(me, dest, dest).wait_send()
    for step in range(1, count):
        src = lax.rem(me + count - step, count)
        remote(src, src, src).wait_recv()


def spread(own, count):
    return pl.pallas_call(
        spread_kernel,
        out_shape=jax.ShapeDtypeStruct(
            (count // PAIR * own.shape[0], PAIR * own.shape[1]), own.dtype
        ),
        in_specs=[pl.BlockSpec(memory_space=pl.ANY)],
        out_specs=pl.BlockSpec(memory_space=pl.ANY),
        scratch_shapes=[
            pltpu.SemaphoreType.DMA((count,)),
            pltpu.SemaphoreType.DMA((count,)),
            pltpu.SemaphoreType.DMA,
        ],
        compiler_params=pltpu.CompilerParams(has_side_effects=True),
    )(own)


def gather_alpha_kernel(own_ref, out_ref, send_sem, recv_sem, local_sem):
    count = lax.axis_size("alpha")
    group = lax.axis_index("g")
    member = lax.axis_index("m")
    me = lax.axis_index("alpha")

    def remote(slot, sem_slot, peer):
        return pltpu.make_async_remote_copy(
            src_ref=own_ref,
            dst_ref=out_ref.at[slot],
            send_sem=send_sem.at[sem_slot],
            recv_sem=recv_sem.at[slot],
            device_id=(peer, group, member),
            device_id_type=pl.DeviceIdType.MESH,
        )

    barrier = pltpu.get_barrier_semaphore()
    for step in range(1, count):
        peer = lax.rem(me + step, count)
        pl.semaphore_signal(
            barrier, 1, device_id=(peer, group, member), device_id_type=pl.DeviceIdType.MESH
        )
    pl.semaphore_wait(barrier, count - 1)

    for step in range(1, count):
        dest = lax.rem(me + step, count)
        remote(me, dest, dest).start()
    local = pltpu.make_async_copy(own_ref, out_ref.at[me], local_sem)
    local.start()
    local.wait()
    for step in range(1, count):
        dest = lax.rem(me + step, count)
        remote(me, dest, dest).wait_send()
    for step in range(1, count):
        src = lax.rem(me + count - step, count)
        remote(src, src, src).wait_recv()


def gather_alpha(own, count):
    return pl.pallas_call(
        gather_alpha_kernel,
        out_shape=jax.ShapeDtypeStruct((count,) + own.shape, own.dtype),
        in_specs=[pl.BlockSpec(memory_space=pl.ANY)],
        out_specs=pl.BlockSpec(memory_space=pl.ANY),
        scratch_shapes=[
            pltpu.SemaphoreType.DMA((count,)),
            pltpu.SemaphoreType.DMA((count,)),
            pltpu.SemaphoreType.DMA,
        ],
        compiler_params=pltpu.CompilerParams(collective_id=1, has_side_effects=True),
    )(own)


def on_device(
    coefficients, diagonal, integrals, alpha_row, alpha_sign, beta_block, beta_sign, block_irrep
):
    alpha_rank = lax.axis_index("alpha")
    member = lax.axis_index("m")
    pair_count = integrals.shape[0]
    local_rows, local_cols = coefficients.shape
    block_len = beta_sign.shape[1] // pair_count
    per_device = local_rows // block_len
    src_blocks = local_cols // block_len
    total_blocks = lax.axis_size("g") * PAIR * src_blocks
    pairs = -(-pair_count // 16) * 16
    extra = pairs - pair_count
    sub_rows = block_len // PAIR

    alpha_size = lax.axis_size("alpha")
    gathered = spread(coefficients, alpha_size * PAIR)
    live_flags = (block_irrep == 0).astype(jnp.int32)
    live_rows = jnp.repeat(live_flags, block_len)
    gathered = gathered * live_rows[:, None].astype(jnp.bfloat16)
    window_rows, wide_cols = gathered.shape
    coeff_ext = jnp.concatenate(
        [gathered, -gathered, jnp.zeros((16, wide_cols), jnp.bfloat16)], axis=0
    )
    zero_row = 2 * window_rows

    integ_pad = jnp.pad(integrals, ((0, extra), (0, extra)))
    beta_block2 = lax.all_gather(beta_block.astype(jnp.bfloat16), "m", axis=0, tiled=True)
    beta_block2 = beta_block2.astype(jnp.int32)
    beta_sign2 = lax.all_gather(beta_sign.astype(jnp.bfloat16), "m", axis=0, tiled=True)
    sign_q = (
        beta_sign2.reshape(PAIR, src_blocks, pair_count, block_len)
        .transpose(0, 2, 1, 3)
        .reshape(PAIR, pair_count, local_cols)
    )
    sign_q = jnp.pad(sign_q, ((0, 0), (0, extra), (0, 0))).astype(jnp.bfloat16)
    target_iota = jnp.arange(total_blocks, dtype=jnp.int32)
    table_all = (target_iota[None, :, None] == beta_block2[:, None, :]).astype(jnp.bfloat16)
    table_all = jnp.pad(
        table_all.reshape(PAIR, src_blocks * total_blocks, pair_count),
        ((0, 0), (0, 0), (0, extra)),
    )

    own_flags = lax.dynamic_slice_in_dim(live_flags, alpha_rank * per_device, per_device, 0)

    dims = lax.GatherDimensionNumbers(
        offset_dims=(2,), collapsed_slice_dims=(0,), start_index_map=(0,)
    )

    block_count = live_flags.shape[0]
    block_iota = jnp.arange(block_count, dtype=jnp.int32)
    in_group = jnp.cumsum(live_flags.reshape(-1, per_device), axis=1).reshape(-1)
    is_first = (live_flags == 1) & (in_group == 1)
    is_extra = ((live_flags == 1) & jnp.logical_not(is_first)).astype(jnp.int32)
    extra_rank = jnp.cumsum(is_extra) - is_extra
    extra_total = jnp.sum(is_extra)
    block_of_extra = jnp.sum(
        jnp.where(
            (is_extra[None, :] == 1) & (extra_rank[None, :] == block_iota[:, None]),
            block_iota[None, :],
            0,
        ),
        axis=1,
    )
    own_first = lax.dynamic_slice_in_dim(is_first, alpha_rank * per_device, per_device, 0)
    first_blk = alpha_rank * per_device + jnp.argmax(own_first).astype(jnp.int32)
    my_count = 1 + jnp.maximum(extra_total - alpha_rank + alpha_size - 1, 0) // alpha_size
    beta_size = total_blocks // src_blocks

    def one_block(slot, buffer):
        block_id = jnp.where(
            slot == 0,
            first_blk,
            block_of_extra[jnp.maximum(slot - 1, 0) * alpha_size + alpha_rank],
        )
        first_row = block_id * block_len + member * sub_rows
        rows_src = lax.dynamic_slice_in_dim(alpha_row, first_row, sub_rows, 1)
        signs_src = lax.dynamic_slice_in_dim(alpha_sign, first_row, sub_rows, 1)
        row_ids = jnp.where(
            signs_src == 0,
            zero_row,
            jnp.where(signs_src < 0, rows_src + window_rows, rows_src),
        )
        row_ids = jnp.pad(row_ids, ((0, extra), (0, 0)), constant_values=zero_row).T
        picked = lax.gather(
            coeff_ext,
            row_ids[:, :, None],
            dims,
            slice_sizes=(1, wide_cols),
            mode=lax.GatherScatterMode.PROMISE_IN_BOUNDS,
        )
        summed = mix_block(integ_pad, picked, sign_q, table_all, total_blocks, block_len)
        part = summed.reshape(sub_rows, beta_size, local_cols).transpose(1, 0, 2)
        recv = exchange(part)
        groups = recv.shape[0] // PAIR
        rows = recv.reshape(groups, PAIR * sub_rows, local_cols).sum(axis=0)
        return lax.dynamic_update_slice(buffer, rows[None], (slot, 0, 0))

    empty = jnp.zeros((per_device, block_len, local_cols), jnp.float32)
    done = lax.fori_loop(0, my_count, one_block, empty)
    pushes = jnp.maximum(extra_total + alpha_size - 1, 0) // alpha_size

    def push(step, held):
        arrived = gather_alpha(done[step + 1], alpha_size)
        return lax.dynamic_update_slice(held, arrived[None], (step, 0, 0, 0))

    everyone = lax.fori_loop(
        0, pushes, push, jnp.zeros((per_device - 1, alpha_size, block_len, local_cols), jnp.float32)
    ).reshape((per_device - 1) * alpha_size, block_len, local_cols)
    own_rank = lax.dynamic_slice_in_dim(extra_rank, alpha_rank * per_device, per_device, 0)
    pick = jnp.minimum(own_rank // alpha_size, per_device - 2) * alpha_size + own_rank % alpha_size
    placed = jnp.where(own_first[:, None, None], done[0][None], everyone[pick])
    placed = placed.reshape(local_rows, local_cols)
    own_live_rows = jnp.repeat(own_flags, block_len)
    total = diagonal * coefficients.astype(jnp.float32) + placed
    return jnp.where(own_live_rows[:, None] == 1, total, jnp.zeros_like(total))


def solution(mesh):
    alpha_size, beta_size = mesh.devices.shape
    split_mesh = Mesh(
        mesh.devices.reshape(alpha_size, beta_size // PAIR, PAIR), ("alpha", "g", "m")
    )
    beta = ("g", "m")
    return jax.shard_map(
        on_device,
        mesh=split_mesh,
        in_specs=(
            P("alpha", beta),
            P("alpha", beta),
            P(),
            P(),
            P(),
            P(beta, None),
            P(beta, None),
            P(),
        ),
        out_specs=P("alpha", beta),
        check_vma=False,
    )
```

```python
import jax
import jax.numpy as jnp
from jax import lax
from jax.experimental import pallas as pl
from jax.experimental.pallas import tpu as pltpu
from jax.sharding import Mesh
from jax.sharding import PartitionSpec as P

ROWS = 8
PAIR = 2


def mix_kernel(integ_ref, picked_ref, sign_ref, table_ref, out_ref):
    halves, _, width = sign_ref.shape
    targets = out_ref.shape[1]
    block_len = out_ref.shape[2]
    src_blocks = width // block_len
    lane = lax.broadcasted_iota(jnp.int32, (targets, 2 * block_len), 1)
    upper = lane >= block_len
    integ = integ_ref[...]
    for row in range(picked_ref.shape[0]):
        mixed = jnp.dot(integ, picked_ref[row], preferred_element_type=jnp.float32)
        folded = jnp.zeros((targets, 2 * block_len), jnp.float32)
        for half in range(halves):
            weighted = mixed[:, half * width : (half + 1) * width] * sign_ref[half].astype(
                jnp.float32
            )
            high = weighted.astype(jnp.bfloat16)
            low = (weighted - high.astype(jnp.float32)).astype(jnp.bfloat16)
            table = table_ref[half]
            res = jnp.dot(table, high, preferred_element_type=jnp.float32) + jnp.dot(
                table, low, preferred_element_type=jnp.float32
            )
            for s in range(src_blocks):
                lanes = (s // 2) * 2 * block_len
                piece = res[s * targets : (s + 1) * targets, lanes : lanes + 2 * block_len]
                keep = upper if s % 2 else jnp.logical_not(upper)
                folded = folded + jnp.where(keep, piece, 0.0)
        folded = folded + pltpu.roll(folded, block_len, 1)
        out_ref[row] = folded[:, :block_len]


def mix_block(integ_pad, picked, sign_q, table_all, targets, block_len):
    rows, pairs, width = picked.shape
    return pl.pallas_call(
        mix_kernel,
        out_shape=jax.ShapeDtypeStruct((rows, targets, block_len), jnp.float32),
        grid=(rows // ROWS,),
        in_specs=[
            pl.BlockSpec((pairs, pairs), lambda i: (0, 0)),
            pl.BlockSpec((ROWS, pairs, width), lambda i: (i, 0, 0)),
            pl.BlockSpec(sign_q.shape, lambda i: (0, 0, 0)),
            pl.BlockSpec(table_all.shape, lambda i: (0, 0, 0)),
        ],
        out_specs=pl.BlockSpec((ROWS, targets, block_len), lambda i: (i, 0, 0)),
        compiler_params=pltpu.CompilerParams(dimension_semantics=("arbitrary",)),
    )(integ_pad, picked, sign_q, table_all)


def exchange_kernel(send_ref, recv_ref, send_sem, recv_sem, local_sem):
    groups = lax.axis_size("g")
    count = groups * PAIR
    alpha = lax.axis_index("alpha")
    me = lax.axis_index("g") * PAIR + lax.axis_index("m")

    def remote(src_slot, dst_slot, sem_slot, peer):
        return pltpu.make_async_remote_copy(
            src_ref=send_ref.at[src_slot],
            dst_ref=recv_ref.at[dst_slot],
            send_sem=send_sem.at[sem_slot],
            recv_sem=recv_sem.at[dst_slot],
            device_id=(alpha, peer // PAIR, peer % PAIR),
            device_id_type=pl.DeviceIdType.MESH,
        )

    barrier = pltpu.get_barrier_semaphore()
    for step in range(1, count):
        peer = lax.rem(me + step, count)
        pl.semaphore_signal(
            barrier, 1, device_id=(alpha, peer // PAIR, peer % PAIR),
            device_id_type=pl.DeviceIdType.MESH,
        )
    pl.semaphore_wait(barrier, count - 1)

    for step in range(1, count):
        dest = lax.rem(me + step, count)
        remote(dest, me, dest, dest).start()
    local = pltpu.make_async_copy(send_ref.at[me], recv_ref.at[me], local_sem)
    local.start()
    local.wait()
    for step in range(1, count):
        dest = lax.rem(me + step, count)
        remote(dest, me, dest, dest).wait_send()
    for step in range(1, count):
        src = lax.rem(me + count - step, count)
        remote(src, src, src, src).wait_recv()


def exchange(send):
    count = send.shape[0]
    return pl.pallas_call(
        exchange_kernel,
        out_shape=jax.ShapeDtypeStruct(send.shape, send.dtype),
        in_specs=[pl.BlockSpec(memory_space=pl.ANY)],
        out_specs=pl.BlockSpec(memory_space=pl.ANY),
        scratch_shapes=[
            pltpu.SemaphoreType.DMA((count,)),
            pltpu.SemaphoreType.DMA((count,)),
            pltpu.SemaphoreType.DMA,
        ],
        compiler_params=pltpu.CompilerParams(collective_id=0, has_side_effects=True),
    )(send)


def spread_kernel(own_ref, out_ref, send_sem, recv_sem, local_sem, pair_send, pair_recv):
    count = lax.axis_size("alpha")
    rows, cols = own_ref.shape
    group = lax.axis_index("g")
    member = lax.axis_index("m")
    me = lax.axis_index("alpha")
    other = 1 - member

    def window(slot):
        return out_ref.at[pl.ds(slot * rows, rows), pl.ds(member * cols, cols)]

    def remote(slot, sem_slot, peer):
        return pltpu.make_async_remote_copy(
            src_ref=own_ref,
            dst_ref=window(slot),
            send_sem=send_sem.at[sem_slot],
            recv_sem=recv_sem.at[slot],
            device_id=(peer, group, member),
            device_id_type=pl.DeviceIdType.MESH,
        )

    for step in range(1, count):
        dest = lax.rem(me + step, count)
        remote(me, dest, dest).start()
    local = pltpu.make_async_copy(own_ref, window(me), local_sem)
    local.start()
    local.wait()
    for step in range(1, count):
        dest = lax.rem(me + step, count)
        remote(me, dest, dest).wait_send()
    for step in range(1, count):
        src = lax.rem(me + count - step, count)
        remote(src, src, src).wait_recv()

    def half(col):
        return out_ref.at[:, pl.ds(col * cols, cols)]

    def pair(col):
        return pltpu.make_async_remote_copy(
            src_ref=half(col),
            dst_ref=half(col),
            send_sem=pair_send,
            recv_sem=pair_recv,
            device_id=(me, group, other),
            device_id_type=pl.DeviceIdType.MESH,
        )

    pair(member).start()
    pair(member).wait_send()
    pair(other).wait_recv()


def spread(own, count):
    return pl.pallas_call(
        spread_kernel,
        out_shape=jax.ShapeDtypeStruct(
            (count // PAIR * own.shape[0], PAIR * own.shape[1]), own.dtype
        ),
        in_specs=[pl.BlockSpec(memory_space=pl.ANY)],
        out_specs=pl.BlockSpec(memory_space=pl.ANY),
        scratch_shapes=[
            pltpu.SemaphoreType.DMA((count // PAIR,)),
            pltpu.SemaphoreType.DMA((count // PAIR,)),
            pltpu.SemaphoreType.DMA,
            pltpu.SemaphoreType.DMA,
            pltpu.SemaphoreType.DMA,
        ],
        compiler_params=pltpu.CompilerParams(has_side_effects=True),
    )(own)


def gather_alpha_kernel(own_ref, out_ref, send_sem, recv_sem, local_sem):
    count = lax.axis_size("alpha")
    group = lax.axis_index("g")
    member = lax.axis_index("m")
    me = lax.axis_index("alpha")

    def remote(slot, sem_slot, peer):
        return pltpu.make_async_remote_copy(
            src_ref=own_ref,
            dst_ref=out_ref.at[slot],
            send_sem=send_sem.at[sem_slot],
            recv_sem=recv_sem.at[slot],
            device_id=(peer, group, member),
            device_id_type=pl.DeviceIdType.MESH,
        )

    barrier = pltpu.get_barrier_semaphore()
    for step in range(1, count):
        peer = lax.rem(me + step, count)
        pl.semaphore_signal(
            barrier, 1, device_id=(peer, group, member), device_id_type=pl.DeviceIdType.MESH
        )
    pl.semaphore_wait(barrier, count - 1)

    for step in range(1, count):
        dest = lax.rem(me + step, count)
        remote(me, dest, dest).start()
    local = pltpu.make_async_copy(own_ref, out_ref.at[me], local_sem)
    local.start()
    local.wait()
    for step in range(1, count):
        dest = lax.rem(me + step, count)
        remote(me, dest, dest).wait_send()
    for step in range(1, count):
        src = lax.rem(me + count - step, count)
        remote(src, src, src).wait_recv()


def gather_alpha(own, count):
    return pl.pallas_call(
        gather_alpha_kernel,
        out_shape=jax.ShapeDtypeStruct((count,) + own.shape, own.dtype),
        in_specs=[pl.BlockSpec(memory_space=pl.ANY)],
        out_specs=pl.BlockSpec(memory_space=pl.ANY),
        scratch_shapes=[
            pltpu.SemaphoreType.DMA((count,)),
            pltpu.SemaphoreType.DMA((count,)),
            pltpu.SemaphoreType.DMA,
        ],
        compiler_params=pltpu.CompilerParams(collective_id=1, has_side_effects=True),
    )(own)


def on_device(
    coefficients, diagonal, integrals, alpha_row, alpha_sign, beta_block, beta_sign, block_irrep
):
    alpha_rank = lax.axis_index("alpha")
    member = lax.axis_index("m")
    pair_count = integrals.shape[0]
    local_rows, local_cols = coefficients.shape
    block_len = beta_sign.shape[1] // pair_count
    per_device = local_rows // block_len
    src_blocks = local_cols // block_len
    total_blocks = lax.axis_size("g") * PAIR * src_blocks
    pairs = -(-pair_count // 16) * 16
    extra = pairs - pair_count
    sub_rows = block_len // PAIR

    alpha_size = lax.axis_size("alpha")
    gathered = spread(coefficients, alpha_size * PAIR)
    live_flags = (block_irrep == 0).astype(jnp.int32)
    live_rows = jnp.repeat(live_flags, block_len)
    gathered = gathered * live_rows[:, None].astype(jnp.bfloat16)
    window_rows, wide_cols = gathered.shape
    coeff_ext = jnp.concatenate(
        [gathered, -gathered, jnp.zeros((16, wide_cols), jnp.bfloat16)], axis=0
    )
    zero_row = 2 * window_rows

    integ_pad = jnp.pad(integrals, ((0, extra), (0, extra)))
    beta_block2 = lax.all_gather(beta_block.astype(jnp.bfloat16), "m", axis=0, tiled=True)
    beta_block2 = beta_block2.astype(jnp.int32)
    beta_sign2 = lax.all_gather(beta_sign.astype(jnp.bfloat16), "m", axis=0, tiled=True)
    sign_q = (
        beta_sign2.reshape(PAIR, src_blocks, pair_count, block_len)
        .transpose(0, 2, 1, 3)
        .reshape(PAIR, pair_count, local_cols)
    )
    sign_q = jnp.pad(sign_q, ((0, 0), (0, extra), (0, 0))).astype(jnp.bfloat16)
    target_iota = jnp.arange(total_blocks, dtype=jnp.int32)
    table_all = (target_iota[None, :, None] == beta_block2[:, None, :]).astype(jnp.bfloat16)
    table_all = jnp.pad(
        table_all.reshape(PAIR, src_blocks * total_blocks, pair_count),
        ((0, 0), (0, 0), (0, extra)),
    )

    own_flags = lax.dynamic_slice_in_dim(live_flags, alpha_rank * per_device, per_device, 0)

    dims = lax.GatherDimensionNumbers(
        offset_dims=(2,), collapsed_slice_dims=(0,), start_index_map=(0,)
    )

    block_count = live_flags.shape[0]
    block_iota = jnp.arange(block_count, dtype=jnp.int32)
    in_group = jnp.cumsum(live_flags.reshape(-1, per_device), axis=1).reshape(-1)
    is_first = (live_flags == 1) & (in_group == 1)
    is_extra = ((live_flags == 1) & jnp.logical_not(is_first)).astype(jnp.int32)
    extra_rank = jnp.cumsum(is_extra) - is_extra
    extra_total = jnp.sum(is_extra)
    block_of_extra = jnp.sum(
        jnp.where(
            (is_extra[None, :] == 1) & (extra_rank[None, :] == block_iota[:, None]),
            block_iota[None, :],
            0,
        ),
        axis=1,
    )
    own_first = lax.dynamic_slice_in_dim(is_first, alpha_rank * per_device, per_device, 0)
    first_blk = alpha_rank * per_device + jnp.argmax(own_first).astype(jnp.int32)
    my_count = 1 + jnp.maximum(extra_total - alpha_rank + alpha_size - 1, 0) // alpha_size
    beta_size = total_blocks // src_blocks

    def one_block(slot, buffer):
        block_id = jnp.where(
            slot == 0,
            first_blk,
            block_of_extra[jnp.maximum(slot - 1, 0) * alpha_size + alpha_rank],
        )
        first_row = block_id * block_len + member * sub_rows
        rows_src = lax.dynamic_slice_in_dim(alpha_row, first_row, sub_rows, 1)
        signs_src = lax.dynamic_slice_in_dim(alpha_sign, first_row, sub_rows, 1)
        row_ids = jnp.where(
            signs_src == 0,
            zero_row,
            jnp.where(signs_src < 0, rows_src + window_rows, rows_src),
        )
        row_ids = jnp.pad(row_ids, ((0, extra), (0, 0)), constant_values=zero_row).T
        picked = lax.gather(
            coeff_ext,
            row_ids[:, :, None],
            dims,
            slice_sizes=(1, wide_cols),
            mode=lax.GatherScatterMode.PROMISE_IN_BOUNDS,
        )
        summed = mix_block(integ_pad, picked, sign_q, table_all, total_blocks, block_len)
        part = summed.reshape(sub_rows, beta_size, local_cols).transpose(1, 0, 2)
        recv = exchange(part)
        groups = recv.shape[0] // PAIR
        rows = recv.reshape(groups, PAIR * sub_rows, local_cols).sum(axis=0)
        return lax.dynamic_update_slice(buffer, rows[None], (slot, 0, 0))

    empty = jnp.zeros((per_device, block_len, local_cols), jnp.float32)
    done = lax.fori_loop(0, my_count, one_block, empty)
    pushes = jnp.maximum(extra_total + alpha_size - 1, 0) // alpha_size

    def push(step, held):
        arrived = gather_alpha(done[step + 1], alpha_size)
        return lax.dynamic_update_slice(held, arrived[None], (step, 0, 0, 0))

    everyone = lax.fori_loop(
        0, pushes, push, jnp.zeros((per_device - 1, alpha_size, block_len, local_cols), jnp.float32)
    ).reshape((per_device - 1) * alpha_size, block_len, local_cols)
    own_rank = lax.dynamic_slice_in_dim(extra_rank, alpha_rank * per_device, per_device, 0)
    pick = jnp.minimum(own_rank // alpha_size, per_device - 2) * alpha_size + own_rank % alpha_size
    placed = jnp.where(own_first[:, None, None], done[0][None], everyone[pick])
    placed = placed.reshape(local_rows, local_cols)
    own_live_rows = jnp.repeat(own_flags, block_len)
    total = diagonal * coefficients.astype(jnp.float32) + placed
    return jnp.where(own_live_rows[:, None] == 1, total, jnp.zeros_like(total))


def solution(mesh):
    alpha_size, beta_size = mesh.devices.shape
    split_mesh = Mesh(
        mesh.devices.reshape(alpha_size, beta_size // PAIR, PAIR), ("alpha", "g", "m")
    )
    beta = ("g", "m")
    return jax.shard_map(
        on_device,
        mesh=split_mesh,
        in_specs=(
            P("alpha", beta),
            P("alpha", beta),
            P(),
            P(),
            P(),
            P(beta, None),
            P(beta, None),
            P(),
        ),
        out_specs=P("alpha", beta),
        check_vma=False,
    )
```

```python
import jax
import jax.numpy as jnp
from jax import lax
from jax.experimental import pallas as pl
from jax.experimental.pallas import tpu as pltpu
from jax.sharding import Mesh
from jax.sharding import PartitionSpec as P

ROWS = 8
PAIR = 2


def mix_kernel(integ_ref, picked_ref, sign_ref, table_ref, out_ref):
    halves, _, width = sign_ref.shape
    targets = out_ref.shape[1]
    block_len = out_ref.shape[2]
    src_blocks = width // block_len
    lane = lax.broadcasted_iota(jnp.int32, (targets, 2 * block_len), 1)
    upper = lane >= block_len
    integ = integ_ref[...]
    for row in range(picked_ref.shape[0]):
        mixed = jnp.dot(integ, picked_ref[row], preferred_element_type=jnp.float32)
        folded = jnp.zeros((targets, 2 * block_len), jnp.float32)
        for half in range(halves):
            weighted = mixed[:, half * width : (half + 1) * width] * sign_ref[half].astype(
                jnp.float32
            )
            high = weighted.astype(jnp.bfloat16)
            low = (weighted - high.astype(jnp.float32)).astype(jnp.bfloat16)
            stacked = jnp.concatenate([high, low], axis=0)
            res = jnp.dot(table_ref[half], stacked, preferred_element_type=jnp.float32)
            for s in range(src_blocks):
                lanes = (s // 2) * 2 * block_len
                piece = res[s * targets : (s + 1) * targets, lanes : lanes + 2 * block_len]
                keep = upper if s % 2 else jnp.logical_not(upper)
                folded = folded + jnp.where(keep, piece, 0.0)
        folded = folded + pltpu.roll(folded, block_len, 1)
        out_ref[row] = folded[:, :block_len]


def mix_block(integ_pad, picked, sign_q, table_all, targets, block_len):
    rows, pairs, width = picked.shape
    return pl.pallas_call(
        mix_kernel,
        out_shape=jax.ShapeDtypeStruct((rows, targets, block_len), jnp.float32),
        grid=(rows // ROWS,),
        in_specs=[
            pl.BlockSpec((pairs, pairs), lambda i: (0, 0)),
            pl.BlockSpec((ROWS, pairs, width), lambda i: (i, 0, 0)),
            pl.BlockSpec(sign_q.shape, lambda i: (0, 0, 0)),
            pl.BlockSpec(table_all.shape, lambda i: (0, 0, 0)),
        ],
        out_specs=pl.BlockSpec((ROWS, targets, block_len), lambda i: (i, 0, 0)),
        compiler_params=pltpu.CompilerParams(dimension_semantics=("arbitrary",)),
    )(integ_pad, picked, sign_q, table_all)


def exchange_kernel(send_ref, recv_ref, send_sem, recv_sem, local_sem):
    groups = lax.axis_size("g")
    count = groups * PAIR
    alpha = lax.axis_index("alpha")
    me = lax.axis_index("g") * PAIR + lax.axis_index("m")

    def remote(src_slot, dst_slot, sem_slot, peer):
        return pltpu.make_async_remote_copy(
            src_ref=send_ref.at[src_slot],
            dst_ref=recv_ref.at[dst_slot],
            send_sem=send_sem.at[sem_slot],
            recv_sem=recv_sem.at[dst_slot],
            device_id=(alpha, peer // PAIR, peer % PAIR),
            device_id_type=pl.DeviceIdType.MESH,
        )

    barrier = pltpu.get_barrier_semaphore()
    for step in range(1, count):
        peer = lax.rem(me + step, count)
        pl.semaphore_signal(
            barrier, 1, device_id=(alpha, peer // PAIR, peer % PAIR),
            device_id_type=pl.DeviceIdType.MESH,
        )
    pl.semaphore_wait(barrier, count - 1)

    for step in range(1, count):
        dest = lax.rem(me + step, count)
        remote(dest, me, dest, dest).start()
    local = pltpu.make_async_copy(send_ref.at[me], recv_ref.at[me], local_sem)
    local.start()
    local.wait()
    for step in range(1, count):
        dest = lax.rem(me + step, count)
        remote(dest, me, dest, dest).wait_send()
    for step in range(1, count):
        src = lax.rem(me + count - step, count)
        remote(src, src, src, src).wait_recv()


def exchange(send):
    count = send.shape[0]
    return pl.pallas_call(
        exchange_kernel,
        out_shape=jax.ShapeDtypeStruct(send.shape, send.dtype),
        in_specs=[pl.BlockSpec(memory_space=pl.ANY)],
        out_specs=pl.BlockSpec(memory_space=pl.ANY),
        scratch_shapes=[
            pltpu.SemaphoreType.DMA((count,)),
            pltpu.SemaphoreType.DMA((count,)),
            pltpu.SemaphoreType.DMA,
        ],
        compiler_params=pltpu.CompilerParams(collective_id=0, has_side_effects=True),
    )(send)


def spread_kernel(own_ref, out_ref, send_sem, recv_sem, local_sem, pair_send, pair_recv):
    count = lax.axis_size("alpha")
    rows, cols = own_ref.shape
    group = lax.axis_index("g")
    member = lax.axis_index("m")
    me = lax.axis_index("alpha")
    other = 1 - member

    def window(slot):
        return out_ref.at[pl.ds(slot * rows, rows), pl.ds(member * cols, cols)]

    def remote(slot, sem_slot, peer):
        return pltpu.make_async_remote_copy(
            src_ref=own_ref,
            dst_ref=window(slot),
            send_sem=send_sem.at[sem_slot],
            recv_sem=recv_sem.at[slot],
            device_id=(peer, group, member),
            device_id_type=pl.DeviceIdType.MESH,
        )

    for step in range(1, count):
        dest = lax.rem(me + step, count)
        remote(me, dest, dest).start()
    local = pltpu.make_async_copy(own_ref, window(me), local_sem)
    local.start()
    local.wait()
    for step in range(1, count):
        dest = lax.rem(me + step, count)
        remote(me, dest, dest).wait_send()
    for step in range(1, count):
        src = lax.rem(me + count - step, count)
        remote(src, src, src).wait_recv()

    def half(col):
        return out_ref.at[:, pl.ds(col * cols, cols)]

    def pair(col):
        return pltpu.make_async_remote_copy(
            src_ref=half(col),
            dst_ref=half(col),
            send_sem=pair_send,
            recv_sem=pair_recv,
            device_id=(me, group, other),
            device_id_type=pl.DeviceIdType.MESH,
        )

    pair(member).start()
    pair(member).wait_send()
    pair(other).wait_recv()


def spread(own, count):
    return pl.pallas_call(
        spread_kernel,
        out_shape=jax.ShapeDtypeStruct(
            (count // PAIR * own.shape[0], PAIR * own.shape[1]), own.dtype
        ),
        in_specs=[pl.BlockSpec(memory_space=pl.ANY)],
        out_specs=pl.BlockSpec(memory_space=pl.ANY),
        scratch_shapes=[
            pltpu.SemaphoreType.DMA((count // PAIR,)),
            pltpu.SemaphoreType.DMA((count // PAIR,)),
            pltpu.SemaphoreType.DMA,
            pltpu.SemaphoreType.DMA,
            pltpu.SemaphoreType.DMA,
        ],
        compiler_params=pltpu.CompilerParams(has_side_effects=True),
    )(own)


def gather_alpha_kernel(own_ref, out_ref, send_sem, recv_sem, local_sem):
    count = lax.axis_size("alpha")
    group = lax.axis_index("g")
    member = lax.axis_index("m")
    me = lax.axis_index("alpha")

    def remote(slot, sem_slot, peer):
        return pltpu.make_async_remote_copy(
            src_ref=own_ref,
            dst_ref=out_ref.at[slot],
            send_sem=send_sem.at[sem_slot],
            recv_sem=recv_sem.at[slot],
            device_id=(peer, group, member),
            device_id_type=pl.DeviceIdType.MESH,
        )

    barrier = pltpu.get_barrier_semaphore()
    for step in range(1, count):
        peer = lax.rem(me + step, count)
        pl.semaphore_signal(
            barrier, 1, device_id=(peer, group, member), device_id_type=pl.DeviceIdType.MESH
        )
    pl.semaphore_wait(barrier, count - 1)

    for step in range(1, count):
        dest = lax.rem(me + step, count)
        remote(me, dest, dest).start()
    local = pltpu.make_async_copy(own_ref, out_ref.at[me], local_sem)
    local.start()
    local.wait()
    for step in range(1, count):
        dest = lax.rem(me + step, count)
        remote(me, dest, dest).wait_send()
    for step in range(1, count):
        src = lax.rem(me + count - step, count)
        remote(src, src, src).wait_recv()


def gather_alpha(own, count):
    return pl.pallas_call(
        gather_alpha_kernel,
        out_shape=jax.ShapeDtypeStruct((count,) + own.shape, own.dtype),
        in_specs=[pl.BlockSpec(memory_space=pl.ANY)],
        out_specs=pl.BlockSpec(memory_space=pl.ANY),
        scratch_shapes=[
            pltpu.SemaphoreType.DMA((count,)),
            pltpu.SemaphoreType.DMA((count,)),
            pltpu.SemaphoreType.DMA,
        ],
        compiler_params=pltpu.CompilerParams(collective_id=1, has_side_effects=True),
    )(own)


def on_device(
    coefficients, diagonal, integrals, alpha_row, alpha_sign, beta_block, beta_sign, block_irrep
):
    alpha_rank = lax.axis_index("alpha")
    member = lax.axis_index("m")
    pair_count = integrals.shape[0]
    local_rows, local_cols = coefficients.shape
    block_len = beta_sign.shape[1] // pair_count
    per_device = local_rows // block_len
    src_blocks = local_cols // block_len
    total_blocks = lax.axis_size("g") * PAIR * src_blocks
    pairs = -(-pair_count // 16) * 16
    extra = pairs - pair_count
    sub_rows = block_len // PAIR

    alpha_size = lax.axis_size("alpha")
    gathered = spread(coefficients, alpha_size * PAIR)
    live_flags = (block_irrep == 0).astype(jnp.int32)
    live_rows = jnp.repeat(live_flags, block_len)
    gathered = gathered * live_rows[:, None].astype(jnp.bfloat16)
    window_rows, wide_cols = gathered.shape
    coeff_ext = jnp.concatenate(
        [gathered, -gathered, jnp.zeros((16, wide_cols), jnp.bfloat16)], axis=0
    )
    zero_row = 2 * window_rows

    integ_pad = jnp.pad(integrals, ((0, extra), (0, extra)))
    beta_block2 = lax.all_gather(beta_block.astype(jnp.bfloat16), "m", axis=0, tiled=True)
    beta_block2 = beta_block2.astype(jnp.int32)
    beta_sign2 = lax.all_gather(beta_sign.astype(jnp.bfloat16), "m", axis=0, tiled=True)
    sign_q = (
        beta_sign2.reshape(PAIR, src_blocks, pair_count, block_len)
        .transpose(0, 2, 1, 3)
        .reshape(PAIR, pair_count, local_cols)
    )
    sign_q = jnp.pad(sign_q, ((0, 0), (0, extra), (0, 0))).astype(jnp.bfloat16)
    target_iota = jnp.arange(total_blocks, dtype=jnp.int32)
    table_all = (target_iota[None, :, None] == beta_block2[:, None, :]).astype(jnp.bfloat16)
    table_all = jnp.pad(
        table_all.reshape(PAIR, src_blocks * total_blocks, pair_count),
        ((0, 0), (0, 0), (0, extra)),
    )
    table_all = jnp.concatenate([table_all, table_all], axis=2)

    own_flags = lax.dynamic_slice_in_dim(live_flags, alpha_rank * per_device, per_device, 0)

    dims = lax.GatherDimensionNumbers(
        offset_dims=(2,), collapsed_slice_dims=(0,), start_index_map=(0,)
    )

    block_count = live_flags.shape[0]
    block_iota = jnp.arange(block_count, dtype=jnp.int32)
    in_group = jnp.cumsum(live_flags.reshape(-1, per_device), axis=1).reshape(-1)
    is_first = (live_flags == 1) & (in_group == 1)
    is_extra = ((live_flags == 1) & jnp.logical_not(is_first)).astype(jnp.int32)
    extra_rank = jnp.cumsum(is_extra) - is_extra
    extra_total = jnp.sum(is_extra)
    block_of_extra = jnp.sum(
        jnp.where(
            (is_extra[None, :] == 1) & (extra_rank[None, :] == block_iota[:, None]),
            block_iota[None, :],
            0,
        ),
        axis=1,
    )
    own_first = lax.dynamic_slice_in_dim(is_first, alpha_rank * per_device, per_device, 0)
    first_blk = alpha_rank * per_device + jnp.argmax(own_first).astype(jnp.int32)
    my_count = 1 + jnp.maximum(extra_total - alpha_rank + alpha_size - 1, 0) // alpha_size
    beta_size = total_blocks // src_blocks

    def one_block(slot, buffer):
        block_id = jnp.where(
            slot == 0,
            first_blk,
            block_of_extra[jnp.maximum(slot - 1, 0) * alpha_size + alpha_rank],
        )
        first_row = block_id * block_len + member * sub_rows
        rows_src = lax.dynamic_slice_in_dim(alpha_row, first_row, sub_rows, 1)
        signs_src = lax.dynamic_slice_in_dim(alpha_sign, first_row, sub_rows, 1)
        row_ids = jnp.where(
            signs_src == 0,
            zero_row,
            jnp.where(signs_src < 0, rows_src + window_rows, rows_src),
        )
        row_ids = jnp.pad(row_ids, ((0, extra), (0, 0)), constant_values=zero_row).T
        picked = lax.gather(
            coeff_ext,
            row_ids[:, :, None],
            dims,
            slice_sizes=(1, wide_cols),
            mode=lax.GatherScatterMode.PROMISE_IN_BOUNDS,
        )
        summed = mix_block(integ_pad, picked, sign_q, table_all, total_blocks, block_len)
        part = summed.reshape(sub_rows, beta_size, local_cols).transpose(1, 0, 2)
        recv = exchange(part)
        groups = recv.shape[0] // PAIR
        rows = recv.reshape(groups, PAIR * sub_rows, local_cols).sum(axis=0)
        return lax.dynamic_update_slice(buffer, rows[None], (slot, 0, 0))

    empty = jnp.zeros((per_device, block_len, local_cols), jnp.float32)
    done = lax.fori_loop(0, my_count, one_block, empty)
    pushes = jnp.maximum(extra_total + alpha_size - 1, 0) // alpha_size

    def push(step, held):
        arrived = gather_alpha(done[step + 1], alpha_size)
        return lax.dynamic_update_slice(held, arrived[None], (step, 0, 0, 0))

    everyone = lax.fori_loop(
        0, pushes, push, jnp.zeros((per_device - 1, alpha_size, block_len, local_cols), jnp.float32)
    ).reshape((per_device - 1) * alpha_size, block_len, local_cols)
    own_rank = lax.dynamic_slice_in_dim(extra_rank, alpha_rank * per_device, per_device, 0)
    pick = jnp.minimum(own_rank // alpha_size, per_device - 2) * alpha_size + own_rank % alpha_size
    placed = jnp.where(own_first[:, None, None], done[0][None], everyone[pick])
    placed = placed.reshape(local_rows, local_cols)
    own_live_rows = jnp.repeat(own_flags, block_len)
    total = diagonal * coefficients.astype(jnp.float32) + placed
    return jnp.where(own_live_rows[:, None] == 1, total, jnp.zeros_like(total))


def solution(mesh):
    alpha_size, beta_size = mesh.devices.shape
    split_mesh = Mesh(
        mesh.devices.reshape(alpha_size, beta_size // PAIR, PAIR), ("alpha", "g", "m")
    )
    beta = ("g", "m")
    return jax.shard_map(
        on_device,
        mesh=split_mesh,
        in_specs=(
            P("alpha", beta),
            P("alpha", beta),
            P(),
            P(),
            P(),
            P(beta, None),
            P(beta, None),
            P(),
        ),
        out_specs=P("alpha", beta),
        check_vma=False,
    )
```

```python
import jax
import jax.numpy as jnp
from jax import lax
from jax.experimental import pallas as pl
from jax.experimental.pallas import tpu as pltpu
from jax.sharding import Mesh
from jax.sharding import PartitionSpec as P

ROWS = 8
PAIR = 2


def mix_kernel(integ_ref, picked_ref, sign_ref, table_ref, out_ref):
    halves, _, width = sign_ref.shape
    targets = out_ref.shape[1]
    block_len = out_ref.shape[2]
    src_blocks = width // block_len
    lane = lax.broadcasted_iota(jnp.int32, (targets, 2 * block_len), 1)
    upper = lane >= block_len
    integ = integ_ref[...]
    for row in range(picked_ref.shape[0]):
        mixed = jnp.dot(integ, picked_ref[row], preferred_element_type=jnp.float32)
        parts = []
        for half in range(halves):
            weighted = mixed[:, half * width : (half + 1) * width] * sign_ref[half].astype(
                jnp.float32
            )
            high = weighted.astype(jnp.bfloat16)
            low = (weighted - high.astype(jnp.float32)).astype(jnp.bfloat16)
            parts += [high, low]
        res = jnp.dot(
            table_ref[...], jnp.concatenate(parts, axis=0), preferred_element_type=jnp.float32
        )
        folded = jnp.zeros((targets, 2 * block_len), jnp.float32)
        for s in range(src_blocks):
            lanes = (s // 2) * 2 * block_len
            piece = res[s * targets : (s + 1) * targets, lanes : lanes + 2 * block_len]
            keep = upper if s % 2 else jnp.logical_not(upper)
            folded = folded + jnp.where(keep, piece, 0.0)
        folded = folded + pltpu.roll(folded, block_len, 1)
        out_ref[row] = folded[:, :block_len]


def mix_block(integ_pad, picked, sign_q, table_all, targets, block_len):
    rows, pairs, width = picked.shape
    return pl.pallas_call(
        mix_kernel,
        out_shape=jax.ShapeDtypeStruct((rows, targets, block_len), jnp.float32),
        grid=(rows // ROWS,),
        in_specs=[
            pl.BlockSpec((pairs, pairs), lambda i: (0, 0)),
            pl.BlockSpec((ROWS, pairs, width), lambda i: (i, 0, 0)),
            pl.BlockSpec(sign_q.shape, lambda i: (0, 0, 0)),
            pl.BlockSpec(table_all.shape, lambda i: (0, 0)),
        ],
        out_specs=pl.BlockSpec((ROWS, targets, block_len), lambda i: (i, 0, 0)),
        compiler_params=pltpu.CompilerParams(dimension_semantics=("arbitrary",)),
    )(integ_pad, picked, sign_q, table_all)


def exchange_kernel(send_ref, recv_ref, send_sem, recv_sem, local_sem):
    groups = lax.axis_size("g")
    count = groups * PAIR
    alpha = lax.axis_index("alpha")
    me = lax.axis_index("g") * PAIR + lax.axis_index("m")

    def remote(src_slot, dst_slot, sem_slot, peer):
        return pltpu.make_async_remote_copy(
            src_ref=send_ref.at[src_slot],
            dst_ref=recv_ref.at[dst_slot],
            send_sem=send_sem.at[sem_slot],
            recv_sem=recv_sem.at[dst_slot],
            device_id=(alpha, peer // PAIR, peer % PAIR),
            device_id_type=pl.DeviceIdType.MESH,
        )

    barrier = pltpu.get_barrier_semaphore()
    for step in range(1, count):
        peer = lax.rem(me + step, count)
        pl.semaphore_signal(
            barrier, 1, device_id=(alpha, peer // PAIR, peer % PAIR),
            device_id_type=pl.DeviceIdType.MESH,
        )
    pl.semaphore_wait(barrier, count - 1)

    for step in range(1, count):
        dest = lax.rem(me + step, count)
        remote(dest, me, dest, dest).start()
    local = pltpu.make_async_copy(send_ref.at[me], recv_ref.at[me], local_sem)
    local.start()
    local.wait()
    for step in range(1, count):
        dest = lax.rem(me + step, count)
        remote(dest, me, dest, dest).wait_send()
    for step in range(1, count):
        src = lax.rem(me + count - step, count)
        remote(src, src, src, src).wait_recv()


def exchange(send):
    count = send.shape[0]
    return pl.pallas_call(
        exchange_kernel,
        out_shape=jax.ShapeDtypeStruct(send.shape, send.dtype),
        in_specs=[pl.BlockSpec(memory_space=pl.ANY)],
        out_specs=pl.BlockSpec(memory_space=pl.ANY),
        scratch_shapes=[
            pltpu.SemaphoreType.DMA((count,)),
            pltpu.SemaphoreType.DMA((count,)),
            pltpu.SemaphoreType.DMA,
        ],
        compiler_params=pltpu.CompilerParams(collective_id=0, has_side_effects=True),
    )(send)


def spread_kernel(own_ref, out_ref, send_sem, recv_sem, local_sem, pair_send, pair_recv):
    count = lax.axis_size("alpha")
    rows, cols = own_ref.shape
    group = lax.axis_index("g")
    member = lax.axis_index("m")
    me = lax.axis_index("alpha")
    other = 1 - member

    def window(slot):
        return out_ref.at[pl.ds(slot * rows, rows), pl.ds(member * cols, cols)]

    def remote(slot, sem_slot, peer):
        return pltpu.make_async_remote_copy(
            src_ref=own_ref,
            dst_ref=window(slot),
            send_sem=send_sem.at[sem_slot],
            recv_sem=recv_sem.at[slot],
            device_id=(peer, group, member),
            device_id_type=pl.DeviceIdType.MESH,
        )

    for step in range(1, count):
        dest = lax.rem(me + step, count)
        remote(me, dest, dest).start()
    local = pltpu.make_async_copy(own_ref, window(me), local_sem)
    local.start()
    local.wait()
    for step in range(1, count):
        dest = lax.rem(me + step, count)
        remote(me, dest, dest).wait_send()
    for step in range(1, count):
        src = lax.rem(me + count - step, count)
        remote(src, src, src).wait_recv()

    def half(col):
        return out_ref.at[:, pl.ds(col * cols, cols)]

    def pair(col):
        return pltpu.make_async_remote_copy(
            src_ref=half(col),
            dst_ref=half(col),
            send_sem=pair_send,
            recv_sem=pair_recv,
            device_id=(me, group, other),
            device_id_type=pl.DeviceIdType.MESH,
        )

    pair(member).start()
    pair(member).wait_send()
    pair(other).wait_recv()


def spread(own, count):
    return pl.pallas_call(
        spread_kernel,
        out_shape=jax.ShapeDtypeStruct(
            (count // PAIR * own.shape[0], PAIR * own.shape[1]), own.dtype
        ),
        in_specs=[pl.BlockSpec(memory_space=pl.ANY)],
        out_specs=pl.BlockSpec(memory_space=pl.ANY),
        scratch_shapes=[
            pltpu.SemaphoreType.DMA((count // PAIR,)),
            pltpu.SemaphoreType.DMA((count // PAIR,)),
            pltpu.SemaphoreType.DMA,
            pltpu.SemaphoreType.DMA,
            pltpu.SemaphoreType.DMA,
        ],
        compiler_params=pltpu.CompilerParams(has_side_effects=True),
    )(own)


def gather_alpha_kernel(own_ref, out_ref, send_sem, recv_sem, local_sem):
    count = lax.axis_size("alpha")
    group = lax.axis_index("g")
    member = lax.axis_index("m")
    me = lax.axis_index("alpha")

    def remote(slot, sem_slot, peer):
        return pltpu.make_async_remote_copy(
            src_ref=own_ref,
            dst_ref=out_ref.at[slot],
            send_sem=send_sem.at[sem_slot],
            recv_sem=recv_sem.at[slot],
            device_id=(peer, group, member),
            device_id_type=pl.DeviceIdType.MESH,
        )

    barrier = pltpu.get_barrier_semaphore()
    for step in range(1, count):
        peer = lax.rem(me + step, count)
        pl.semaphore_signal(
            barrier, 1, device_id=(peer, group, member), device_id_type=pl.DeviceIdType.MESH
        )
    pl.semaphore_wait(barrier, count - 1)

    for step in range(1, count):
        dest = lax.rem(me + step, count)
        remote(me, dest, dest).start()
    local = pltpu.make_async_copy(own_ref, out_ref.at[me], local_sem)
    local.start()
    local.wait()
    for step in range(1, count):
        dest = lax.rem(me + step, count)
        remote(me, dest, dest).wait_send()
    for step in range(1, count):
        src = lax.rem(me + count - step, count)
        remote(src, src, src).wait_recv()


def gather_alpha(own, count):
    return pl.pallas_call(
        gather_alpha_kernel,
        out_shape=jax.ShapeDtypeStruct((count,) + own.shape, own.dtype),
        in_specs=[pl.BlockSpec(memory_space=pl.ANY)],
        out_specs=pl.BlockSpec(memory_space=pl.ANY),
        scratch_shapes=[
            pltpu.SemaphoreType.DMA((count,)),
            pltpu.SemaphoreType.DMA((count,)),
            pltpu.SemaphoreType.DMA,
        ],
        compiler_params=pltpu.CompilerParams(collective_id=1, has_side_effects=True),
    )(own)


def on_device(
    coefficients, diagonal, integrals, alpha_row, alpha_sign, beta_block, beta_sign, block_irrep
):
    alpha_rank = lax.axis_index("alpha")
    member = lax.axis_index("m")
    pair_count = integrals.shape[0]
    local_rows, local_cols = coefficients.shape
    block_len = beta_sign.shape[1] // pair_count
    per_device = local_rows // block_len
    src_blocks = local_cols // block_len
    total_blocks = lax.axis_size("g") * PAIR * src_blocks
    pairs = -(-pair_count // 16) * 16
    extra = pairs - pair_count
    sub_rows = block_len // PAIR

    alpha_size = lax.axis_size("alpha")
    gathered = spread(coefficients, alpha_size * PAIR)
    live_flags = (block_irrep == 0).astype(jnp.int32)
    live_rows = jnp.repeat(live_flags, block_len)
    gathered = gathered * live_rows[:, None].astype(jnp.bfloat16)
    window_rows, wide_cols = gathered.shape
    coeff_ext = jnp.concatenate(
        [gathered, -gathered, jnp.zeros((16, wide_cols), jnp.bfloat16)], axis=0
    )
    zero_row = 2 * window_rows

    integ_pad = jnp.pad(integrals, ((0, extra), (0, extra)))
    beta_block2 = lax.all_gather(beta_block.astype(jnp.bfloat16), "m", axis=0, tiled=True)
    beta_block2 = beta_block2.astype(jnp.int32)
    beta_sign2 = lax.all_gather(beta_sign.astype(jnp.bfloat16), "m", axis=0, tiled=True)
    sign_q = (
        beta_sign2.reshape(PAIR, src_blocks, pair_count, block_len)
        .transpose(0, 2, 1, 3)
        .reshape(PAIR, pair_count, local_cols)
    )
    sign_q = jnp.pad(sign_q, ((0, 0), (0, extra), (0, 0))).astype(jnp.bfloat16)
    target_iota = jnp.arange(total_blocks, dtype=jnp.int32)
    table_all = (target_iota[None, :, None] == beta_block2[:, None, :]).astype(jnp.bfloat16)
    table_all = jnp.pad(
        table_all.reshape(PAIR, src_blocks * total_blocks, pair_count),
        ((0, 0), (0, 0), (0, extra)),
    )
    table_all = jnp.concatenate([table_all[h] for h in range(PAIR) for _ in range(2)], axis=1)

    own_flags = lax.dynamic_slice_in_dim(live_flags, alpha_rank * per_device, per_device, 0)

    dims = lax.GatherDimensionNumbers(
        offset_dims=(2,), collapsed_slice_dims=(0,), start_index_map=(0,)
    )

    block_count = live_flags.shape[0]
    block_iota = jnp.arange(block_count, dtype=jnp.int32)
    in_group = jnp.cumsum(live_flags.reshape(-1, per_device), axis=1).reshape(-1)
    is_first = (live_flags == 1) & (in_group == 1)
    is_extra = ((live_flags == 1) & jnp.logical_not(is_first)).astype(jnp.int32)
    extra_rank = jnp.cumsum(is_extra) - is_extra
    extra_total = jnp.sum(is_extra)
    block_of_extra = jnp.sum(
        jnp.where(
            (is_extra[None, :] == 1) & (extra_rank[None, :] == block_iota[:, None]),
            block_iota[None, :],
            0,
        ),
        axis=1,
    )
    own_first = lax.dynamic_slice_in_dim(is_first, alpha_rank * per_device, per_device, 0)
    first_blk = alpha_rank * per_device + jnp.argmax(own_first).astype(jnp.int32)
    my_count = 1 + jnp.maximum(extra_total - alpha_rank + alpha_size - 1, 0) // alpha_size
    beta_size = total_blocks // src_blocks

    def one_block(slot, buffer):
        block_id = jnp.where(
            slot == 0,
            first_blk,
            block_of_extra[jnp.maximum(slot - 1, 0) * alpha_size + alpha_rank],
        )
        first_row = block_id * block_len + member * sub_rows
        rows_src = lax.dynamic_slice_in_dim(alpha_row, first_row, sub_rows, 1)
        signs_src = lax.dynamic_slice_in_dim(alpha_sign, first_row, sub_rows, 1)
        row_ids = jnp.where(
            signs_src == 0,
            zero_row,
            jnp.where(signs_src < 0, rows_src + window_rows, rows_src),
        )
        row_ids = jnp.pad(row_ids, ((0, extra), (0, 0)), constant_values=zero_row).T
        picked = lax.gather(
            coeff_ext,
            row_ids[:, :, None],
            dims,
            slice_sizes=(1, wide_cols),
            mode=lax.GatherScatterMode.PROMISE_IN_BOUNDS,
        )
        summed = mix_block(integ_pad, picked, sign_q, table_all, total_blocks, block_len)
        part = summed.reshape(sub_rows, beta_size, local_cols).transpose(1, 0, 2)
        recv = exchange(part)
        groups = recv.shape[0] // PAIR
        rows = recv.reshape(groups, PAIR * sub_rows, local_cols).sum(axis=0)
        return lax.dynamic_update_slice(buffer, rows[None], (slot, 0, 0))

    empty = jnp.zeros((per_device, block_len, local_cols), jnp.float32)
    done = lax.fori_loop(0, my_count, one_block, empty)
    pushes = jnp.maximum(extra_total + alpha_size - 1, 0) // alpha_size

    def push(step, held):
        arrived = gather_alpha(done[step + 1], alpha_size)
        return lax.dynamic_update_slice(held, arrived[None], (step, 0, 0, 0))

    everyone = lax.fori_loop(
        0, pushes, push, jnp.zeros((per_device - 1, alpha_size, block_len, local_cols), jnp.float32)
    ).reshape((per_device - 1) * alpha_size, block_len, local_cols)
    own_rank = lax.dynamic_slice_in_dim(extra_rank, alpha_rank * per_device, per_device, 0)
    pick = jnp.minimum(own_rank // alpha_size, per_device - 2) * alpha_size + own_rank % alpha_size
    placed = jnp.where(own_first[:, None, None], done[0][None], everyone[pick])
    placed = placed.reshape(local_rows, local_cols)
    own_live_rows = jnp.repeat(own_flags, block_len)
    total = diagonal * coefficients.astype(jnp.float32) + placed
    return jnp.where(own_live_rows[:, None] == 1, total, jnp.zeros_like(total))


def solution(mesh):
    alpha_size, beta_size = mesh.devices.shape
    split_mesh = Mesh(
        mesh.devices.reshape(alpha_size, beta_size // PAIR, PAIR), ("alpha", "g", "m")
    )
    beta = ("g", "m")
    return jax.shard_map(
        on_device,
        mesh=split_mesh,
        in_specs=(
            P("alpha", beta),
            P("alpha", beta),
            P(),
            P(),
            P(),
            P(beta, None),
            P(beta, None),
            P(),
        ),
        out_specs=P("alpha", beta),
        check_vma=False,
    )
```

```python
import jax
import jax.numpy as jnp
from jax import lax
from jax.experimental import pallas as pl
from jax.experimental.pallas import tpu as pltpu
from jax.sharding import Mesh
from jax.sharding import PartitionSpec as P

ROWS = 8
PAIR = 2


def mix_kernel(integ_ref, picked_ref, sign_ref, table_ref, out_ref):
    halves, _, width = sign_ref.shape
    targets = out_ref.shape[1]
    block_len = out_ref.shape[2]
    src_blocks = width // block_len
    lane = lax.broadcasted_iota(jnp.int32, (targets, 2 * block_len), 1)
    upper = lane >= block_len
    integ = integ_ref[...]
    for row in range(picked_ref.shape[0]):
        mixed = jnp.dot(integ, picked_ref[row], preferred_element_type=jnp.float32)
        parts = []
        for half in range(halves):
            weighted = mixed[:, half * width : (half + 1) * width] * sign_ref[half].astype(
                jnp.float32
            )
            high = weighted.astype(jnp.bfloat16)
            low = (weighted - high.astype(jnp.float32)).astype(jnp.bfloat16)
            parts += [high, low]
        res = jnp.dot(
            table_ref[...], jnp.concatenate(parts, axis=0), preferred_element_type=jnp.float32
        )
        folded = jnp.zeros((targets, 2 * block_len), jnp.float32)
        for s in range(src_blocks):
            lanes = (s // 2) * 2 * block_len
            piece = res[s * targets : (s + 1) * targets, lanes : lanes + 2 * block_len]
            keep = upper if s % 2 else jnp.logical_not(upper)
            folded = folded + jnp.where(keep, piece, 0.0)
        folded = folded + pltpu.roll(folded, block_len, 1)
        out_ref[row] = folded[:, :block_len]


def mix_block(integ_pad, picked, sign_q, table_all, targets, block_len):
    rows, pairs, width = picked.shape
    return pl.pallas_call(
        mix_kernel,
        out_shape=jax.ShapeDtypeStruct((rows, targets, block_len), jnp.float32),
        grid=(rows // ROWS,),
        in_specs=[
            pl.BlockSpec((pairs, pairs), lambda i: (0, 0)),
            pl.BlockSpec((ROWS, pairs, width), lambda i: (i, 0, 0)),
            pl.BlockSpec(sign_q.shape, lambda i: (0, 0, 0)),
            pl.BlockSpec(table_all.shape, lambda i: (0, 0)),
        ],
        out_specs=pl.BlockSpec((ROWS, targets, block_len), lambda i: (i, 0, 0)),
        compiler_params=pltpu.CompilerParams(dimension_semantics=("arbitrary",)),
    )(integ_pad, picked, sign_q, table_all)


def exchange_kernel(send_ref, recv_ref, send_sem, recv_sem, local_sem):
    groups = lax.axis_size("g")
    count = groups * PAIR
    alpha = lax.axis_index("alpha")
    me = lax.axis_index("g") * PAIR + lax.axis_index("m")

    def remote(src_slot, dst_slot, sem_slot, peer):
        return pltpu.make_async_remote_copy(
            src_ref=send_ref.at[src_slot],
            dst_ref=recv_ref.at[dst_slot],
            send_sem=send_sem.at[sem_slot],
            recv_sem=recv_sem.at[dst_slot],
            device_id=(alpha, peer // PAIR, peer % PAIR),
            device_id_type=pl.DeviceIdType.MESH,
        )

    barrier = pltpu.get_barrier_semaphore()
    for step in range(1, count):
        peer = lax.rem(me + step, count)
        pl.semaphore_signal(
            barrier, 1, device_id=(alpha, peer // PAIR, peer % PAIR),
            device_id_type=pl.DeviceIdType.MESH,
        )
    pl.semaphore_wait(barrier, count - 1)

    for step in range(1, count):
        dest = lax.rem(me + step, count)
        remote(dest, me, dest, dest).start()
    local = pltpu.make_async_copy(send_ref.at[me], recv_ref.at[me], local_sem)
    local.start()
    local.wait()
    for step in range(1, count):
        dest = lax.rem(me + step, count)
        remote(dest, me, dest, dest).wait_send()
    for step in range(1, count):
        src = lax.rem(me + count - step, count)
        remote(src, src, src, src).wait_recv()


def exchange(send):
    count = send.shape[0]
    return pl.pallas_call(
        exchange_kernel,
        out_shape=jax.ShapeDtypeStruct(send.shape, send.dtype),
        in_specs=[pl.BlockSpec(memory_space=pl.ANY)],
        out_specs=pl.BlockSpec(memory_space=pl.ANY),
        scratch_shapes=[
            pltpu.SemaphoreType.DMA((count,)),
            pltpu.SemaphoreType.DMA((count,)),
            pltpu.SemaphoreType.DMA,
        ],
        compiler_params=pltpu.CompilerParams(collective_id=0, has_side_effects=True),
    )(send)


def spread_kernel(own_ref, out_ref, send_sem, recv_sem, local_sem, pair_send, pair_recv):
    count = lax.axis_size("alpha")
    rows, cols = own_ref.shape
    group = lax.axis_index("g")
    member = lax.axis_index("m")
    me = lax.axis_index("alpha")
    other = 1 - member

    def window(slot):
        return out_ref.at[pl.ds(slot * rows, rows), pl.ds(member * cols, cols)]

    def remote(slot, sem_slot, peer):
        return pltpu.make_async_remote_copy(
            src_ref=own_ref,
            dst_ref=window(slot),
            send_sem=send_sem.at[sem_slot],
            recv_sem=recv_sem.at[slot],
            device_id=(peer, group, member),
            device_id_type=pl.DeviceIdType.MESH,
        )

    for step in range(1, count):
        dest = lax.rem(me + step, count)
        remote(me, dest, dest).start()
    local = pltpu.make_async_copy(own_ref, window(me), local_sem)
    local.start()
    local.wait()
    for step in range(1, count):
        dest = lax.rem(me + step, count)
        remote(me, dest, dest).wait_send()
    for step in range(1, count):
        src = lax.rem(me + count - step, count)
        remote(src, src, src).wait_recv()

    def half(col):
        return out_ref.at[:, pl.ds(col * cols, cols)]

    def pair(col):
        return pltpu.make_async_remote_copy(
            src_ref=half(col),
            dst_ref=half(col),
            send_sem=pair_send,
            recv_sem=pair_recv,
            device_id=(me, group, other),
            device_id_type=pl.DeviceIdType.MESH,
        )

    pair(member).start()
    pair(member).wait_send()
    pair(other).wait_recv()


def spread(own, count):
    return pl.pallas_call(
        spread_kernel,
        out_shape=jax.ShapeDtypeStruct(
            (count // PAIR * own.shape[0], PAIR * own.shape[1]), own.dtype
        ),
        in_specs=[pl.BlockSpec(memory_space=pl.ANY)],
        out_specs=pl.BlockSpec(memory_space=pl.ANY),
        scratch_shapes=[
            pltpu.SemaphoreType.DMA((count // PAIR,)),
            pltpu.SemaphoreType.DMA((count // PAIR,)),
            pltpu.SemaphoreType.DMA,
            pltpu.SemaphoreType.DMA,
            pltpu.SemaphoreType.DMA,
        ],
        compiler_params=pltpu.CompilerParams(has_side_effects=True),
    )(own)


def gather_alpha_kernel(own_ref, out_ref, send_sem, recv_sem, local_sem):
    count = lax.axis_size("alpha")
    group = lax.axis_index("g")
    member = lax.axis_index("m")
    me = lax.axis_index("alpha")

    def remote(slot, sem_slot, peer):
        return pltpu.make_async_remote_copy(
            src_ref=own_ref,
            dst_ref=out_ref.at[slot],
            send_sem=send_sem.at[sem_slot],
            recv_sem=recv_sem.at[slot],
            device_id=(peer, group, member),
            device_id_type=pl.DeviceIdType.MESH,
        )

    barrier = pltpu.get_barrier_semaphore()
    for step in range(1, count):
        peer = lax.rem(me + step, count)
        pl.semaphore_signal(
            barrier, 1, device_id=(peer, group, member), device_id_type=pl.DeviceIdType.MESH
        )
    pl.semaphore_wait(barrier, count - 1)

    for step in range(1, count):
        dest = lax.rem(me + step, count)
        remote(me, dest, dest).start()
    local = pltpu.make_async_copy(own_ref, out_ref.at[me], local_sem)
    local.start()
    local.wait()
    for step in range(1, count):
        dest = lax.rem(me + step, count)
        remote(me, dest, dest).wait_send()
    for step in range(1, count):
        src = lax.rem(me + count - step, count)
        remote(src, src, src).wait_recv()


def gather_alpha(own, count):
    return pl.pallas_call(
        gather_alpha_kernel,
        out_shape=jax.ShapeDtypeStruct((count,) + own.shape, own.dtype),
        in_specs=[pl.BlockSpec(memory_space=pl.ANY)],
        out_specs=pl.BlockSpec(memory_space=pl.ANY),
        scratch_shapes=[
            pltpu.SemaphoreType.DMA((count,)),
            pltpu.SemaphoreType.DMA((count,)),
            pltpu.SemaphoreType.DMA,
        ],
        compiler_params=pltpu.CompilerParams(collective_id=1, has_side_effects=True),
    )(own)


def on_device(
    coefficients, diagonal, integrals, alpha_row, alpha_sign, beta_block, beta_sign, block_irrep
):
    alpha_rank = lax.axis_index("alpha")
    member = lax.axis_index("m")
    pair_count = integrals.shape[0]
    local_rows, local_cols = coefficients.shape
    block_len = beta_sign.shape[1] // pair_count
    per_device = local_rows // block_len
    src_blocks = local_cols // block_len
    total_blocks = lax.axis_size("g") * PAIR * src_blocks
    pairs = -(-pair_count // 16) * 16
    extra = pairs - pair_count
    sub_rows = block_len // PAIR

    alpha_size = lax.axis_size("alpha")
    gathered = spread(coefficients, alpha_size * PAIR)
    live_flags = (block_irrep == 0).astype(jnp.int32)
    live_rows = jnp.repeat(live_flags, block_len)
    gathered = gathered * live_rows[:, None].astype(jnp.bfloat16)
    window_rows, wide_cols = gathered.shape
    coeff_ext = jnp.concatenate(
        [gathered, -gathered, jnp.zeros((16, wide_cols), jnp.bfloat16)], axis=0
    )
    zero_row = 2 * window_rows

    integ_pad = jnp.pad(integrals, ((0, extra), (0, extra)))
    beta_block2 = lax.all_gather(beta_block.astype(jnp.bfloat16), "m", axis=0, tiled=True)
    beta_block2 = beta_block2.astype(jnp.int32)
    beta_sign2 = lax.all_gather(beta_sign.astype(jnp.bfloat16), "m", axis=0, tiled=True)
    sign_q = (
        beta_sign2.reshape(PAIR, src_blocks, pair_count, block_len)
        .transpose(0, 2, 1, 3)
        .reshape(PAIR, pair_count, local_cols)
    )
    sign_q = jnp.pad(sign_q, ((0, 0), (0, extra), (0, 0))).astype(jnp.bfloat16)
    target_iota = jnp.arange(total_blocks, dtype=jnp.int32)
    table_all = (target_iota[None, :, None] == beta_block2[:, None, :]).astype(jnp.bfloat16)
    table_all = jnp.pad(
        table_all.reshape(PAIR, src_blocks * total_blocks, pair_count),
        ((0, 0), (0, 0), (0, extra)),
    )
    table_all = jnp.concatenate([table_all[h] for h in range(PAIR) for _ in range(2)], axis=1)

    own_flags = lax.dynamic_slice_in_dim(live_flags, alpha_rank * per_device, per_device, 0)

    dims = lax.GatherDimensionNumbers(
        offset_dims=(2,), collapsed_slice_dims=(0,), start_index_map=(0,)
    )

    block_count = live_flags.shape[0]
    block_iota = jnp.arange(block_count, dtype=jnp.int32)
    in_group = jnp.cumsum(live_flags.reshape(-1, per_device), axis=1).reshape(-1)
    is_first = (live_flags == 1) & (in_group == 1)
    is_extra = ((live_flags == 1) & jnp.logical_not(is_first)).astype(jnp.int32)
    extra_rank = jnp.cumsum(is_extra) - is_extra
    extra_total = jnp.sum(is_extra)
    block_of_extra = jnp.sum(
        jnp.where(
            (is_extra[None, :] == 1) & (extra_rank[None, :] == block_iota[:, None]),
            block_iota[None, :],
            0,
        ),
        axis=1,
    )
    own_first = lax.dynamic_slice_in_dim(is_first, alpha_rank * per_device, per_device, 0)
    first_blk = alpha_rank * per_device + jnp.argmax(own_first).astype(jnp.int32)
    my_count = 1 + jnp.maximum(extra_total - alpha_rank + alpha_size - 1, 0) // alpha_size
    beta_size = total_blocks // src_blocks

    def one_block(slot, buffer):
        block_id = jnp.where(
            slot == 0,
            first_blk,
            block_of_extra[jnp.maximum(slot - 1, 0) * alpha_size + alpha_rank],
        )
        first_row = block_id * block_len + member * sub_rows
        rows_src = lax.dynamic_slice_in_dim(alpha_row, first_row, sub_rows, 1)
        signs_src = lax.dynamic_slice_in_dim(alpha_sign, first_row, sub_rows, 1)
        row_ids = jnp.where(
            signs_src == 0,
            zero_row,
            jnp.where(signs_src < 0, rows_src + window_rows, rows_src),
        )
        row_ids = jnp.pad(row_ids, ((0, extra), (0, 0)), constant_values=zero_row).T
        picked = lax.gather(
            coeff_ext,
            row_ids[:, :, None],
            dims,
            slice_sizes=(1, wide_cols),
            mode=lax.GatherScatterMode.PROMISE_IN_BOUNDS,
        )
        summed = mix_block(integ_pad, picked, sign_q, table_all, total_blocks, block_len)
        part = summed.reshape(sub_rows, beta_size, local_cols).transpose(1, 0, 2)
        recv = exchange(part)
        groups = recv.shape[0] // PAIR
        rows = recv.reshape(groups, PAIR * sub_rows, local_cols).sum(axis=0)
        return lax.dynamic_update_slice(buffer, rows[None], (slot, 0, 0))

    empty = jnp.zeros((per_device, block_len, local_cols), jnp.float32)
    done = lax.fori_loop(0, my_count, one_block, empty)
    pushes = jnp.maximum(extra_total + alpha_size - 1, 0) // alpha_size

    def push(step, held):
        arrived = gather_alpha(done[step + 1], alpha_size)
        return lax.dynamic_update_slice(held, arrived[None], (step, 0, 0, 0))

    everyone = lax.fori_loop(
        0, pushes, push, jnp.zeros((per_device - 1, alpha_size, block_len, local_cols), jnp.float32)
    ).reshape((per_device - 1) * alpha_size, block_len, local_cols)
    own_rank = lax.dynamic_slice_in_dim(extra_rank, alpha_rank * per_device, per_device, 0)
    pick = jnp.minimum(own_rank // alpha_size, per_device - 2) * alpha_size + own_rank % alpha_size
    chosen = jnp.stack(
        [lax.dynamic_index_in_dim(everyone, pick[b], 0, keepdims=False) for b in range(per_device)]
    )
    placed = jnp.where(own_first[:, None, None], done[0][None], chosen)
    placed = placed.reshape(local_rows, local_cols)
    own_live_rows = jnp.repeat(own_flags, block_len)
    total = diagonal * coefficients.astype(jnp.float32) + placed
    return jnp.where(own_live_rows[:, None] == 1, total, jnp.zeros_like(total))


def solution(mesh):
    alpha_size, beta_size = mesh.devices.shape
    split_mesh = Mesh(
        mesh.devices.reshape(alpha_size, beta_size // PAIR, PAIR), ("alpha", "g", "m")
    )
    beta = ("g", "m")
    return jax.shard_map(
        on_device,
        mesh=split_mesh,
        in_specs=(
            P("alpha", beta),
            P("alpha", beta),
            P(),
            P(),
            P(),
            P(beta, None),
            P(beta, None),
            P(),
        ),
        out_specs=P("alpha", beta),
        check_vma=False,
    )
```

```python
import jax
import jax.numpy as jnp
from jax import lax
from jax.experimental import pallas as pl
from jax.experimental.pallas import tpu as pltpu
from jax.sharding import Mesh
from jax.sharding import PartitionSpec as P

ROWS = 8
PAIR = 2


def mix_kernel(integ_ref, picked_ref, sign_ref, table_ref, out_ref):
    halves, _, width = sign_ref.shape
    targets = out_ref.shape[1]
    block_len = out_ref.shape[2]
    src_blocks = width // block_len
    lane = lax.broadcasted_iota(jnp.int32, (targets, 2 * block_len), 1)
    upper = lane >= block_len
    integ = integ_ref[...]
    for row in range(picked_ref.shape[0]):
        mixed = jnp.dot(integ, picked_ref[row], preferred_element_type=jnp.float32)
        parts = []
        for half in range(halves):
            weighted = mixed[:, half * width : (half + 1) * width] * sign_ref[half].astype(
                jnp.float32
            )
            high = weighted.astype(jnp.bfloat16)
            low = (weighted - high.astype(jnp.float32)).astype(jnp.bfloat16)
            parts += [high, low]
        res = jnp.dot(
            table_ref[...], jnp.concatenate(parts, axis=0), preferred_element_type=jnp.float32
        )
        folded = jnp.zeros((targets, 2 * block_len), jnp.float32)
        for s in range(src_blocks):
            lanes = (s // 2) * 2 * block_len
            piece = res[s * targets : (s + 1) * targets, lanes : lanes + 2 * block_len]
            keep = upper if s % 2 else jnp.logical_not(upper)
            folded = folded + jnp.where(keep, piece, 0.0)
        folded = folded + pltpu.roll(folded, block_len, 1)
        out_ref[row] = folded[:, :block_len]


def mix_block(integ_pad, picked, sign_q, table_all, targets, block_len):
    rows, pairs, width = picked.shape
    return pl.pallas_call(
        mix_kernel,
        out_shape=jax.ShapeDtypeStruct((rows, targets, block_len), jnp.float32),
        grid=(rows // ROWS,),
        in_specs=[
            pl.BlockSpec((pairs, pairs), lambda i: (0, 0)),
            pl.BlockSpec((ROWS, pairs, width), lambda i: (i, 0, 0)),
            pl.BlockSpec(sign_q.shape, lambda i: (0, 0, 0)),
            pl.BlockSpec(table_all.shape, lambda i: (0, 0)),
        ],
        out_specs=pl.BlockSpec((ROWS, targets, block_len), lambda i: (i, 0, 0)),
        compiler_params=pltpu.CompilerParams(dimension_semantics=("arbitrary",)),
    )(integ_pad, picked, sign_q, table_all)


def exchange_kernel(send_ref, recv_ref, send_sem, recv_sem, local_sem):
    groups = lax.axis_size("g")
    count = groups * PAIR
    alpha = lax.axis_index("alpha")
    me = lax.axis_index("g") * PAIR + lax.axis_index("m")

    def remote(src_slot, dst_slot, sem_slot, peer):
        return pltpu.make_async_remote_copy(
            src_ref=send_ref.at[src_slot],
            dst_ref=recv_ref.at[dst_slot],
            send_sem=send_sem.at[sem_slot],
            recv_sem=recv_sem.at[dst_slot],
            device_id=(alpha, peer // PAIR, peer % PAIR),
            device_id_type=pl.DeviceIdType.MESH,
        )

    barrier = pltpu.get_barrier_semaphore()
    for step in range(1, count):
        peer = lax.rem(me + step, count)
        pl.semaphore_signal(
            barrier, 1, device_id=(alpha, peer // PAIR, peer % PAIR),
            device_id_type=pl.DeviceIdType.MESH,
        )
    pl.semaphore_wait(barrier, count - 1)

    for step in range(1, count):
        dest = lax.rem(me + step, count)
        remote(dest, me, dest, dest).start()
    local = pltpu.make_async_copy(send_ref.at[me], recv_ref.at[me], local_sem)
    local.start()
    local.wait()
    for step in range(1, count):
        dest = lax.rem(me + step, count)
        remote(dest, me, dest, dest).wait_send()
    for step in range(1, count):
        src = lax.rem(me + count - step, count)
        remote(src, src, src, src).wait_recv()


def exchange(send):
    count = send.shape[0]
    return pl.pallas_call(
        exchange_kernel,
        out_shape=jax.ShapeDtypeStruct(send.shape, send.dtype),
        in_specs=[pl.BlockSpec(memory_space=pl.ANY)],
        out_specs=pl.BlockSpec(memory_space=pl.ANY),
        scratch_shapes=[
            pltpu.SemaphoreType.DMA((count,)),
            pltpu.SemaphoreType.DMA((count,)),
            pltpu.SemaphoreType.DMA,
        ],
        compiler_params=pltpu.CompilerParams(collective_id=0, has_side_effects=True),
    )(send)


def spread_kernel(own_ref, out_ref, send_sem, recv_sem, local_sem, pair_send, pair_recv):
    count = lax.axis_size("alpha")
    rows, cols = own_ref.shape
    group = lax.axis_index("g")
    member = lax.axis_index("m")
    me = lax.axis_index("alpha")
    other = 1 - member

    def window(slot):
        return out_ref.at[pl.ds(slot * rows, rows), pl.ds(member * cols, cols)]

    def remote(slot, sem_slot, peer):
        return pltpu.make_async_remote_copy(
            src_ref=own_ref,
            dst_ref=window(slot),
            send_sem=send_sem.at[sem_slot],
            recv_sem=recv_sem.at[slot],
            device_id=(peer, group, member),
            device_id_type=pl.DeviceIdType.MESH,
        )

    for step in range(1, count):
        dest = lax.rem(me + step, count)
        remote(me, dest, dest).start()
    local = pltpu.make_async_copy(own_ref, window(me), local_sem)
    local.start()
    local.wait()
    for step in range(1, count):
        dest = lax.rem(me + step, count)
        remote(me, dest, dest).wait_send()
    for step in range(1, count):
        src = lax.rem(me + count - step, count)
        remote(src, src, src).wait_recv()

    def half(col):
        return out_ref.at[:, pl.ds(col * cols, cols)]

    def pair(col):
        return pltpu.make_async_remote_copy(
            src_ref=half(col),
            dst_ref=half(col),
            send_sem=pair_send,
            recv_sem=pair_recv,
            device_id=(me, group, other),
            device_id_type=pl.DeviceIdType.MESH,
        )

    pair(member).start()
    pair(member).wait_send()
    pair(other).wait_recv()


def spread(own, count):
    return pl.pallas_call(
        spread_kernel,
        out_shape=jax.ShapeDtypeStruct(
            (count // PAIR * own.shape[0], PAIR * own.shape[1]), own.dtype
        ),
        in_specs=[pl.BlockSpec(memory_space=pl.ANY)],
        out_specs=pl.BlockSpec(memory_space=pl.ANY),
        scratch_shapes=[
            pltpu.SemaphoreType.DMA((count // PAIR,)),
            pltpu.SemaphoreType.DMA((count // PAIR,)),
            pltpu.SemaphoreType.DMA,
            pltpu.SemaphoreType.DMA,
            pltpu.SemaphoreType.DMA,
        ],
        compiler_params=pltpu.CompilerParams(has_side_effects=True),
    )(own)


def gather_alpha_kernel(own_ref, out_ref, send_sem, recv_sem, local_sem):
    count = lax.axis_size("alpha")
    group = lax.axis_index("g")
    member = lax.axis_index("m")
    me = lax.axis_index("alpha")

    def remote(slot, sem_slot, peer):
        return pltpu.make_async_remote_copy(
            src_ref=own_ref,
            dst_ref=out_ref.at[slot],
            send_sem=send_sem.at[sem_slot],
            recv_sem=recv_sem.at[slot],
            device_id=(peer, group, member),
            device_id_type=pl.DeviceIdType.MESH,
        )

    barrier = pltpu.get_barrier_semaphore()
    for step in range(1, count):
        peer = lax.rem(me + step, count)
        pl.semaphore_signal(
            barrier, 1, device_id=(peer, group, member), device_id_type=pl.DeviceIdType.MESH
        )
    pl.semaphore_wait(barrier, count - 1)

    for step in range(1, count):
        dest = lax.rem(me + step, count)
        remote(me, dest, dest).start()
    local = pltpu.make_async_copy(own_ref, out_ref.at[me], local_sem)
    local.start()
    local.wait()
    for step in range(1, count):
        dest = lax.rem(me + step, count)
        remote(me, dest, dest).wait_send()
    for step in range(1, count):
        src = lax.rem(me + count - step, count)
        remote(src, src, src).wait_recv()


def gather_alpha(own, count):
    return pl.pallas_call(
        gather_alpha_kernel,
        out_shape=jax.ShapeDtypeStruct((count,) + own.shape, own.dtype),
        in_specs=[pl.BlockSpec(memory_space=pl.ANY)],
        out_specs=pl.BlockSpec(memory_space=pl.ANY),
        scratch_shapes=[
            pltpu.SemaphoreType.DMA((count,)),
            pltpu.SemaphoreType.DMA((count,)),
            pltpu.SemaphoreType.DMA,
        ],
        compiler_params=pltpu.CompilerParams(collective_id=1, has_side_effects=True),
    )(own)


def on_device(
    coefficients, diagonal, integrals, alpha_row, alpha_sign, beta_block, beta_sign, block_irrep
):
    alpha_rank = lax.axis_index("alpha")
    member = lax.axis_index("m")
    pair_count = integrals.shape[0]
    local_rows, local_cols = coefficients.shape
    block_len = beta_sign.shape[1] // pair_count
    per_device = local_rows // block_len
    src_blocks = local_cols // block_len
    total_blocks = lax.axis_size("g") * PAIR * src_blocks
    pairs = -(-pair_count // 16) * 16
    extra = pairs - pair_count
    sub_rows = block_len // PAIR

    alpha_size = lax.axis_size("alpha")
    gathered = spread(coefficients, alpha_size * PAIR)
    live_flags = (block_irrep == 0).astype(jnp.int32)
    live_rows = jnp.repeat(live_flags, block_len)
    gathered = gathered * live_rows[:, None].astype(jnp.bfloat16)
    window_rows, wide_cols = gathered.shape
    coeff_ext = jnp.concatenate(
        [gathered, -gathered, jnp.zeros((16, wide_cols), jnp.bfloat16)], axis=0
    )
    zero_row = 2 * window_rows

    integ_pad = jnp.pad(integrals, ((0, extra), (0, extra)))
    tables_both = jnp.concatenate([beta_sign, beta_block], axis=1).astype(jnp.bfloat16)
    tables_both = lax.all_gather(tables_both, "m", axis=0, tiled=True)
    beta_sign2 = tables_both[:, : beta_sign.shape[1]]
    beta_block2 = tables_both[:, beta_sign.shape[1] :].astype(jnp.int32)
    sign_q = (
        beta_sign2.reshape(PAIR, src_blocks, pair_count, block_len)
        .transpose(0, 2, 1, 3)
        .reshape(PAIR, pair_count, local_cols)
    )
    sign_q = jnp.pad(sign_q, ((0, 0), (0, extra), (0, 0))).astype(jnp.bfloat16)
    target_iota = jnp.arange(total_blocks, dtype=jnp.int32)
    table_all = (target_iota[None, :, None] == beta_block2[:, None, :]).astype(jnp.bfloat16)
    table_all = jnp.pad(
        table_all.reshape(PAIR, src_blocks * total_blocks, pair_count),
        ((0, 0), (0, 0), (0, extra)),
    )
    table_all = jnp.concatenate([table_all[h] for h in range(PAIR) for _ in range(2)], axis=1)

    own_flags = lax.dynamic_slice_in_dim(live_flags, alpha_rank * per_device, per_device, 0)

    dims = lax.GatherDimensionNumbers(
        offset_dims=(2,), collapsed_slice_dims=(0,), start_index_map=(0,)
    )

    block_count = live_flags.shape[0]
    block_iota = jnp.arange(block_count, dtype=jnp.int32)
    in_group = jnp.cumsum(live_flags.reshape(-1, per_device), axis=1).reshape(-1)
    is_first = (live_flags == 1) & (in_group == 1)
    is_extra = ((live_flags == 1) & jnp.logical_not(is_first)).astype(jnp.int32)
    extra_rank = jnp.cumsum(is_extra) - is_extra
    extra_total = jnp.sum(is_extra)
    block_of_extra = jnp.sum(
        jnp.where(
            (is_extra[None, :] == 1) & (extra_rank[None, :] == block_iota[:, None]),
            block_iota[None, :],
            0,
        ),
        axis=1,
    )
    own_first = lax.dynamic_slice_in_dim(is_first, alpha_rank * per_device, per_device, 0)
    first_blk = alpha_rank * per_device + jnp.argmax(own_first).astype(jnp.int32)
    my_count = 1 + jnp.maximum(extra_total - alpha_rank + alpha_size - 1, 0) // alpha_size
    beta_size = total_blocks // src_blocks

    def one_block(slot, buffer):
        block_id = jnp.where(
            slot == 0,
            first_blk,
            block_of_extra[jnp.maximum(slot - 1, 0) * alpha_size + alpha_rank],
        )
        first_row = block_id * block_len + member * sub_rows
        rows_src = lax.dynamic_slice_in_dim(alpha_row, first_row, sub_rows, 1)
        signs_src = lax.dynamic_slice_in_dim(alpha_sign, first_row, sub_rows, 1)
        row_ids = jnp.where(
            signs_src == 0,
            zero_row,
            jnp.where(signs_src < 0, rows_src + window_rows, rows_src),
        )
        row_ids = jnp.pad(row_ids, ((0, extra), (0, 0)), constant_values=zero_row).T
        picked = lax.gather(
            coeff_ext,
            row_ids[:, :, None],
            dims,
            slice_sizes=(1, wide_cols),
            mode=lax.GatherScatterMode.PROMISE_IN_BOUNDS,
        )
        summed = mix_block(integ_pad, picked, sign_q, table_all, total_blocks, block_len)
        part = summed.reshape(sub_rows, beta_size, local_cols).transpose(1, 0, 2)
        recv = exchange(part)
        groups = recv.shape[0] // PAIR
        rows = recv.reshape(groups, PAIR * sub_rows, local_cols).sum(axis=0)
        return lax.dynamic_update_slice(buffer, rows[None], (slot, 0, 0))

    empty = jnp.zeros((per_device, block_len, local_cols), jnp.float32)
    done = lax.fori_loop(0, my_count, one_block, empty)
    pushes = jnp.maximum(extra_total + alpha_size - 1, 0) // alpha_size

    def push(step, held):
        arrived = gather_alpha(done[step + 1], alpha_size)
        return lax.dynamic_update_slice(held, arrived[None], (step, 0, 0, 0))

    everyone = lax.fori_loop(
        0, pushes, push, jnp.zeros((per_device - 1, alpha_size, block_len, local_cols), jnp.float32)
    ).reshape((per_device - 1) * alpha_size, block_len, local_cols)
    own_rank = lax.dynamic_slice_in_dim(extra_rank, alpha_rank * per_device, per_device, 0)
    pick = jnp.minimum(own_rank // alpha_size, per_device - 2) * alpha_size + own_rank % alpha_size
    placed = jnp.where(own_first[:, None, None], done[0][None], everyone[pick])
    placed = placed.reshape(local_rows, local_cols)
    own_live_rows = jnp.repeat(own_flags, block_len)
    total = diagonal * coefficients.astype(jnp.float32) + placed
    return jnp.where(own_live_rows[:, None] == 1, total, jnp.zeros_like(total))


def solution(mesh):
    alpha_size, beta_size = mesh.devices.shape
    split_mesh = Mesh(
        mesh.devices.reshape(alpha_size, beta_size // PAIR, PAIR), ("alpha", "g", "m")
    )
    beta = ("g", "m")
    return jax.shard_map(
        on_device,
        mesh=split_mesh,
        in_specs=(
            P("alpha", beta),
            P("alpha", beta),
            P(),
            P(),
            P(),
            P(beta, None),
            P(beta, None),
            P(),
        ),
        out_specs=P("alpha", beta),
        check_vma=False,
    )
```

```python
import jax
import jax.numpy as jnp
from jax import lax
from jax.experimental import pallas as pl
from jax.experimental.pallas import tpu as pltpu
from jax.sharding import Mesh
from jax.sharding import PartitionSpec as P

ROWS = 8
PAIR = 2


def mix_kernel(integ_ref, picked_ref, sign_ref, table_ref, out_ref):
    halves, _, width = sign_ref.shape
    targets = out_ref.shape[1]
    block_len = out_ref.shape[2]
    src_blocks = width // block_len
    lane = lax.broadcasted_iota(jnp.int32, (targets, 2 * block_len), 1)
    upper = lane >= block_len
    integ = integ_ref[...]
    for row in range(picked_ref.shape[0]):
        mixed = jnp.dot(integ, picked_ref[row], preferred_element_type=jnp.float32)
        parts = []
        for half in range(halves):
            weighted = mixed[:, half * width : (half + 1) * width] * sign_ref[half]
            high = weighted.astype(jnp.bfloat16)
            low = (weighted - high.astype(jnp.float32)).astype(jnp.bfloat16)
            parts += [high, low]
        res = jnp.dot(
            table_ref[...], jnp.concatenate(parts, axis=0), preferred_element_type=jnp.float32
        )
        folded = jnp.zeros((targets, 2 * block_len), jnp.float32)
        for s in range(src_blocks):
            lanes = (s // 2) * 2 * block_len
            piece = res[s * targets : (s + 1) * targets, lanes : lanes + 2 * block_len]
            keep = upper if s % 2 else jnp.logical_not(upper)
            folded = folded + jnp.where(keep, piece, 0.0)
        folded = folded + pltpu.roll(folded, block_len, 1)
        out_ref[row] = folded[:, :block_len]


def mix_block(integ_pad, picked, sign_q, table_all, targets, block_len):
    rows, pairs, width = picked.shape
    return pl.pallas_call(
        mix_kernel,
        out_shape=jax.ShapeDtypeStruct((rows, targets, block_len), jnp.float32),
        grid=(rows // ROWS,),
        in_specs=[
            pl.BlockSpec((pairs, pairs), lambda i: (0, 0)),
            pl.BlockSpec((ROWS, pairs, width), lambda i: (i, 0, 0)),
            pl.BlockSpec(sign_q.shape, lambda i: (0, 0, 0)),
            pl.BlockSpec(table_all.shape, lambda i: (0, 0)),
        ],
        out_specs=pl.BlockSpec((ROWS, targets, block_len), lambda i: (i, 0, 0)),
        compiler_params=pltpu.CompilerParams(dimension_semantics=("arbitrary",)),
    )(integ_pad, picked, sign_q, table_all)


def exchange_kernel(send_ref, recv_ref, send_sem, recv_sem, local_sem):
    groups = lax.axis_size("g")
    count = groups * PAIR
    alpha = lax.axis_index("alpha")
    me = lax.axis_index("g") * PAIR + lax.axis_index("m")

    def remote(src_slot, dst_slot, sem_slot, peer):
        return pltpu.make_async_remote_copy(
            src_ref=send_ref.at[src_slot],
            dst_ref=recv_ref.at[dst_slot],
            send_sem=send_sem.at[sem_slot],
            recv_sem=recv_sem.at[dst_slot],
            device_id=(alpha, peer // PAIR, peer % PAIR),
            device_id_type=pl.DeviceIdType.MESH,
        )

    barrier = pltpu.get_barrier_semaphore()
    for step in range(1, count):
        peer = lax.rem(me + step, count)
        pl.semaphore_signal(
            barrier, 1, device_id=(alpha, peer // PAIR, peer % PAIR),
            device_id_type=pl.DeviceIdType.MESH,
        )
    pl.semaphore_wait(barrier, count - 1)

    for step in range(1, count):
        dest = lax.rem(me + step, count)
        remote(dest, me, dest, dest).start()
    local = pltpu.make_async_copy(send_ref.at[me], recv_ref.at[me], local_sem)
    local.start()
    local.wait()
    for step in range(1, count):
        dest = lax.rem(me + step, count)
        remote(dest, me, dest, dest).wait_send()
    for step in range(1, count):
        src = lax.rem(me + count - step, count)
        remote(src, src, src, src).wait_recv()


def exchange(send):
    count = send.shape[0]
    return pl.pallas_call(
        exchange_kernel,
        out_shape=jax.ShapeDtypeStruct(send.shape, send.dtype),
        in_specs=[pl.BlockSpec(memory_space=pl.ANY)],
        out_specs=pl.BlockSpec(memory_space=pl.ANY),
        scratch_shapes=[
            pltpu.SemaphoreType.DMA((count,)),
            pltpu.SemaphoreType.DMA((count,)),
            pltpu.SemaphoreType.DMA,
        ],
        compiler_params=pltpu.CompilerParams(collective_id=0, has_side_effects=True),
    )(send)


def spread_kernel(own_ref, out_ref, send_sem, recv_sem, local_sem, pair_send, pair_recv):
    count = lax.axis_size("alpha")
    rows, cols = own_ref.shape
    group = lax.axis_index("g")
    member = lax.axis_index("m")
    me = lax.axis_index("alpha")
    other = 1 - member

    def window(slot):
        return out_ref.at[pl.ds(slot * rows, rows), pl.ds(member * cols, cols)]

    def remote(slot, sem_slot, peer):
        return pltpu.make_async_remote_copy(
            src_ref=own_ref,
            dst_ref=window(slot),
            send_sem=send_sem.at[sem_slot],
            recv_sem=recv_sem.at[slot],
            device_id=(peer, group, member),
            device_id_type=pl.DeviceIdType.MESH,
        )

    for step in range(1, count):
        dest = lax.rem(me + step, count)
        remote(me, dest, dest).start()
    local = pltpu.make_async_copy(own_ref, window(me), local_sem)
    local.start()
    local.wait()
    for step in range(1, count):
        dest = lax.rem(me + step, count)
        remote(me, dest, dest).wait_send()
    for step in range(1, count):
        src = lax.rem(me + count - step, count)
        remote(src, src, src).wait_recv()

    def half(col):
        return out_ref.at[:, pl.ds(col * cols, cols)]

    def pair(col):
        return pltpu.make_async_remote_copy(
            src_ref=half(col),
            dst_ref=half(col),
            send_sem=pair_send,
            recv_sem=pair_recv,
            device_id=(me, group, other),
            device_id_type=pl.DeviceIdType.MESH,
        )

    pair(member).start()
    pair(member).wait_send()
    pair(other).wait_recv()


def spread(own, count):
    return pl.pallas_call(
        spread_kernel,
        out_shape=jax.ShapeDtypeStruct(
            (count // PAIR * own.shape[0], PAIR * own.shape[1]), own.dtype
        ),
        in_specs=[pl.BlockSpec(memory_space=pl.ANY)],
        out_specs=pl.BlockSpec(memory_space=pl.ANY),
        scratch_shapes=[
            pltpu.SemaphoreType.DMA((count // PAIR,)),
            pltpu.SemaphoreType.DMA((count // PAIR,)),
            pltpu.SemaphoreType.DMA,
            pltpu.SemaphoreType.DMA,
            pltpu.SemaphoreType.DMA,
        ],
        compiler_params=pltpu.CompilerParams(has_side_effects=True),
    )(own)


def gather_alpha_kernel(own_ref, out_ref, send_sem, recv_sem, local_sem):
    count = lax.axis_size("alpha")
    group = lax.axis_index("g")
    member = lax.axis_index("m")
    me = lax.axis_index("alpha")

    def remote(slot, sem_slot, peer):
        return pltpu.make_async_remote_copy(
            src_ref=own_ref,
            dst_ref=out_ref.at[slot],
            send_sem=send_sem.at[sem_slot],
            recv_sem=recv_sem.at[slot],
            device_id=(peer, group, member),
            device_id_type=pl.DeviceIdType.MESH,
        )

    barrier = pltpu.get_barrier_semaphore()
    for step in range(1, count):
        peer = lax.rem(me + step, count)
        pl.semaphore_signal(
            barrier, 1, device_id=(peer, group, member), device_id_type=pl.DeviceIdType.MESH
        )
    pl.semaphore_wait(barrier, count - 1)

    for step in range(1, count):
        dest = lax.rem(me + step, count)
        remote(me, dest, dest).start()
    local = pltpu.make_async_copy(own_ref, out_ref.at[me], local_sem)
    local.start()
    local.wait()
    for step in range(1, count):
        dest = lax.rem(me + step, count)
        remote(me, dest, dest).wait_send()
    for step in range(1, count):
        src = lax.rem(me + count - step, count)
        remote(src, src, src).wait_recv()


def gather_alpha(own, count):
    return pl.pallas_call(
        gather_alpha_kernel,
        out_shape=jax.ShapeDtypeStruct((count,) + own.shape, own.dtype),
        in_specs=[pl.BlockSpec(memory_space=pl.ANY)],
        out_specs=pl.BlockSpec(memory_space=pl.ANY),
        scratch_shapes=[
            pltpu.SemaphoreType.DMA((count,)),
            pltpu.SemaphoreType.DMA((count,)),
            pltpu.SemaphoreType.DMA,
        ],
        compiler_params=pltpu.CompilerParams(collective_id=1, has_side_effects=True),
    )(own)


def on_device(
    coefficients, diagonal, integrals, alpha_row, alpha_sign, beta_block, beta_sign, block_irrep
):
    alpha_rank = lax.axis_index("alpha")
    member = lax.axis_index("m")
    pair_count = integrals.shape[0]
    local_rows, local_cols = coefficients.shape
    block_len = beta_sign.shape[1] // pair_count
    per_device = local_rows // block_len
    src_blocks = local_cols // block_len
    total_blocks = lax.axis_size("g") * PAIR * src_blocks
    pairs = -(-pair_count // 16) * 16
    extra = pairs - pair_count
    sub_rows = block_len // PAIR

    alpha_size = lax.axis_size("alpha")
    gathered = spread(coefficients, alpha_size * PAIR)
    live_flags = (block_irrep == 0).astype(jnp.int32)
    live_rows = jnp.repeat(live_flags, block_len)
    gathered = gathered * live_rows[:, None].astype(jnp.bfloat16)
    window_rows, wide_cols = gathered.shape
    coeff_ext = jnp.concatenate(
        [gathered, -gathered, jnp.zeros((16, wide_cols), jnp.bfloat16)], axis=0
    )
    zero_row = 2 * window_rows

    integ_pad = jnp.pad(integrals, ((0, extra), (0, extra)))
    tables_both = jnp.concatenate([beta_sign, beta_block], axis=1).astype(jnp.bfloat16)
    tables_both = lax.all_gather(tables_both, "m", axis=0, tiled=True)
    beta_sign2 = tables_both[:, : beta_sign.shape[1]]
    beta_block2 = tables_both[:, beta_sign.shape[1] :].astype(jnp.int32)
    sign_q = (
        beta_sign2.reshape(PAIR, src_blocks, pair_count, block_len)
        .transpose(0, 2, 1, 3)
        .reshape(PAIR, pair_count, local_cols)
    )
    sign_q = jnp.pad(sign_q, ((0, 0), (0, extra), (0, 0))).astype(jnp.float32)
    target_iota = jnp.arange(total_blocks, dtype=jnp.int32)
    table_all = (target_iota[None, :, None] == beta_block2[:, None, :]).astype(jnp.bfloat16)
    table_all = jnp.pad(
        table_all.reshape(PAIR, src_blocks * total_blocks, pair_count),
        ((0, 0), (0, 0), (0, extra)),
    )
    table_all = jnp.concatenate([table_all[h] for h in range(PAIR) for _ in range(2)], axis=1)

    own_flags = lax.dynamic_slice_in_dim(live_flags, alpha_rank * per_device, per_device, 0)

    dims = lax.GatherDimensionNumbers(
        offset_dims=(2,), collapsed_slice_dims=(0,), start_index_map=(0,)
    )

    block_count = live_flags.shape[0]
    block_iota = jnp.arange(block_count, dtype=jnp.int32)
    in_group = jnp.cumsum(live_flags.reshape(-1, per_device), axis=1).reshape(-1)
    is_first = (live_flags == 1) & (in_group == 1)
    is_extra = ((live_flags == 1) & jnp.logical_not(is_first)).astype(jnp.int32)
    extra_rank = jnp.cumsum(is_extra) - is_extra
    extra_total = jnp.sum(is_extra)
    block_of_extra = jnp.sum(
        jnp.where(
            (is_extra[None, :] == 1) & (extra_rank[None, :] == block_iota[:, None]),
            block_iota[None, :],
            0,
        ),
        axis=1,
    )
    own_first = lax.dynamic_slice_in_dim(is_first, alpha_rank * per_device, per_device, 0)
    first_blk = alpha_rank * per_device + jnp.argmax(own_first).astype(jnp.int32)
    my_count = 1 + jnp.maximum(extra_total - alpha_rank + alpha_size - 1, 0) // alpha_size
    beta_size = total_blocks // src_blocks

    def one_block(slot, buffer):
        block_id = jnp.where(
            slot == 0,
            first_blk,
            block_of_extra[jnp.maximum(slot - 1, 0) * alpha_size + alpha_rank],
        )
        first_row = block_id * block_len + member * sub_rows
        rows_src = lax.dynamic_slice_in_dim(alpha_row, first_row, sub_rows, 1)
        signs_src = lax.dynamic_slice_in_dim(alpha_sign, first_row, sub_rows, 1)
        row_ids = jnp.where(
            signs_src == 0,
            zero_row,
            jnp.where(signs_src < 0, rows_src + window_rows, rows_src),
        )
        row_ids = jnp.pad(row_ids, ((0, extra), (0, 0)), constant_values=zero_row).T
        picked = lax.gather(
            coeff_ext,
            row_ids[:, :, None],
            dims,
            slice_sizes=(1, wide_cols),
            mode=lax.GatherScatterMode.PROMISE_IN_BOUNDS,
        )
        summed = mix_block(integ_pad, picked, sign_q, table_all, total_blocks, block_len)
        part = summed.reshape(sub_rows, beta_size, local_cols).transpose(1, 0, 2)
        recv = exchange(part)
        groups = recv.shape[0] // PAIR
        rows = recv.reshape(groups, PAIR * sub_rows, local_cols).sum(axis=0)
        return lax.dynamic_update_slice(buffer, rows[None], (slot, 0, 0))

    empty = jnp.zeros((per_device, block_len, local_cols), jnp.float32)
    done = lax.fori_loop(0, my_count, one_block, empty)
    pushes = jnp.maximum(extra_total + alpha_size - 1, 0) // alpha_size

    def push(step, held):
        arrived = gather_alpha(done[step + 1], alpha_size)
        return lax.dynamic_update_slice(held, arrived[None], (step, 0, 0, 0))

    everyone = lax.fori_loop(
        0, pushes, push, jnp.zeros((per_device - 1, alpha_size, block_len, local_cols), jnp.float32)
    ).reshape((per_device - 1) * alpha_size, block_len, local_cols)
    own_rank = lax.dynamic_slice_in_dim(extra_rank, alpha_rank * per_device, per_device, 0)
    pick = jnp.minimum(own_rank // alpha_size, per_device - 2) * alpha_size + own_rank % alpha_size
    placed = jnp.where(own_first[:, None, None], done[0][None], everyone[pick])
    placed = placed.reshape(local_rows, local_cols)
    own_live_rows = jnp.repeat(own_flags, block_len)
    total = diagonal * coefficients.astype(jnp.float32) + placed
    return jnp.where(own_live_rows[:, None] == 1, total, jnp.zeros_like(total))


def solution(mesh):
    alpha_size, beta_size = mesh.devices.shape
    split_mesh = Mesh(
        mesh.devices.reshape(alpha_size, beta_size // PAIR, PAIR), ("alpha", "g", "m")
    )
    beta = ("g", "m")
    return jax.shard_map(
        on_device,
        mesh=split_mesh,
        in_specs=(
            P("alpha", beta),
            P("alpha", beta),
            P(),
            P(),
            P(),
            P(beta, None),
            P(beta, None),
            P(),
        ),
        out_specs=P("alpha", beta),
        check_vma=False,
    )
```
